32 devices in a mesh: dp: 2 (over core), ep: 16 (over z, y, x).
Axes of the slice: x: 2, y: 2, z: 4, core: 2. Of those that a mesh axis runs over, the one named last changes fastest.
Arguments:
- latent_cache: bfloat16 [16, 4, 512, 576], P('ep', 'dp'), may hold values from -6 to 6
- lengths: int32 [16, 4], P(None, 'dp'), may hold values from 2 to 512
- new_home: int32 [16, 4], P(None, 'dp'), may hold values from 0 to 15, as said below
- queries: bfloat16 [2, 16, 4, 128, 576], P(None, 'ep', 'dp'), may hold values from -32 to 32
- new_latent: bfloat16 [2, 16, 4, 576], P(None, 'ep', 'dp'), may hold values from -6 to 6
- hidden: bfloat16 [2, 16, 4, 3584], P(None, 'ep', 'dp'), may hold values from -6 to 6
- routes: int32 [2, 16, 4, 8], P(None, 'ep', 'dp'), may hold values from 0 to 15, all different within a row; in each aligned block of 4 rows (0 to 3, 4 to 7, ..., all dimensions but the last counted through in order) at most 4 rows name the same one
- route_logits: bfloat16 [2, 16, 4, 8], P(None, 'ep', 'dp'), may hold values from -8 to 8
- w_gate: bfloat16 [16, 3584, 1024], P('ep', None, 'dp'), may hold values from -0.09375 to 0.09375
- w_up: bfloat16 [16, 3584, 1024], P('ep', None, 'dp'), may hold values from -0.09375 to 0.09375
- w_down: bfloat16 [16, 1024, 3584], P('ep', 'dp'), may hold values from -0.1875 to 0.1875
Outputs:
- attended: bfloat16 [2, 16, 4, 128, 512], P(None, 'ep', 'dp')
- moe_out: bfloat16 [2, 16, 4, 3584], P(None, 'ep', 'dp')
The draws below stay inside these ranges and needn't reach their ends.
Inputs may be any that keep to these rules, and one draw needn't show every extreme that they name: `routes`: in each step, the 4 requests of one ep index name any one expert in at most 4 of their choices, and this bound is reached. For each request index c, new_home[., c] exchanges exactly two ep indices and leaves every other one in place, so new_home[new_home[e, c], c] == e; the two indices lie 16 // 2 apart for even c and 1 apart (modulo 16) for odd c.
All inputs are finite; a program needn't handle non-finite values.
Results may differ from the reference program's by a relative error of at most 0.0057.
Values may be sent and summed in bfloat16 or wider, within the bound.
A program may use at most 128 MiB of HBM per device.

```python
import math
import jax
import jax.numpy as jnp
import numpy as np
from jax import lax

D = 3584
FF = 1024
HEADS = 128
KV_RANK = 512
ROPE = 64
HEAD_QK = 192
TOP = 8
STEPS = 2
CACHE = 512
EXPERTS = 16
COLROWS = 4
CAP = 4
N_DP = 2


def integer_parts(key):
    subkeys = jax.random.split(jax.random.fold_in(key, 5), 5)
    heavy_rank = jax.random.randint(subkeys[0], (EXPERTS, 1), 0, 6) == 0
    long_rows = jax.random.randint(subkeys[1], (EXPERTS, COLROWS), CACHE // 2, CACHE + 1)
    short_rows = jax.random.randint(subkeys[2], (EXPERTS, COLROWS), 2, CACHE // 4 + 2)
    flat_lengths = jnp.where(heavy_rank, long_rows, short_rows).reshape(-1)
    total_rows = EXPERTS * COLROWS
    first_spot = jax.random.randint(subkeys[3], (), 0, total_rows)
    second_spot = (first_spot + 1 + jax.random.randint(subkeys[4], (), 0, total_rows - 1)) % total_rows
    spots = jnp.arange(total_rows)
    flat_lengths = jnp.where(spots == first_spot, CACHE, flat_lengths)
    flat_lengths = jnp.where(spots == second_spot, 2, flat_lengths)
    lengths = flat_lengths.reshape(EXPERTS, COLROWS).astype(jnp.int32)
    rank_ids = jnp.arange(EXPERTS, dtype=jnp.int32)[:, None]
    long_score = lengths * EXPERTS + (EXPERTS - 1 - rank_ids)
    heavy_pick = jnp.argmax(long_score, 0).astype(jnp.int32)
    request_ids = jnp.arange(COLROWS, dtype=jnp.int32)
    offset = jnp.where(request_ids % 2 == 0, EXPERTS // 2, 1).astype(jnp.int32)
    light_pick = ((heavy_pick + offset) % EXPERTS).astype(jnp.int32)
    homes = jnp.where(rank_ids == heavy_pick[None, :], light_pick[None, :], jnp.where(rank_ids == light_pick[None, :], heavy_pick[None, :], rank_ids))
    return (lengths, homes.astype(jnp.int32))


def draw_lengths(key, part):
    return integer_parts(key)[0]


def draw_new_home(key, part):
    return integer_parts(key)[1]


def float_parts(key):
    subkeys = jax.random.split(jax.random.fold_in(key, 9), 3)
    lat_width = KV_RANK + ROPE
    cache_shape = (EXPERTS, COLROWS, CACHE, lat_width)
    fresh_shape = (STEPS, EXPERTS, COLROWS, lat_width)
    query_shape = (STEPS, EXPERTS, COLROWS, HEADS, lat_width)
    cache_rows = jax.random.truncated_normal(subkeys[0], -6.0, 6.0, cache_shape, jnp.float32)
    fresh_rows = jax.random.truncated_normal(subkeys[1], -6.0, 6.0, fresh_shape, jnp.float32)
    query_rows = 0.9 * jax.random.truncated_normal(subkeys[2], -6.0, 6.0, query_shape, jnp.float32) + 0.1 * fresh_rows[:, :, :, None, :]
    return (cache_rows.astype(jnp.bfloat16), fresh_rows.astype(jnp.bfloat16), query_rows.astype(jnp.bfloat16))


def draw_latent_cache(key, part):
    return float_parts(key)[0]


def draw_new_latent(key, part):
    return float_parts(key)[1]


def draw_queries(key, part):
    return float_parts(key)[2]


def block_levels(rng, extent, cuts, least, largest):
    gain = 1.0
    for position, parts in cuts:
        heights = jax.random.uniform(jax.random.fold_in(jax.random.fold_in(rng, 6), position), (parts,), jnp.float32, least / len(cuts), largest / len(cuts))
        gain = gain * jnp.repeat(jnp.exp(heights), extent[position] // parts).reshape((-1,) + (1,) * (len(extent) - 1 - position))
    return gain


def assign_block(key, own, number, rows, count, top, most, lean):
    ranking = jax.random.permutation(key, count)
    crowded, ordinary = load_shares(count, rows * top, most, lean, True), load_shares(count, rows * top, most, lean, False)
    places = jnp.arange(count)

    def named(sizes, rotation):
        used = int((sizes > 0).sum())
        fixed = max(1, used // 4)
        shifted = fixed + (places - fixed + rotation * (used - fixed)) % max(1, count - fixed)
        return jnp.zeros((count,), jnp.int32).at[ranking[jnp.where(places < fixed, places, shifted)]].set(jnp.asarray(sizes, jnp.int32))

    sizes = jnp.where(number % 4 == 0, named(crowded, number // 4), named(ordinary, number - number // 4 - 1))
    mixed = jax.random.permutation(jax.random.fold_in(own, 3), count)
    giver, receiver = mixed[0:count // 2 * 2:2], mixed[1:count // 2 * 2:2]
    margin = jnp.minimum(sizes[giver] - 1, most - sizes[receiver]) // 2
    margin = jnp.where((giver == ranking[0]) | (receiver == ranking[0]) | (sizes[receiver] == 0), 0, jnp.maximum(margin, 0))
    shifted = jax.random.randint(jax.random.fold_in(own, 4), (count // 2,), 0, 1 << 20) % (margin + 1)
    sizes = sizes.at[giver].add(-shifted).at[receiver].add(shifted)
    members = jnp.searchsorted(jnp.cumsum(sizes), jnp.arange(rows * top), side="right").astype(jnp.int32)
    listing = members.reshape(top, rows).T
    listing = listing[jax.random.permutation(jax.random.fold_in(own, 1), rows)]
    rotation = jax.random.randint(jax.random.fold_in(own, 2), (rows, 1), 0, top)
    return jnp.take_along_axis(listing, (jnp.arange(top)[None, :] + rotation) % top, axis=1)


def load_shares(amount, total, limit, skew, full):
    portions = [(1 << 20) // math.isqrt(rank ** skew) + 1 for rank in range(1, amount + 1)]
    largest = limit if full else min(limit, max(-(-total // amount), total * portions[0] // sum(portions)))
    least = 1 if total - largest >= amount - 1 else 0
    holding, rest = [largest] + [least] * (amount - 1), total - largest - least * (amount - 1)
    while rest > 0:
        candidates = [i for i in range(1, amount) if holding[i] < largest] or [i for i in range(1, amount) if holding[i] < limit]
        whole, remaining = sum([portions[i] for i in candidates]), rest
        for i in candidates:
            extra = min(limit - holding[i], max(1, remaining * portions[i] // whole), rest)
            holding[i] = holding[i] + extra
            rest = rest - extra
    return np.array(holding)


def gaussian(rng, shape, scale, most, cuts=(), kind=jnp.bfloat16):
    result = scale * jax.random.normal(rng, shape, jnp.float32)
    if cuts:
        result = result * block_levels(rng, shape, cuts, -0.22, 0.18)
    return jnp.clip(result, -most, most).astype(kind)


def setup_inputs(seed: int = 0) -> dict:
    key_of = jax.random.split(jax.random.key(seed), 12)
    latent_cache = draw_latent_cache(jax.random.fold_in(key_of[11], 71), 0)
    lengths = draw_lengths(jax.random.fold_in(key_of[11], 71), 0)
    new_home = draw_new_home(jax.random.fold_in(key_of[11], 71), 0)
    queries = draw_queries(jax.random.fold_in(key_of[11], 71), 0)
    new_latent = draw_new_latent(jax.random.fold_in(key_of[11], 71), 0)
    hidden = gaussian(key_of[5], (STEPS, EXPERTS, COLROWS, D), 1.0, 6.0, ((1, 16), (2, 2)))
    routes_keys = jax.random.split(jax.random.fold_in(key_of[6], 1), STEPS * EXPERTS * COLROWS // COLROWS)
    routes_turns = jax.random.permutation(jax.random.fold_in(key_of[6], 3), STEPS * EXPERTS * COLROWS // COLROWS)
    routes = jax.vmap(lambda own, number: assign_block(jax.random.fold_in(key_of[6], 2), own, number, COLROWS, EXPERTS, TOP, CAP, 2))(routes_keys, routes_turns).reshape((STEPS, EXPERTS, COLROWS, TOP))
    route_logits = gaussian(key_of[7], (STEPS, EXPERTS, COLROWS, TOP), 2.0, 8.0, ((1, 16), (2, 2)))
    w_gate = gaussian(key_of[8], (EXPERTS, D, FF), D ** -0.5, 0.09375, ((0, 16), (2, 2)))
    w_up = gaussian(key_of[9], (EXPERTS, D, FF), D ** -0.5, 0.09375, ((0, 16), (2, 2)))
    w_down = gaussian(key_of[10], (EXPERTS, FF, D), FF ** -0.5, 0.1875, ((0, 16), (1, 2)))
    return dict(latent_cache=latent_cache, lengths=lengths, new_home=new_home, queries=queries, new_latent=new_latent, hidden=hidden, routes=routes, route_logits=route_logits, w_gate=w_gate, w_up=w_up, w_down=w_down)


def attend_one(query_rows, cache_rows, fresh_rows, length):
    step_count, head_count, lat_width = query_rows.shape
    softmax_scale = HEAD_QK ** -0.5
    flat_query = query_rows.reshape(step_count * head_count, lat_width)
    cache_scores = jnp.dot(flat_query, cache_rows.T, preferred_element_type=jnp.float32) * softmax_scale
    key_place = jnp.arange(cache_rows.shape[0], dtype=jnp.int32)
    cache_scores = jnp.where(key_place[None, :] < length, cache_scores, -jnp.inf)
    fresh_scores = jnp.dot(flat_query, fresh_rows.T, preferred_element_type=jnp.float32) * softmax_scale
    row_step = jnp.arange(step_count * head_count, dtype=jnp.int32) // head_count
    fresh_step = jnp.arange(step_count, dtype=jnp.int32)
    fresh_scores = jnp.where(fresh_step[None, :] <= row_step[:, None], fresh_scores, -jnp.inf)
    all_scores = jnp.concatenate([cache_scores, fresh_scores], 1)
    row_max = jnp.max(all_scores, 1, keepdims=True)
    weights = jnp.exp(all_scores - row_max)
    probs_all = (weights / jnp.sum(weights, 1, keepdims=True)).astype(jnp.bfloat16)
    key_values = jnp.concatenate([cache_rows, fresh_rows], 0)[:, :KV_RANK]
    served = jnp.dot(probs_all, key_values, preferred_element_type=jnp.float32).astype(jnp.bfloat16)
    return served.reshape(step_count, head_count, KV_RANK)


def expert(items):
    expert_rows, gate_w, up_w, down_w = items
    gate_part = jnp.dot(expert_rows, gate_w, preferred_element_type=jnp.float32)
    up_part = jnp.dot(expert_rows, up_w, preferred_element_type=jnp.float32)
    hidden_units = lax.optimization_barrier((jax.nn.silu(gate_part) * up_part).astype(jnp.bfloat16))
    slices = hidden_units.astype(jnp.float32).reshape(-1, N_DP, FF // N_DP).transpose(1, 0, 2)
    down_slices = down_w.astype(jnp.float32).reshape(N_DP, FF // N_DP, D)
    slice_out = jnp.einsum("jrf,jfd->jrd", slices, down_slices, precision=lax.Precision.HIGHEST)
    rounded = lax.optimization_barrier(slice_out.astype(jnp.bfloat16))
    return jnp.sum(rounded.astype(jnp.float32), 0)


def reference(latent_cache, lengths, new_home, queries, new_latent, hidden, routes, route_logits, w_gate, w_up, w_down):
    query_cols = jnp.transpose(queries, (1, 2, 0, 3, 4))
    fresh_cols = jnp.transpose(new_latent, (1, 2, 0, 3))

    def per_rank(items):
        cache_rank, length_rank, query_rank, fresh_rank = items
        return jax.vmap(attend_one)(query_rank, cache_rank, fresh_rank, length_rank)

    results = lax.map(per_rank, (latent_cache, lengths, query_cols, fresh_cols))
    relocated = results[new_home, jnp.arange(COLROWS, dtype=jnp.int32)[None, :]]
    attended = jnp.transpose(relocated, (2, 0, 1, 3, 4))

    sigmoid_part = jax.nn.sigmoid(route_logits.astype(jnp.float32))
    gate_weights = 2.5 * sigmoid_part / jnp.sum(sigmoid_part, -1, keepdims=True)
    rank_ids = jnp.arange(EXPERTS, dtype=jnp.int32)
    outputs = []
    for number in range(STEPS):
        flat_routes = routes[number].reshape(EXPERTS, COLROWS * TOP)
        onehot = (flat_routes[:, :, None] == rank_ids[None, None, :]).astype(jnp.int32)
        slot_rank = jnp.sum(jnp.cumsum(onehot, 1) * onehot, 2) - 1
        slot_index = flat_routes * CAP + slot_rank
        tokens = jnp.repeat(hidden[number], TOP, axis=1)
        buffer = jnp.zeros((EXPERTS, EXPERTS * CAP, D), jnp.bfloat16)
        buffer = buffer.at[rank_ids[:, None], slot_index].set(tokens)
        by_expert = buffer.reshape(EXPERTS, EXPERTS, CAP, D).transpose(1, 0, 2, 3).reshape(EXPERTS, EXPERTS * CAP, D)
        expert_out = lax.map(expert, (by_expert, w_gate, w_up, w_down)).reshape(EXPERTS, EXPERTS, CAP, D)
        picked = expert_out[flat_routes, rank_ids[:, None], slot_rank]
        weighted = picked.reshape(EXPERTS, COLROWS, TOP, D) * gate_weights[number][..., None]
        outputs.append(jnp.sum(weighted, 2).astype(jnp.bfloat16))
    moe_out = jnp.stack(outputs, 0)
    return attended, moe_out
```

```python
import functools

import jax
import jax.numpy as jnp
from jax import lax
from jax.experimental import pallas as pl
from jax.experimental.pallas import tpu as pltpu
from jax.sharding import PartitionSpec as P


KV_RANK = 512
HEAD_QK = 192
LANES = 128
MESH = pl.DeviceIdType.MESH
GATHER_CHUNKS = 2
RETURN_CHUNKS = 4


def ladder_kernel(
    plan,
    lengths_ref,
    homes_ref,
    fresh_ref,
    hidden_ref,
    routes_ref,
    logits_ref,
    cache_hbm,
    query_hbm,
    gate_hbm,
    up_hbm,
    down_hbm,
    attended_hbm,
    moe_ref,
    column,
    tokens,
    query,
    cache,
    w_gate,
    w_up,
    w_down,
    served,
    far,
    near,
    onward,
    moved,
    own_part,
    pair_send,
    pair_recv,
    chip_part,
    chip_send,
    first_recv,
    second_keep,
    second_send,
    second_recv,
    line_part,
    line_send,
    line_recv,
    load_sem,
    send_sem,
    recv_sem,
):
    ranks, line = plan["ranks"], plan["line"]
    steps, requests = hidden_ref.shape[0], hidden_ref.shape[2]
    own_rows = steps * requests
    lat = cache.shape[1]
    heads = query.shape[-1]
    width = hidden_ref.shape[-1]
    blocks = width // LANES
    layers = blocks + 1
    half = 4
    core = lax.axis_index("dp")
    rank = lax.axis_index("ep")
    side, up, place = lax.rem(rank, 2), lax.rem(lax.div(rank, 2), 2), lax.div(rank, 4)
    cell = lax.rem(rank, 4)
    across_side, across_up = rank + 1 - 2 * side, rank + 2 - 4 * up
    first = across_up * (1 - core) + across_side * core
    second = across_side * (1 - core) + across_up * core
    first_cell, corner = lax.rem(first, 4), 3 - cell
    second_cell = lax.rem(second, 4)
    other = 1 - core
    far_rank = lax.rem(rank + ranks // 2, ranks)
    onward_rank = lax.rem(rank + 2 - 4 * side + ranks, ranks)
    behind_rank = lax.rem(rank - 2 + 4 * side + ranks, ranks)

    loads, sends = [], []

    def load(source, target):
        copy = pltpu.make_async_copy(source, target, load_sem.at[len(loads)])
        copy.start()
        loads.append(copy)
        return copy

    def send(source, target, to_core, to_rank):
        spot = len(sends)
        copy = pltpu.make_async_remote_copy(
            src_ref=source,
            dst_ref=target,
            send_sem=send_sem.at[spot],
            recv_sem=recv_sem.at[spot],
            device_id=(to_core, to_rank),
            device_id_type=MESH,
        )
        copy.start()
        sends.append(copy)
        return copy

    barrier = pltpu.get_barrier_semaphore()
    peers = [(other, rank), (core, across_side), (core, across_up)]
    peers += [(core, lax.rem(rank + 4 * step, ranks)) for step in range(1, line)]
    peers += [(core, onward_rank), (core, behind_rank), (core, far_rank)]
    for peer in peers:
        pl.semaphore_signal(barrier, inc=1, device_id=peer, device_id_type=MESH)

    attend_loads = {}
    for request in reversed(range(requests)):
        attend_loads[request] = (
            load(query_hbm.at[:, 0, request], query.at[request]),
            load(cache_hbm.at[0, request], cache.at[request]),
        )
    parts = 4
    rows = width // parts
    gate_loads = []
    for part in range(parts):
        span = pl.ds(part * rows, rows)
        gate_loads.append(
            (load(gate_hbm.at[0, span], w_gate.at[span]), load(up_hbm.at[0, span], w_up.at[span]))
        )
    down_load = load(down_hbm.at[0], w_down)

    lane = lax.broadcasted_iota(jnp.int32, (requests, LANES), 1)
    expert = lane - jnp.where(lane >= 2 * ranks, 2 * ranks, jnp.where(lane >= ranks, ranks, 0))
    dense = []
    for step in range(steps):
        logits = logits_ref[step, 0].astype(jnp.float32)
        chosen = routes_ref[step, 0]
        sigmoid_part = 1.0 / (1.0 + jnp.exp(-logits))
        gates = 2.5 * sigmoid_part / jnp.sum(sigmoid_part, 1, keepdims=True)
        total = jnp.zeros((requests, LANES), jnp.float32)
        for k in range(chosen.shape[1]):
            total = total + jnp.where(chosen[:, k : k + 1] == expert, gates[:, k : k + 1], 0.0)
        dense.append(total)
    dense = jnp.concatenate(dense, 0)
    lane = lax.broadcasted_iota(jnp.int32, (own_rows, LANES), 1)
    high = dense.astype(jnp.bfloat16).astype(jnp.float32)
    middle = (dense - high).astype(jnp.bfloat16).astype(jnp.float32)
    low = dense - high - middle
    coded = jnp.where(lane < ranks, high, jnp.where(lane < 2 * ranks, middle, low))
    coded = jnp.where(lane < 3 * ranks, coded, 0.0)
    own = jnp.concatenate(
        [hidden_ref[step, 0].astype(jnp.float32) for step in range(steps)], 0
    )
    for block in range(blocks):
        column[place, block] = own[:, block * LANES : (block + 1) * LANES].astype(jnp.bfloat16)
    column[place, blocks] = coded.astype(jnp.bfloat16)

    pl.semaphore_wait(barrier, len(peers))

    cuts = [blocks * c // GATHER_CHUNKS for c in range(GATHER_CHUNKS)] + [layers]
    spans = [pl.ds(cuts[c], cuts[c + 1] - cuts[c]) for c in range(GATHER_CHUNKS)]
    line_sends = []
    for span in spans:
        line_sends.append(
            [
                send(
                    column.at[place, span],
                    column.at[place, span],
                    core,
                    lax.rem(rank + 4 * step, ranks),
                )
                for step in range(1, line)
            ]
        )

    def attend(request):
        for copy in attend_loads[request]:
            copy.wait()
        length = lengths_ref[request, rank]
        scale = HEAD_QK ** (-0.5)
        lines = jnp.concatenate([query[request, step] for step in range(steps)], 1)
        keys = cache[request]
        scores = (
            lax.dot_general(
                lines, keys, (((0,), (0,)), ((), ())), preferred_element_type=jnp.float32
            )
            * scale
        )
        spot = lax.broadcasted_iota(jnp.int32, scores.shape, 1)
        scores = jnp.where(spot < length, scores, -jnp.inf)
        row_step = lax.broadcasted_iota(jnp.int32, (steps * heads, 1), 0) // heads
        fresh = [
            fresh_ref[step, 0].astype(jnp.float32)[request : request + 1] for step in range(steps)
        ]
        pad = jnp.zeros((16 - steps, lat), jnp.float32)
        fresh_keys = jnp.concatenate(fresh + [pad], 0).astype(jnp.bfloat16)
        fresh_all = (
            lax.dot_general(
                lines, fresh_keys, (((0,), (1,)), ((), ())), preferred_element_type=jnp.float32
            )
            * scale
        )
        row_max = jnp.max(scores, 1, keepdims=True)
        fresh_scores = []
        for step in range(steps):
            one = jnp.where(row_step >= step, fresh_all[:, step : step + 1], -jnp.inf)
            row_max = jnp.maximum(row_max, one)
            fresh_scores.append(one)
        weights = jnp.exp(scores - row_max)
        fresh_weights = [jnp.exp(one - row_max) for one in fresh_scores]
        total = jnp.sum(weights, 1, keepdims=True)
        for one in fresh_weights:
            total = total + one
        share = 1.0 / total
        probs = (weights * share).astype(jnp.bfloat16)
        result = lax.dot_general(
            probs, keys[:KV_RANK], (((1,), (1,)), ((), ())), preferred_element_type=jnp.float32
        )
        for step in range(steps):
            part = (fresh_weights[step] * share).astype(jnp.bfloat16).astype(jnp.float32)
            result = result + part * fresh[step][:, :KV_RANK]
        result = result.astype(jnp.bfloat16)
        for step in range(steps):
            served[request, step] = result[step * heads : (step + 1) * heads]

    attend(1)

    mine = core * half + cell
    first_sends, pair_sends = [], []
    for c, span in enumerate(spans):
        for copy in line_sends[c]:
            copy.wait_recv()
        merged = [column[spot, span].astype(jnp.float32) for spot in range(line)]
        tokens[mine, span] = jnp.concatenate(merged, 1).astype(jnp.bfloat16)
        first_sends.append(send(tokens.at[mine, span], tokens.at[mine, span], core, first))
        pair_sends.append([send(tokens.at[mine, span], tokens.at[mine, span], other, rank)])

    attend(0)

    second_sends = []
    near_block = core * half + first_cell
    for c, span in enumerate(spans):
        first_sends[c].wait_recv()
        second_sends.append(
            [
                send(tokens.at[block, span], tokens.at[block, span], core, second)
                for block in (mine, near_block)
            ]
        )
        pair_sends[c].append(
            send(tokens.at[near_block, span], tokens.at[near_block, span], other, rank)
        )
    far_send = send(served.at[0], far, core, far_rank)
    near_send = send(served.at[1], near, core, across_side)

    gate_part = jnp.zeros((2 * half * line * own_rows, w_gate.shape[1]), jnp.float32)
    up_part = gate_part
    piece = blocks // parts
    done = 0
    for c, span in enumerate(spans):
        for copy, block in zip(second_sends[c], (core * half + second_cell, core * half + corner)):
            copy.wait_recv()
            pair_sends[c].append(
                send(tokens.at[block, span], tokens.at[block, span], other, rank)
            )
        for copy in pair_sends[c]:
            copy.wait_recv()
        while done < parts and (done + 1) * piece <= cuts[c + 1]:
            for copy in gate_loads[done]:
                copy.wait()
            pieces = [
                tokens[:, block].reshape(gate_part.shape[0], LANES)
                for block in range(done * piece, (done + 1) * piece)
            ]
            values = jnp.concatenate(pieces, 1)
            span_rows = pl.ds(done * rows, rows)
            gate_part = gate_part + jnp.dot(
                values, w_gate[span_rows], preferred_element_type=jnp.float32
            )
            up_part = up_part + jnp.dot(
                values, w_up[span_rows], preferred_element_type=jnp.float32
            )
            done += 1
    units = (gate_part / (1.0 + jnp.exp(-gate_part)) * up_part).astype(jnp.bfloat16)
    coded = tokens[:, blocks].reshape(gate_part.shape[0], LANES).astype(jnp.float32)
    lane = lax.broadcasted_iota(jnp.int32, coded.shape, 1)
    hit = (lane == rank) | (lane == rank + ranks) | (lane == rank + 2 * ranks)
    gain = jnp.sum(jnp.where(hit, coded, 0.0), 1, keepdims=True)
    down_load.wait()

    chunk = width // RETURN_CHUNKS
    side_rows = half * line * own_rows
    cell_rows = line * own_rows
    pairs, firsts, seconds, lines = {}, {}, {}, {}

    def stage_down(c):
        out = jnp.dot(
            units, w_down[:, c * chunk : (c + 1) * chunk], preferred_element_type=jnp.float32
        )
        out = out * gain
        for part in range(2):
            value = out[part * side_rows : (part + 1) * side_rows]
            own_part[c, part] = value
            pair_send[c, part] = value.astype(jnp.bfloat16)
        pairs[c] = send(pair_send.at[c, other], pair_recv.at[c], other, rank)

    def stage_chip(c):
        pairs[c].wait_recv()
        value = own_part[c, core] + pair_recv[c].astype(jnp.float32)
        for part in range(half):
            cut = value[part * cell_rows : (part + 1) * cell_rows]
            chip_part[c, part] = cut
            chip_send[c, part] = cut.astype(jnp.bfloat16)
        firsts[c] = [
            send(chip_send.at[c, corner], first_recv.at[c, 1], core, second),
            send(chip_send.at[c, second_cell], first_recv.at[c, 0], core, second),
        ]

    def stage_plane(c):
        firsts[c][0].wait_recv()
        value = chip_part[c, first_cell] + first_recv[c, 1].astype(jnp.float32)
        second_send[c] = value.astype(jnp.bfloat16)
        seconds[c] = send(second_send.at[c], second_recv.at[c], core, first)
        firsts[c][1].wait_recv()
        second_keep[c] = chip_part[c, cell] + first_recv[c, 0].astype(jnp.float32)

    def stage_line(c):
        seconds[c].wait_recv()
        value = second_keep[c] + second_recv[c].astype(jnp.float32)
        for spot in range(line):
            cut = value[spot * own_rows : (spot + 1) * own_rows]
            line_part[c, spot] = cut
            line_send[c, spot] = cut.astype(jnp.bfloat16)
        lines[c] = [
            send(
                line_send.at[c, lax.rem(place + step, line)],
                line_recv.at[c, step - 1],
                core,
                lax.rem(rank + 4 * step, ranks),
            )
            for step in range(1, line)
        ]

    def stage_sum(c):
        value = line_part[c, place]
        for step in range(1, line):
            lines[c][step - 1].wait_recv()
            value = value + line_recv[c, step - 1].astype(jnp.float32)
        value = value.astype(jnp.bfloat16)
        for step in range(steps):
            moe_ref[step, 0, :, c * chunk : (c + 1) * chunk] = value[
                step * requests : (step + 1) * requests
            ]

    stages = (stage_down, stage_chip, stage_plane, stage_line, stage_sum)
    stores = []

    def settle(request, value):
        moved[request] = value
        stores.append(load(moved.at[request], attended_hbm.at[:, 0, request]))

    for turn in range(RETURN_CHUNKS + len(stages) - 1):
        for depth, stage in enumerate(stages):
            if 0 <= turn - depth < RETURN_CHUNKS:
                stage(turn - depth)
        if turn == 1:
            near_send.wait_recv()
            onward_send = send(near, onward, core, onward_rank)
        if turn == RETURN_CHUNKS + 2:
            far_send.wait_recv()
            settle(0, jnp.where(homes_ref[0, rank] == rank, served[0], far[...]))
    onward_send.wait_recv()
    home = homes_ref[1, rank]
    arrived = jnp.where(home == across_side, near[...], onward[...])
    settle(1, jnp.where(home == rank, served[1], arrived))
    for copy in sends:
        copy.wait_send()
    for copy in stores:
        copy.wait()


def ladder(
    latent_cache,
    lengths,
    new_home,
    queries,
    new_latent,
    hidden,
    routes,
    route_logits,
    w_gate,
    w_up,
    w_down,
):
    ranks, slices = lax.axis_size("ep"), lax.axis_size("dp")
    line = ranks // 4
    steps, _, requests, width = hidden.shape
    heads, lat = queries.shape[3:]
    keys = latent_cache.shape[2]
    units = w_gate.shape[2]
    layers = width // LANES + 1
    own_rows = steps * requests
    chunk = width // RETURN_CHUNKS
    cell_rows = line * own_rows
    bf16, f32 = jnp.bfloat16, jnp.float32
    vmem = pl.BlockSpec(memory_space=pltpu.VMEM)
    smem = pl.BlockSpec(memory_space=pltpu.SMEM)
    hbm = pl.BlockSpec(memory_space=pl.ANY)
    gather_sends = GATHER_CHUNKS * (line - 1 + 1 + 2 + 4)
    return_sends = RETURN_CHUNKS * (1 + 2 + 1 + line - 1)
    sends = gather_sends + return_sends + 3
    loads = 2 * requests + 8 + 1 + requests
    return pl.pallas_call(
        functools.partial(ladder_kernel, dict(ranks=ranks, line=line)),
        out_shape=(
            jax.ShapeDtypeStruct((steps, 1, requests, heads, KV_RANK), bf16),
            jax.ShapeDtypeStruct((steps, 1, requests, width), bf16),
        ),
        in_specs=[smem, smem, vmem, vmem, vmem, vmem] + [hbm] * 5,
        out_specs=(hbm, vmem),
        scratch_shapes=[
            pltpu.VMEM((line, layers, own_rows, LANES), bf16),
            pltpu.VMEM((slices * 4, layers, cell_rows, LANES), bf16),
            pltpu.VMEM((requests, steps, lat, heads), bf16),
            pltpu.VMEM((requests, lat, keys), bf16),
            pltpu.VMEM((width, units), bf16),
            pltpu.VMEM((width, units), bf16),
            pltpu.VMEM((units, width), bf16),
            pltpu.VMEM((requests, steps, heads, KV_RANK), bf16),
            pltpu.VMEM((steps, heads, KV_RANK), bf16),
            pltpu.VMEM((steps, heads, KV_RANK), bf16),
            pltpu.VMEM((steps, heads, KV_RANK), bf16),
            pltpu.VMEM((requests, steps, heads, KV_RANK), bf16),
            pltpu.VMEM((RETURN_CHUNKS, 2, 4 * cell_rows, chunk), f32),
            pltpu.VMEM((RETURN_CHUNKS, 2, 4 * cell_rows, chunk), bf16),
            pltpu.VMEM((RETURN_CHUNKS, 4 * cell_rows, chunk), bf16),
            pltpu.VMEM((RETURN_CHUNKS, 4, cell_rows, chunk), f32),
            pltpu.VMEM((RETURN_CHUNKS, 4, cell_rows, chunk), bf16),
            pltpu.VMEM((RETURN_CHUNKS, 2, cell_rows, chunk), bf16),
            pltpu.VMEM((RETURN_CHUNKS, cell_rows, chunk), f32),
            pltpu.VMEM((RETURN_CHUNKS, cell_rows, chunk), bf16),
            pltpu.VMEM((RETURN_CHUNKS, cell_rows, chunk), bf16),
            pltpu.VMEM((RETURN_CHUNKS, line, own_rows, chunk), f32),
            pltpu.VMEM((RETURN_CHUNKS, line, own_rows, chunk), bf16),
            pltpu.VMEM((RETURN_CHUNKS, line - 1, own_rows, chunk), bf16),
            pltpu.SemaphoreType.DMA((loads,)),
            pltpu.SemaphoreType.DMA((sends,)),
            pltpu.SemaphoreType.DMA((sends,)),
        ],
        compiler_params=pltpu.CompilerParams(
            collective_id=0, has_side_effects=True, vmem_limit_bytes=56 * 1024 * 1024
        ),
        name="ladder",
    )(
        lengths.T,
        new_home.T,
        new_latent,
        hidden,
        routes,
        route_logits,
        jnp.swapaxes(latent_cache, 2, 3),
        jnp.swapaxes(queries, 3, 4),
        w_gate,
        w_up,
        w_down,
    )


def attend_kernel(length_ref, query_ref, cache_ref, fresh_ref, out_ref):
    step_count, head_count, lat_width = query_ref.shape
    rows = step_count * head_count
    length = length_ref[pl.program_id(0)]
    scale = HEAD_QK ** (-0.5)
    query = query_ref[...].reshape(rows, lat_width)
    keys = cache_ref[...]
    scores = (
        lax.dot_general(
            query, keys, (((1,), (1,)), ((), ())), preferred_element_type=jnp.float32
        )
        * scale
    )
    place = lax.broadcasted_iota(jnp.int32, scores.shape, 1)
    scores = jnp.where(place < length, scores, -jnp.inf)
    row_step = lax.broadcasted_iota(jnp.int32, (rows, 1), 0) // head_count
    wide_query = query.astype(jnp.float32)
    fresh = fresh_ref[...].astype(jnp.float32)
    fresh_scores = []
    row_max = jnp.max(scores, 1, keepdims=True)
    for step in range(step_count):
        one = jnp.sum(wide_query * fresh[step : step + 1], 1, keepdims=True) * scale
        one = jnp.where(row_step >= step, one, -jnp.inf)
        row_max = jnp.maximum(row_max, one)
        fresh_scores.append(one)
    weights = jnp.exp(scores - row_max)
    fresh_weights = [jnp.exp(one - row_max) for one in fresh_scores]
    total = jnp.sum(weights, 1, keepdims=True)
    for one in fresh_weights:
        total = total + one
    probs = (weights / total).astype(jnp.bfloat16)
    served = jnp.dot(probs, keys[:, :KV_RANK], preferred_element_type=jnp.float32)
    for step in range(step_count):
        part = (fresh_weights[step] / total).astype(jnp.bfloat16).astype(jnp.float32)
        served = served + part * fresh[step : step + 1, :KV_RANK]
    out_ref[...] = served.astype(jnp.bfloat16).reshape(step_count, head_count, KV_RANK)


def attend(own_lengths, queries, cache, fresh):
    step_count, _, requests, heads, lat = queries.shape
    keys = cache.shape[2]
    return pl.pallas_call(
        attend_kernel,
        grid_spec=pltpu.PrefetchScalarGridSpec(
            num_scalar_prefetch=1,
            grid=(requests,),
            in_specs=[
                pl.BlockSpec((step_count, None, None, heads, lat), lambda r, n: (0, 0, r, 0, 0)),
                pl.BlockSpec((None, None, keys, lat), lambda r, n: (0, r, 0, 0)),
                pl.BlockSpec((None, step_count, lat), lambda r, n: (r, 0, 0)),
            ],
            out_specs=pl.BlockSpec((None, step_count, heads, KV_RANK), lambda r, n: (r, 0, 0, 0)),
        ),
        out_shape=jax.ShapeDtypeStruct((requests, step_count, heads, KV_RANK), jnp.bfloat16),
        name="attend",
    )(own_lengths, queries, cache, fresh)


def travel(even, odd, ranks):
    half = ranks // 2
    across = [(e, (e + half) % ranks) for e in range(ranks)]
    ahead = [(e, (e + 1) % ranks) for e in range(ranks)]
    behind = [(e, (e - 1) % ranks) for e in range(ranks)]
    far = lax.ppermute(even, "ep", across)
    left = lax.ppermute(odd, "ep", ahead)
    right = lax.ppermute(odd, "ep", behind)
    return far, left, right


def relocate(computed, arrived, new_home, ranks, own_rank):
    requests = computed.shape[0]
    far, left, right = arrived
    anchor = new_home[own_rank]
    results = []
    for request in range(requests):
        home, slot = anchor[request], request // 2
        if request % 2 == 0:
            moved = far[slot]
        else:
            moved = jnp.where(home == (own_rank + 1) % ranks, right[slot], left[slot])
        results.append(jnp.where(home == own_rank, computed[request], moved))
    return jnp.stack(results, 1)[:, None]


def shards(
    latent_cache,
    lengths,
    new_home,
    queries,
    new_latent,
    hidden,
    routes,
    route_logits,
    w_gate,
    w_up,
    w_down,
):
    ranks = lax.axis_size("ep")
    own_rank = lax.axis_index("ep")
    step_count, _, requests, width = hidden.shape
    own_rows = step_count * requests
    slices = lax.axis_size("dp")

    def shift(value, step):
        return lax.ppermute(value, "dp", [(i, (i + step) % slices) for i in range(slices)])

    rows = hidden.reshape(own_rows, width)
    copies = jnp.broadcast_to(rows[None], (ranks, own_rows, width))
    mine = lax.all_to_all(copies, "ep", split_axis=0, concat_axis=0, tiled=True)
    mine = mine.reshape(ranks * own_rows, width)

    computed = attend(
        lengths[own_rank], queries, latent_cache, jnp.swapaxes(new_latent[:, 0], 0, 1)
    )
    mine, computed, even, odd = lax.optimization_barrier(
        (mine, computed, computed[0::2], computed[1::2])
    )
    arrived = travel(even, odd, ranks)

    tokens = jnp.concatenate([mine] + [shift(mine, step) for step in range(1, slices)], 0)
    gate_part = jnp.dot(tokens, w_gate[0], preferred_element_type=jnp.float32)
    up_part = jnp.dot(tokens, w_up[0], preferred_element_type=jnp.float32)
    units = (jax.nn.silu(gate_part) * up_part).astype(jnp.bfloat16)
    slice_out = jnp.dot(units, w_down[0], preferred_element_type=jnp.float32)
    slice_out = slice_out.astype(jnp.bfloat16)
    parts = slice_out.reshape(slices, ranks * own_rows, width)
    whole = parts[0].astype(jnp.float32)
    for step in range(1, slices):
        whole = whole + shift(parts[step], -step).astype(jnp.float32)
    whole = whole.astype(jnp.bfloat16)
    whole, arrived = lax.optimization_barrier((whole, arrived))
    returned = lax.all_to_all(
        whole.reshape(ranks, own_rows, width), "ep", split_axis=0, concat_axis=0, tiled=True
    )

    attended = relocate(computed, arrived, new_home, ranks, own_rank)
    sigmoid_part = jax.nn.sigmoid(route_logits[:, 0].astype(jnp.float32))
    gates = 2.5 * sigmoid_part / jnp.sum(sigmoid_part, -1, keepdims=True)
    rank_ids = jnp.arange(ranks, dtype=jnp.int32)
    chosen = routes[:, 0, :, :, None] == rank_ids
    dense = jnp.sum(jnp.where(chosen, gates[..., None], 0.0), 2).reshape(own_rows, ranks)
    summed = jnp.sum(returned.astype(jnp.float32) * dense.T[:, :, None], 0)
    moe_out = summed.astype(jnp.bfloat16).reshape(step_count, 1, requests, width)
    return (attended, moe_out)


def solution(mesh):
    placed = (
        P("ep", "dp", None, None),
        P(None, "dp"),
        P(None, "dp"),
        P(None, "ep", "dp", None, None),
        P(None, "ep", "dp", None),
        P(None, "ep", "dp", None),
        P(None, "ep", "dp", None),
        P(None, "ep", "dp", None),
        P("ep", None, "dp"),
        P("ep", None, "dp"),
        P("ep", "dp", None),
    )
    out_specs = (P(None, "ep", "dp", None, None), P(None, "ep", "dp", None))
    ranks = mesh.shape["ep"]
    if mesh.shape["dp"] == 2 and ranks % 8 == 0 and 3 * ranks <= LANES:
        return jax.shard_map(
            ladder, mesh=mesh, in_specs=placed, out_specs=out_specs, check_vma=False
        )
    return jax.shard_map(
        shards,
        mesh=mesh,
        in_specs=placed,
        out_specs=out_specs,
        check_vma=False,
    )
```

```python
import functools

import jax
import jax.numpy as jnp
from jax import lax
from jax.experimental import pallas as pl
from jax.experimental.pallas import tpu as pltpu
from jax.sharding import PartitionSpec as P


KV_RANK = 512
HEAD_QK = 192
LANES = 128
MESH = pl.DeviceIdType.MESH
GATHER_CHUNKS = 2
RETURN_CHUNKS = 4


def ladder_kernel(
    plan,
    lengths_hbm,
    homes_hbm,
    fresh_hbm,
    hidden_hbm,
    routes_hbm,
    logits_hbm,
    cache_hbm,
    query_hbm,
    gate_hbm,
    up_hbm,
    down_hbm,
    attended_hbm,
    moe_hbm,
    lengths_ref,
    homes_ref,
    fresh_ref,
    hidden_ref,
    routes_ref,
    logits_ref,
    moe_ref,
    column,
    tokens,
    query,
    cache,
    w_gate,
    w_up,
    w_down,
    served,
    far,
    near,
    onward,
    moved,
    own_part,
    pair_send,
    pair_recv,
    chip_part,
    chip_send,
    first_recv,
    second_keep,
    second_send,
    second_recv,
    line_part,
    line_send,
    line_recv,
    load_sem,
    send_sem,
    recv_sem,
):
    ranks, line = plan["ranks"], plan["line"]
    steps, requests = hidden_ref.shape[0], hidden_ref.shape[2]
    own_rows = steps * requests
    lat = cache.shape[1]
    heads = query.shape[-1]
    width = hidden_ref.shape[-1]
    blocks = width // LANES
    layers = blocks + 1
    half = 4
    core = lax.axis_index("dp")
    rank = lax.axis_index("ep")
    side, up, place = lax.rem(rank, 2), lax.rem(lax.div(rank, 2), 2), lax.div(rank, 4)
    cell = lax.rem(rank, 4)
    across_side, across_up = rank + 1 - 2 * side, rank + 2 - 4 * up
    first = across_up * (1 - core) + across_side * core
    second = across_side * (1 - core) + across_up * core
    first_cell, corner = lax.rem(first, 4), 3 - cell
    second_cell = lax.rem(second, 4)
    other = 1 - core
    far_rank = lax.rem(rank + ranks // 2, ranks)
    onward_rank = lax.rem(rank + 2 - 4 * side + ranks, ranks)

    loads, sends = [], []

    def load(source, target):
        copy = pltpu.make_async_copy(source, target, load_sem.at[len(loads)])
        copy.start()
        loads.append(copy)
        return copy

    def send(source, target, to_core, to_rank):
        spot = len(sends)
        copy = pltpu.make_async_remote_copy(
            src_ref=source,
            dst_ref=target,
            send_sem=send_sem.at[spot],
            recv_sem=recv_sem.at[spot],
            device_id=(to_core, to_rank),
            device_id_type=MESH,
        )
        copy.start()
        sends.append(copy)
        return copy

    barrier = pltpu.get_barrier_semaphore()
    peers = [(other, rank), (core, across_side), (core, across_up)]
    peers += [(core, lax.rem(rank + 4 * step, ranks)) for step in range(1, line)]
    for peer in peers:
        pl.semaphore_signal(barrier, inc=1, device_id=peer, device_id_type=MESH)

    token_loads = [
        load(hidden_hbm, hidden_ref),
        load(routes_hbm, routes_ref),
        load(logits_hbm, logits_ref),
    ]
    small_loads = [
        load(fresh_hbm, fresh_ref),
        load(lengths_hbm, lengths_ref),
        load(homes_hbm, homes_ref),
    ]
    attend_loads = {}
    for request in reversed(range(requests)):
        attend_loads[request] = (
            load(query_hbm.at[:, 0, request], query.at[request]),
            load(cache_hbm.at[0, request], cache.at[request]),
        )
    parts = 4
    rows = width // parts
    gate_loads = []
    for part in range(parts):
        span = pl.ds(part * rows, rows)
        gate_loads.append(
            (load(gate_hbm.at[0, span], w_gate.at[span]), load(up_hbm.at[0, span], w_up.at[span]))
        )
    down_load = load(down_hbm.at[0], w_down)

    for copy in token_loads:
        copy.wait()
    lane = lax.broadcasted_iota(jnp.int32, (requests, LANES), 1)
    expert = lane - jnp.where(lane >= 2 * ranks, 2 * ranks, jnp.where(lane >= ranks, ranks, 0))
    dense = []
    for step in range(steps):
        logits = logits_ref[step, 0].astype(jnp.float32)
        chosen = routes_ref[step, 0]
        sigmoid_part = 1.0 / (1.0 + jnp.exp(-logits))
        gates = 2.5 * sigmoid_part / jnp.sum(sigmoid_part, 1, keepdims=True)
        total = jnp.zeros((requests, LANES), jnp.float32)
        for k in range(chosen.shape[1]):
            total = total + jnp.where(chosen[:, k : k + 1] == expert, gates[:, k : k + 1], 0.0)
        dense.append(total)
    dense = jnp.concatenate(dense, 0)
    lane = lax.broadcasted_iota(jnp.int32, (own_rows, LANES), 1)
    high = dense.astype(jnp.bfloat16).astype(jnp.float32)
    middle = (dense - high).astype(jnp.bfloat16).astype(jnp.float32)
    low = dense - high - middle
    coded = jnp.where(lane < ranks, high, jnp.where(lane < 2 * ranks, middle, low))
    coded = jnp.where(lane < 3 * ranks, coded, 0.0)
    own = jnp.concatenate(
        [hidden_ref[step, 0].astype(jnp.float32) for step in range(steps)], 0
    )
    for block in range(blocks):
        column[place, block] = own[:, block * LANES : (block + 1) * LANES].astype(jnp.bfloat16)
    column[place, blocks] = coded.astype(jnp.bfloat16)

    pl.semaphore_wait(barrier, len(peers))

    cuts = [blocks * c // GATHER_CHUNKS for c in range(GATHER_CHUNKS)] + [layers]
    spans = [pl.ds(cuts[c], cuts[c + 1] - cuts[c]) for c in range(GATHER_CHUNKS)]
    line_sends = []
    for span in spans:
        line_sends.append(
            [
                send(
                    column.at[place, span],
                    column.at[place, span],
                    core,
                    lax.rem(rank + 4 * step, ranks),
                )
                for step in range(1, line)
            ]
        )

    def attend(request):
        for copy in attend_loads[request]:
            copy.wait()
        length = lengths_ref[request, rank]
        scale = HEAD_QK ** (-0.5)
        lines = jnp.concatenate([query[request, step] for step in range(steps)], 1)
        keys = cache[request]
        scores = (
            lax.dot_general(
                lines, keys, (((0,), (0,)), ((), ())), preferred_element_type=jnp.float32
            )
            * scale
        )
        spot = lax.broadcasted_iota(jnp.int32, scores.shape, 1)
        scores = jnp.where(spot < length, scores, -jnp.inf)
        row_step = lax.broadcasted_iota(jnp.int32, (steps * heads, 1), 0) // heads
        fresh = [
            fresh_ref[step, 0].astype(jnp.float32)[request : request + 1] for step in range(steps)
        ]
        pad = jnp.zeros((16 - steps, lat), jnp.float32)
        fresh_keys = jnp.concatenate(fresh + [pad], 0).astype(jnp.bfloat16)
        fresh_all = (
            lax.dot_general(
                lines, fresh_keys, (((0,), (1,)), ((), ())), preferred_element_type=jnp.float32
            )
            * scale
        )
        row_max = jnp.max(scores, 1, keepdims=True)
        fresh_scores = []
        for step in range(steps):
            one = jnp.where(row_step >= step, fresh_all[:, step : step + 1], -jnp.inf)
            row_max = jnp.maximum(row_max, one)
            fresh_scores.append(one)
        weights = jnp.exp(scores - row_max)
        fresh_weights = [jnp.exp(one - row_max) for one in fresh_scores]
        total = jnp.sum(weights, 1, keepdims=True)
        for one in fresh_weights:
            total = total + one
        share = 1.0 / total
        probs = (weights * share).astype(jnp.bfloat16)
        result = lax.dot_general(
            probs, keys[:KV_RANK], (((1,), (1,)), ((), ())), preferred_element_type=jnp.float32
        )
        for step in range(steps):
            part = (fresh_weights[step] * share).astype(jnp.bfloat16).astype(jnp.float32)
            result = result + part * fresh[step][:, :KV_RANK]
        result = result.astype(jnp.bfloat16)
        for step in range(steps):
            served[request, step] = result[step * heads : (step + 1) * heads]

    for copy in small_loads:
        copy.wait()
    attend(1)
    near_sends = [send(served.at[1, 0], near.at[0], core, across_side)]
    attend(0)
    far_sends = [send(served.at[0, step], far.at[step], core, far_rank) for step in range(steps)]

    mine = core * half + cell
    first_sends, pair_sends = [], []
    for c, span in enumerate(spans):
        for copy in line_sends[c]:
            copy.wait_recv()
        merged = [column[spot, span].astype(jnp.float32) for spot in range(line)]
        tokens[mine, span] = jnp.concatenate(merged, 1).astype(jnp.bfloat16)
        first_sends.append(send(tokens.at[mine, span], tokens.at[mine, span], core, first))
        pair_sends.append([send(tokens.at[mine, span], tokens.at[mine, span], other, rank)])

    second_sends = []
    near_block = core * half + first_cell
    for c, span in enumerate(spans):
        first_sends[c].wait_recv()
        second_sends.append(
            [
                send(tokens.at[block, span], tokens.at[block, span], core, second)
                for block in (mine, near_block)
            ]
        )
        pair_sends[c].append(
            send(tokens.at[near_block, span], tokens.at[near_block, span], other, rank)
        )

    gate_part = jnp.zeros((2 * half * line * own_rows, w_gate.shape[1]), jnp.float32)
    up_part = gate_part
    piece = blocks // parts
    done = 0
    for c, span in enumerate(spans):
        for copy, block in zip(second_sends[c], (core * half + second_cell, core * half + corner)):
            copy.wait_recv()
            pair_sends[c].append(
                send(tokens.at[block, span], tokens.at[block, span], other, rank)
            )
        if c == GATHER_CHUNKS - 1:
            near_sends += [
                send(served.at[1, step], near.at[step], core, across_side)
                for step in range(1, steps)
            ]
            near_sends[0].wait_recv()
            onward_sends = [send(near.at[0], onward.at[0], core, onward_rank)]
        for copy in pair_sends[c]:
            copy.wait_recv()
        while done < parts and (done + 1) * piece <= cuts[c + 1]:
            for copy in gate_loads[done]:
                copy.wait()
            pieces = [
                tokens[:, block].reshape(gate_part.shape[0], LANES)
                for block in range(done * piece, (done + 1) * piece)
            ]
            values = jnp.concatenate(pieces, 1)
            span_rows = pl.ds(done * rows, rows)
            gate_part = gate_part + jnp.dot(
                values, w_gate[span_rows], preferred_element_type=jnp.float32
            )
            up_part = up_part + jnp.dot(
                values, w_up[span_rows], preferred_element_type=jnp.float32
            )
            done += 1
    units = (gate_part / (1.0 + jnp.exp(-gate_part)) * up_part).astype(jnp.bfloat16)
    coded = tokens[:, blocks].reshape(gate_part.shape[0], LANES).astype(jnp.float32)
    lane = lax.broadcasted_iota(jnp.int32, coded.shape, 1)
    hit = (lane == rank) | (lane == rank + ranks) | (lane == rank + 2 * ranks)
    gain = jnp.sum(jnp.where(hit, coded, 0.0), 1, keepdims=True)
    down_load.wait()

    chunk = width // RETURN_CHUNKS
    side_rows = half * line * own_rows
    cell_rows = line * own_rows
    pairs, firsts, seconds, lines = {}, {}, {}, {}

    def stage_down(c):
        out = jnp.dot(
            units, w_down[:, c * chunk : (c + 1) * chunk], preferred_element_type=jnp.float32
        )
        out = out * gain
        for part in range(2):
            value = out[part * side_rows : (part + 1) * side_rows]
            own_part[c, part] = value
            pair_send[c, part] = value.astype(jnp.bfloat16)
        pairs[c] = send(pair_send.at[c, other], pair_recv.at[c], other, rank)

    def stage_chip(c):
        pairs[c].wait_recv()
        value = own_part[c, core] + pair_recv[c].astype(jnp.float32)
        for part in range(half):
            cut = value[part * cell_rows : (part + 1) * cell_rows]
            chip_part[c, part] = cut
            chip_send[c, part] = cut.astype(jnp.bfloat16)
        firsts[c] = [
            send(chip_send.at[c, corner], first_recv.at[c, 1], core, second),
            send(chip_send.at[c, second_cell], first_recv.at[c, 0], core, second),
        ]

    def stage_plane(c):
        firsts[c][0].wait_recv()
        value = chip_part[c, first_cell] + first_recv[c, 1].astype(jnp.float32)
        second_send[c] = value.astype(jnp.bfloat16)
        seconds[c] = send(second_send.at[c], second_recv.at[c], core, first)
        firsts[c][1].wait_recv()
        second_keep[c] = chip_part[c, cell] + first_recv[c, 0].astype(jnp.float32)

    def stage_line(c):
        seconds[c].wait_recv()
        value = second_keep[c] + second_recv[c].astype(jnp.float32)
        for spot in range(line):
            cut = value[spot * own_rows : (spot + 1) * own_rows]
            line_part[c, spot] = cut
            line_send[c, spot] = cut.astype(jnp.bfloat16)
        lines[c] = [
            send(
                line_send.at[c, lax.rem(place + step, line)],
                line_recv.at[c, step - 1],
                core,
                lax.rem(rank + 4 * step, ranks),
            )
            for step in range(1, line)
        ]

    def stage_sum(c):
        value = line_part[c, place]
        for step in range(1, line):
            lines[c][step - 1].wait_recv()
            value = value + line_recv[c, step - 1].astype(jnp.float32)
        value = value.astype(jnp.bfloat16)
        for step in range(steps):
            moe_ref[step, 0, :, c * chunk : (c + 1) * chunk] = value[
                step * requests : (step + 1) * requests
            ]

    stores = []

    def settle(request, step):
        home = homes_ref[request, rank]
        arrived = far[step]
        if request % 2:
            arrived = jnp.where(home == across_side, near[step], onward[step])
        moved[request, step] = jnp.where(home == rank, served[request, step], arrived)
        stores.append(load(moved.at[request, step], attended_hbm.at[step, 0, request]))

    for c in range(RETURN_CHUNKS):
        stage_down(c)
    for c in range(RETURN_CHUNKS):
        stage_chip(c)
    for c in range(RETURN_CHUNKS):
        stage_plane(c)
    for step in range(1, steps):
        near_sends[step].wait_recv()
        onward_sends.append(send(near.at[step], onward.at[step], core, onward_rank))
    for c in range(RETURN_CHUNKS):
        stage_line(c)
    for step in range(steps):
        far_sends[step].wait_recv()
        settle(0, step)
    onward_sends[0].wait_recv()
    settle(1, 0)
    for c in range(RETURN_CHUNKS):
        stage_sum(c)
    stores.append(load(moe_ref, moe_hbm))
    for step in range(1, steps):
        onward_sends[step].wait_recv()
        settle(1, step)
    for copy in sends:
        copy.wait_send()
    for copy in stores:
        copy.wait()


def ladder(
    latent_cache,
    lengths,
    new_home,
    queries,
    new_latent,
    hidden,
    routes,
    route_logits,
    w_gate,
    w_up,
    w_down,
):
    ranks, slices = lax.axis_size("ep"), lax.axis_size("dp")
    line = ranks // 4
    steps, _, requests, width = hidden.shape
    heads, lat = queries.shape[3:]
    keys = latent_cache.shape[2]
    units = w_gate.shape[2]
    layers = width // LANES + 1
    own_rows = steps * requests
    chunk = width // RETURN_CHUNKS
    cell_rows = line * own_rows
    bf16, f32 = jnp.bfloat16, jnp.float32
    hbm = pl.BlockSpec(memory_space=pl.ANY)
    gather_sends = GATHER_CHUNKS * (line - 1 + 1 + 2 + 4)
    return_sends = RETURN_CHUNKS * (1 + 2 + 1 + line - 1)
    sends = gather_sends + return_sends + 3 * steps
    loads = 6 + 2 * requests + 8 + 1 + requests * steps + 1
    return pl.pallas_call(
        functools.partial(ladder_kernel, dict(ranks=ranks, line=line)),
        out_shape=(
            jax.ShapeDtypeStruct((steps, 1, requests, heads, KV_RANK), bf16),
            jax.ShapeDtypeStruct((steps, 1, requests, width), bf16),
        ),
        in_specs=[hbm] * 11,
        out_specs=(hbm, hbm),
        scratch_shapes=[
            pltpu.SMEM((requests, ranks), jnp.int32),
            pltpu.SMEM((requests, ranks), jnp.int32),
            pltpu.VMEM(new_latent.shape, bf16),
            pltpu.VMEM(hidden.shape, bf16),
            pltpu.VMEM(routes.shape, jnp.int32),
            pltpu.VMEM(route_logits.shape, bf16),
            pltpu.VMEM(hidden.shape, bf16),
            pltpu.VMEM((line, layers, own_rows, LANES), bf16),
            pltpu.VMEM((slices * 4, layers, cell_rows, LANES), bf16),
            pltpu.VMEM((requests, steps, lat, heads), bf16),
            pltpu.VMEM((requests, lat, keys), bf16),
            pltpu.VMEM((width, units), bf16),
            pltpu.VMEM((width, units), bf16),
            pltpu.VMEM((units, width), bf16),
            pltpu.VMEM((requests, steps, heads, KV_RANK), bf16),
            pltpu.VMEM((steps, heads, KV_RANK), bf16),
            pltpu.VMEM((steps, heads, KV_RANK), bf16),
            pltpu.VMEM((steps, heads, KV_RANK), bf16),
            pltpu.VMEM((requests, steps, heads, KV_RANK), bf16),
            pltpu.VMEM((RETURN_CHUNKS, 2, 4 * cell_rows, chunk), f32),
            pltpu.VMEM((RETURN_CHUNKS, 2, 4 * cell_rows, chunk), bf16),
            pltpu.VMEM((RETURN_CHUNKS, 4 * cell_rows, chunk), bf16),
            pltpu.VMEM((RETURN_CHUNKS, 4, cell_rows, chunk), f32),
            pltpu.VMEM((RETURN_CHUNKS, 4, cell_rows, chunk), bf16),
            pltpu.VMEM((RETURN_CHUNKS, 2, cell_rows, chunk), bf16),
            pltpu.VMEM((RETURN_CHUNKS, cell_rows, chunk), f32),
            pltpu.VMEM((RETURN_CHUNKS, cell_rows, chunk), bf16),
            pltpu.VMEM((RETURN_CHUNKS, cell_rows, chunk), bf16),
            pltpu.VMEM((RETURN_CHUNKS, line, own_rows, chunk), f32),
            pltpu.VMEM((RETURN_CHUNKS, line, own_rows, chunk), bf16),
            pltpu.VMEM((RETURN_CHUNKS, line - 1, own_rows, chunk), bf16),
            pltpu.SemaphoreType.DMA((loads,)),
            pltpu.SemaphoreType.DMA((sends,)),
            pltpu.SemaphoreType.DMA((sends,)),
        ],
        compiler_params=pltpu.CompilerParams(
            collective_id=0, has_side_effects=True, vmem_limit_bytes=56 * 1024 * 1024
        ),
        name="ladder",
    )(
        lengths.T,
        new_home.T,
        new_latent,
        hidden,
        routes,
        route_logits,
        jnp.swapaxes(latent_cache, 2, 3),
        jnp.swapaxes(queries, 3, 4),
        w_gate,
        w_up,
        w_down,
    )


def attend_kernel(length_ref, query_ref, cache_ref, fresh_ref, out_ref):
    step_count, head_count, lat_width = query_ref.shape
    rows = step_count * head_count
    length = length_ref[pl.program_id(0)]
    scale = HEAD_QK ** (-0.5)
    query = query_ref[...].reshape(rows, lat_width)
    keys = cache_ref[...]
    scores = (
        lax.dot_general(
            query, keys, (((1,), (1,)), ((), ())), preferred_element_type=jnp.float32
        )
        * scale
    )
    place = lax.broadcasted_iota(jnp.int32, scores.shape, 1)
    scores = jnp.where(place < length, scores, -jnp.inf)
    row_step = lax.broadcasted_iota(jnp.int32, (rows, 1), 0) // head_count
    wide_query = query.astype(jnp.float32)
    fresh = fresh_ref[...].astype(jnp.float32)
    fresh_scores = []
    row_max = jnp.max(scores, 1, keepdims=True)
    for step in range(step_count):
        one = jnp.sum(wide_query * fresh[step : step + 1], 1, keepdims=True) * scale
        one = jnp.where(row_step >= step, one, -jnp.inf)
        row_max = jnp.maximum(row_max, one)
        fresh_scores.append(one)
    weights = jnp.exp(scores - row_max)
    fresh_weights = [jnp.exp(one - row_max) for one in fresh_scores]
    total = jnp.sum(weights, 1, keepdims=True)
    for one in fresh_weights:
        total = total + one
    probs = (weights / total).astype(jnp.bfloat16)
    served = jnp.dot(probs, keys[:, :KV_RANK], preferred_element_type=jnp.float32)
    for step in range(step_count):
        part = (fresh_weights[step] / total).astype(jnp.bfloat16).astype(jnp.float32)
        served = served + part * fresh[step : step + 1, :KV_RANK]
    out_ref[...] = served.astype(jnp.bfloat16).reshape(step_count, head_count, KV_RANK)


def attend(own_lengths, queries, cache, fresh):
    step_count, _, requests, heads, lat = queries.shape
    keys = cache.shape[2]
    return pl.pallas_call(
        attend_kernel,
        grid_spec=pltpu.PrefetchScalarGridSpec(
            num_scalar_prefetch=1,
            grid=(requests,),
            in_specs=[
                pl.BlockSpec((step_count, None, None, heads, lat), lambda r, n: (0, 0, r, 0, 0)),
                pl.BlockSpec((None, None, keys, lat), lambda r, n: (0, r, 0, 0)),
                pl.BlockSpec((None, step_count, lat), lambda r, n: (r, 0, 0)),
            ],
            out_specs=pl.BlockSpec((None, step_count, heads, KV_RANK), lambda r, n: (r, 0, 0, 0)),
        ),
        out_shape=jax.ShapeDtypeStruct((requests, step_count, heads, KV_RANK), jnp.bfloat16),
        name="attend",
    )(own_lengths, queries, cache, fresh)


def travel(even, odd, ranks):
    half = ranks // 2
    across = [(e, (e + half) % ranks) for e in range(ranks)]
    ahead = [(e, (e + 1) % ranks) for e in range(ranks)]
    behind = [(e, (e - 1) % ranks) for e in range(ranks)]
    far = lax.ppermute(even, "ep", across)
    left = lax.ppermute(odd, "ep", ahead)
    right = lax.ppermute(odd, "ep", behind)
    return far, left, right


def relocate(computed, arrived, new_home, ranks, own_rank):
    requests = computed.shape[0]
    far, left, right = arrived
    anchor = new_home[own_rank]
    results = []
    for request in range(requests):
        home, slot = anchor[request], request // 2
        if request % 2 == 0:
            moved = far[slot]
        else:
            moved = jnp.where(home == (own_rank + 1) % ranks, right[slot], left[slot])
        results.append(jnp.where(home == own_rank, computed[request], moved))
    return jnp.stack(results, 1)[:, None]


def shards(
    latent_cache,
    lengths,
    new_home,
    queries,
    new_latent,
    hidden,
    routes,
    route_logits,
    w_gate,
    w_up,
    w_down,
):
    ranks = lax.axis_size("ep")
    own_rank = lax.axis_index("ep")
    step_count, _, requests, width = hidden.shape
    own_rows = step_count * requests
    slices = lax.axis_size("dp")

    def shift(value, step):
        return lax.ppermute(value, "dp", [(i, (i + step) % slices) for i in range(slices)])

    rows = hidden.reshape(own_rows, width)
    copies = jnp.broadcast_to(rows[None], (ranks, own_rows, width))
    mine = lax.all_to_all(copies, "ep", split_axis=0, concat_axis=0, tiled=True)
    mine = mine.reshape(ranks * own_rows, width)

    computed = attend(
        lengths[own_rank], queries, latent_cache, jnp.swapaxes(new_latent[:, 0], 0, 1)
    )
    mine, computed, even, odd = lax.optimization_barrier(
        (mine, computed, computed[0::2], computed[1::2])
    )
    arrived = travel(even, odd, ranks)

    tokens = jnp.concatenate([mine] + [shift(mine, step) for step in range(1, slices)], 0)
    gate_part = jnp.dot(tokens, w_gate[0], preferred_element_type=jnp.float32)
    up_part = jnp.dot(tokens, w_up[0], preferred_element_type=jnp.float32)
    units = (jax.nn.silu(gate_part) * up_part).astype(jnp.bfloat16)
    slice_out = jnp.dot(units, w_down[0], preferred_element_type=jnp.float32)
    slice_out = slice_out.astype(jnp.bfloat16)
    parts = slice_out.reshape(slices, ranks * own_rows, width)
    whole = parts[0].astype(jnp.float32)
    for step in range(1, slices):
        whole = whole + shift(parts[step], -step).astype(jnp.float32)
    whole = whole.astype(jnp.bfloat16)
    whole, arrived = lax.optimization_barrier((whole, arrived))
    returned = lax.all_to_all(
        whole.reshape(ranks, own_rows, width), "ep", split_axis=0, concat_axis=0, tiled=True
    )

    attended = relocate(computed, arrived, new_home, ranks, own_rank)
    sigmoid_part = jax.nn.sigmoid(route_logits[:, 0].astype(jnp.float32))
    gates = 2.5 * sigmoid_part / jnp.sum(sigmoid_part, -1, keepdims=True)
    rank_ids = jnp.arange(ranks, dtype=jnp.int32)
    chosen = routes[:, 0, :, :, None] == rank_ids
    dense = jnp.sum(jnp.where(chosen, gates[..., None], 0.0), 2).reshape(own_rows, ranks)
    summed = jnp.sum(returned.astype(jnp.float32) * dense.T[:, :, None], 0)
    moe_out = summed.astype(jnp.bfloat16).reshape(step_count, 1, requests, width)
    return (attended, moe_out)


def solution(mesh):
    placed = (
        P("ep", "dp", None, None),
        P(None, "dp"),
        P(None, "dp"),
        P(None, "ep", "dp", None, None),
        P(None, "ep", "dp", None),
        P(None, "ep", "dp", None),
        P(None, "ep", "dp", None),
        P(None, "ep", "dp", None),
        P("ep", None, "dp"),
        P("ep", None, "dp"),
        P("ep", "dp", None),
    )
    out_specs = (P(None, "ep", "dp", None, None), P(None, "ep", "dp", None))
    ranks = mesh.shape["ep"]
    if mesh.shape["dp"] == 2 and ranks % 8 == 0 and 3 * ranks <= LANES:
        return jax.shard_map(
            ladder, mesh=mesh, in_specs=placed, out_specs=out_specs, check_vma=False
        )
    return jax.shard_map(
        shards,
        mesh=mesh,
        in_specs=placed,
        out_specs=out_specs,
        check_vma=False,
    )
```

```python
import functools

import jax
import jax.numpy as jnp
from jax import lax
from jax.experimental import pallas as pl
from jax.experimental.pallas import tpu as pltpu
from jax.sharding import PartitionSpec as P


KV_RANK = 512
HEAD_QK = 192
LANES = 128
MESH = pl.DeviceIdType.MESH
GATHER_CHUNKS = 2
RETURN_CHUNKS = 4


def ladder_kernel(
    plan,
    lengths_hbm,
    homes_hbm,
    fresh_hbm,
    hidden_hbm,
    routes_hbm,
    logits_hbm,
    cache_hbm,
    query_hbm,
    gate_hbm,
    up_hbm,
    down_hbm,
    attended_ref,
    moe_ref,
    lengths_ref,
    homes_ref,
    fresh_ref,
    hidden_ref,
    routes_ref,
    logits_ref,
    column,
    tokens,
    query,
    cache,
    w_gate,
    w_up,
    w_down,
    served,
    far,
    near,
    onward,
    beyond,
    own_part,
    pair_send,
    pair_recv,
    chip_part,
    chip_send,
    first_recv,
    second_keep,
    second_send,
    second_recv,
    line_part,
    line_send,
    line_recv,
    load_sem,
    send_sem,
    recv_sem,
):
    ranks, line = plan["ranks"], plan["line"]
    steps, requests = hidden_ref.shape[0], hidden_ref.shape[2]
    own_rows = steps * requests
    lat = cache.shape[1]
    heads = query.shape[-1]
    width = hidden_ref.shape[-1]
    blocks = width // LANES
    layers = blocks + 1
    half = 4
    core = lax.axis_index("dp")
    rank = lax.axis_index("ep")
    side, up, place = lax.rem(rank, 2), lax.rem(lax.div(rank, 2), 2), lax.div(rank, 4)
    cell = lax.rem(rank, 4)
    across_side, across_up = rank + 1 - 2 * side, rank + 2 - 4 * up
    diagonal = rank - cell + 3 - cell
    plane = (diagonal, across_side, across_up)
    other = 1 - core
    far_rank = lax.rem(rank + ranks // 2, ranks)
    beyond_rank = lax.rem(rank + 4 - 8 * side + ranks, ranks)

    loads, sends = [], []

    def load(source, target):
        copy = pltpu.make_async_copy(source, target, load_sem.at[len(loads)])
        copy.start()
        loads.append(copy)
        return copy

    def send(source, target, to_core, to_rank):
        spot = len(sends)
        copy = pltpu.make_async_remote_copy(
            src_ref=source,
            dst_ref=target,
            send_sem=send_sem.at[spot],
            recv_sem=recv_sem.at[spot],
            device_id=(to_core, to_rank),
            device_id_type=MESH,
        )
        copy.start()
        sends.append(copy)
        return copy

    barrier = pltpu.get_barrier_semaphore()
    peers = [(other, rank)] + [(core, peer) for peer in plane]
    peers += [(core, lax.rem(rank + 4 * step, ranks)) for step in range(1, line)]
    for peer in peers:
        pl.semaphore_signal(barrier, inc=1, device_id=peer, device_id_type=MESH)

    token_loads = [
        load(hidden_hbm, hidden_ref),
        load(routes_hbm, routes_ref),
        load(logits_hbm, logits_ref),
    ]
    small_loads = [
        load(fresh_hbm, fresh_ref),
        load(lengths_hbm, lengths_ref),
        load(homes_hbm, homes_ref),
    ]
    attend_loads = {}
    for request in reversed(range(requests)):
        attend_loads[request] = (
            load(query_hbm.at[:, 0, request], query.at[request]),
            load(cache_hbm.at[0, request], cache.at[request]),
        )
    parts = 4
    rows = width // parts
    gate_loads = []
    for part in range(parts):
        span = pl.ds(part * rows, rows)
        gate_loads.append(
            (load(gate_hbm.at[0, span], w_gate.at[span]), load(up_hbm.at[0, span], w_up.at[span]))
        )
    down_load = load(down_hbm.at[0], w_down)

    for copy in token_loads:
        copy.wait()
    lane = lax.broadcasted_iota(jnp.int32, (requests, LANES), 1)
    expert = lane - jnp.where(lane >= 2 * ranks, 2 * ranks, jnp.where(lane >= ranks, ranks, 0))
    dense = []
    for step in range(steps):
        logits = logits_ref[step, 0].astype(jnp.float32)
        chosen = routes_ref[step, 0]
        sigmoid_part = 1.0 / (1.0 + jnp.exp(-logits))
        gates = 2.5 * sigmoid_part / jnp.sum(sigmoid_part, 1, keepdims=True)
        total = jnp.zeros((requests, LANES), jnp.float32)
        for k in range(chosen.shape[1]):
            total = total + jnp.where(chosen[:, k : k + 1] == expert, gates[:, k : k + 1], 0.0)
        dense.append(total)
    dense = jnp.concatenate(dense, 0)
    lane = lax.broadcasted_iota(jnp.int32, (own_rows, LANES), 1)
    high = dense.astype(jnp.bfloat16).astype(jnp.float32)
    middle = (dense - high).astype(jnp.bfloat16).astype(jnp.float32)
    low = dense - high - middle
    coded = jnp.where(lane < ranks, high, jnp.where(lane < 2 * ranks, middle, low))
    coded = jnp.where(lane < 3 * ranks, coded, 0.0)
    own = jnp.concatenate(
        [hidden_ref[step, 0].astype(jnp.float32) for step in range(steps)], 0
    )
    for block in range(blocks):
        column[place, block] = own[:, block * LANES : (block + 1) * LANES].astype(jnp.bfloat16)
    column[place, blocks] = coded.astype(jnp.bfloat16)

    pl.semaphore_wait(barrier, len(peers))

    cuts = [blocks * c // GATHER_CHUNKS for c in range(GATHER_CHUNKS)] + [layers]
    spans = [pl.ds(cuts[c], cuts[c + 1] - cuts[c]) for c in range(GATHER_CHUNKS)]
    line_sends = []
    for span in spans:
        line_sends.append(
            [
                send(
                    column.at[place, span],
                    column.at[place, span],
                    core,
                    lax.rem(rank + 4 * step, ranks),
                )
                for step in range(1, line)
            ]
        )

    near_sends, onward_sends, beyond_sends, far_sends = {}, {}, {}, {}
    quarter = heads // 2

    def cut(ref, piece):
        return ref.at[piece // 2, pl.ds(piece % 2 * quarter, quarter)]

    def send_near(piece):
        near_sends[piece] = send(cut(served.at[1], piece), cut(near, piece), core, across_side)

    def send_onward(piece):
        near_sends[piece].wait_recv()
        onward_sends[piece] = send(cut(near, piece), cut(onward, piece), core, across_up)

    def send_beyond(piece):
        onward_sends[piece].wait_recv()
        beyond_sends[piece] = send(cut(onward, piece), cut(beyond, piece), core, beyond_rank)

    def attend(request):
        for copy in attend_loads[request]:
            copy.wait()
        length = lengths_ref[request, rank]
        scale = HEAD_QK ** (-0.5)
        lines = jnp.concatenate([query[request, step] for step in range(steps)], 1)
        keys = cache[request]
        scores = (
            lax.dot_general(
                lines, keys, (((0,), (0,)), ((), ())), preferred_element_type=jnp.float32
            )
            * scale
        )
        spot = lax.broadcasted_iota(jnp.int32, scores.shape, 1)
        scores = jnp.where(spot < length, scores, -jnp.inf)
        row_step = lax.broadcasted_iota(jnp.int32, (steps * heads, 1), 0) // heads
        fresh = [
            fresh_ref[step, 0].astype(jnp.float32)[request : request + 1] for step in range(steps)
        ]
        pad = jnp.zeros((16 - steps, lat), jnp.float32)
        fresh_keys = jnp.concatenate(fresh + [pad], 0).astype(jnp.bfloat16)
        fresh_all = (
            lax.dot_general(
                lines, fresh_keys, (((0,), (1,)), ((), ())), preferred_element_type=jnp.float32
            )
            * scale
        )
        row_max = jnp.max(scores, 1, keepdims=True)
        fresh_scores = []
        for step in range(steps):
            one = jnp.where(row_step >= step, fresh_all[:, step : step + 1], -jnp.inf)
            row_max = jnp.maximum(row_max, one)
            fresh_scores.append(one)
        weights = jnp.exp(scores - row_max)
        fresh_weights = [jnp.exp(one - row_max) for one in fresh_scores]
        total = jnp.sum(weights, 1, keepdims=True)
        for one in fresh_weights:
            total = total + one
        share = 1.0 / total
        probs = (weights * share).astype(jnp.bfloat16)
        result = lax.dot_general(
            probs, keys[:KV_RANK], (((1,), (1,)), ((), ())), preferred_element_type=jnp.float32
        )
        for step in range(steps):
            part = (fresh_weights[step] * share).astype(jnp.bfloat16).astype(jnp.float32)
            result = result + part * fresh[step][:, :KV_RANK]
        result = result.astype(jnp.bfloat16)
        for step in range(steps):
            served[request, step] = result[step * heads : (step + 1) * heads]

    for copy in small_loads:
        copy.wait()
    attend(1)
    send_near(0)
    send_near(1)
    attend(0)
    far_sends = [send(served.at[0, step], far.at[step], core, far_rank) for step in range(steps)]

    mine = core * half + cell
    plane_sends, pair_sends = [], []
    for c, span in enumerate(spans):
        for copy in line_sends[c]:
            copy.wait_recv()
        merged = [column[spot, span].astype(jnp.float32) for spot in range(line)]
        tokens[mine, span] = jnp.concatenate(merged, 1).astype(jnp.bfloat16)
        block = tokens.at[mine, span]
        plane_sends.append([send(block, block, core, peer) for peer in plane])
        pair_sends.append([send(block, block, other, rank)])

    send_near(2)
    send_near(3)
    gate_part = jnp.zeros((2 * half * line * own_rows, w_gate.shape[1]), jnp.float32)
    up_part = gate_part
    piece = blocks // parts
    done = 0
    for c, span in enumerate(spans):
        for copy, peer in zip(plane_sends[c], plane):
            copy.wait_recv()
            block = core * half + lax.rem(peer, 4)
            pair_sends[c].append(
                send(tokens.at[block, span], tokens.at[block, span], other, rank)
            )
        if c == GATHER_CHUNKS - 1:
            send_onward(0)
            send_onward(1)
        for copy in pair_sends[c]:
            copy.wait_recv()
        while done < parts and (done + 1) * piece <= cuts[c + 1]:
            for copy in gate_loads[done]:
                copy.wait()
            pieces = [
                tokens[:, block].reshape(gate_part.shape[0], LANES)
                for block in range(done * piece, (done + 1) * piece)
            ]
            values = jnp.concatenate(pieces, 1)
            span_rows = pl.ds(done * rows, rows)
            gate_part = gate_part + jnp.dot(
                values, w_gate[span_rows], preferred_element_type=jnp.float32
            )
            up_part = up_part + jnp.dot(
                values, w_up[span_rows], preferred_element_type=jnp.float32
            )
            done += 1
    send_onward(2)
    send_onward(3)
    units = (gate_part / (1.0 + jnp.exp(-gate_part)) * up_part).astype(jnp.bfloat16)
    coded = tokens[:, blocks].reshape(gate_part.shape[0], LANES).astype(jnp.float32)
    lane = lax.broadcasted_iota(jnp.int32, coded.shape, 1)
    hit = (lane == rank) | (lane == rank + ranks) | (lane == rank + 2 * ranks)
    gain = jnp.sum(jnp.where(hit, coded, 0.0), 1, keepdims=True)
    down_load.wait()

    chunk = width // RETURN_CHUNKS
    side_rows = half * line * own_rows
    cell_rows = line * own_rows
    pairs, firsts, seconds, lines = {}, {}, {}, {}

    def stage_down(c):
        out = jnp.dot(
            units, w_down[:, c * chunk : (c + 1) * chunk], preferred_element_type=jnp.float32
        )
        out = out * gain
        for part in range(2):
            value = out[part * side_rows : (part + 1) * side_rows]
            own_part[c, part] = value
            pair_send[c, part] = value.astype(jnp.bfloat16)
        pairs[c] = send(pair_send.at[c, other], pair_recv.at[c], other, rank)

    def route():
        turn = core
        to_second = across_side * (1 - turn) + across_up * turn
        to_first = across_up * (1 - turn) + across_side * turn
        return to_first, to_second

    def stage_chip(c):
        _, second = route()
        pairs[c].wait_recv()
        value = own_part[c, core] + pair_recv[c].astype(jnp.float32)
        for part in range(half):
            cut = value[part * cell_rows : (part + 1) * cell_rows]
            chip_part[c, part] = cut
            chip_send[c, part] = cut.astype(jnp.bfloat16)
        firsts[c] = [
            send(chip_send.at[c, 3 - cell], first_recv.at[c, 1], core, second),
            send(chip_send.at[c, lax.rem(second, 4)], first_recv.at[c, 0], core, second),
        ]

    def stage_plane(c):
        first, _ = route()
        firsts[c][0].wait_recv()
        value = chip_part[c, lax.rem(first, 4)] + first_recv[c, 1].astype(jnp.float32)
        second_send[c] = value.astype(jnp.bfloat16)
        seconds[c] = send(second_send.at[c], second_recv.at[c], core, first)
        firsts[c][1].wait_recv()
        second_keep[c] = chip_part[c, cell] + first_recv[c, 0].astype(jnp.float32)

    def stage_line(c):
        seconds[c].wait_recv()
        value = second_keep[c] + second_recv[c].astype(jnp.float32)
        for spot in range(line):
            cut = value[spot * own_rows : (spot + 1) * own_rows]
            line_part[c, spot] = cut
            line_send[c, spot] = cut.astype(jnp.bfloat16)
        lines[c] = [
            send(
                line_send.at[c, lax.rem(place + step, line)],
                line_recv.at[c, step - 1],
                core,
                lax.rem(rank + 4 * step, ranks),
            )
            for step in range(1, line)
        ]

    def stage_sum(c):
        value = line_part[c, place]
        for step in range(1, line):
            lines[c][step - 1].wait_recv()
            value = value + line_recv[c, step - 1].astype(jnp.float32)
        value = value.astype(jnp.bfloat16)
        for step in range(steps):
            moe_ref[step, 0, :, c * chunk : (c + 1) * chunk] = value[
                step * requests : (step + 1) * requests
            ]

    def settle(request, step):
        home = homes_ref[request, rank]
        arrived = far[step]
        if request % 2:
            arrived = jnp.where(side == up, beyond[step], onward[step])
            arrived = jnp.where(home == across_side, near[step], arrived)
        attended_ref[step, 0, request] = jnp.where(home == rank, served[request, step], arrived)

    for c in range(RETURN_CHUNKS):
        stage_down(c)
    send_beyond(0)
    send_beyond(1)
    for c in range(RETURN_CHUNKS):
        stage_chip(c)
    send_beyond(2)
    send_beyond(3)
    for c in range(RETURN_CHUNKS):
        stage_plane(c)
    for c in range(RETURN_CHUNKS):
        stage_line(c)
    for step in range(steps):
        far_sends[step].wait_recv()
        settle(0, step)
    for piece in (0, 1):
        beyond_sends[piece].wait_recv()
    settle(1, 0)
    for c in range(RETURN_CHUNKS):
        stage_sum(c)
    for step in range(1, steps):
        for piece in (2, 3):
            beyond_sends[piece].wait_recv()
        settle(1, step)
    for copy in sends:
        copy.wait_send()


def ladder(
    latent_cache,
    lengths,
    new_home,
    queries,
    new_latent,
    hidden,
    routes,
    route_logits,
    w_gate,
    w_up,
    w_down,
):
    ranks, slices = lax.axis_size("ep"), lax.axis_size("dp")
    line = ranks // 4
    steps, _, requests, width = hidden.shape
    heads, lat = queries.shape[3:]
    keys = latent_cache.shape[2]
    units = w_gate.shape[2]
    layers = width // LANES + 1
    own_rows = steps * requests
    chunk = width // RETURN_CHUNKS
    cell_rows = line * own_rows
    bf16, f32 = jnp.bfloat16, jnp.float32
    hbm = pl.BlockSpec(memory_space=pl.ANY)
    gather_sends = GATHER_CHUNKS * (line - 1 + 3 + 4)
    return_sends = RETURN_CHUNKS * (1 + 2 + 1 + line - 1)
    sends = gather_sends + return_sends + 12 + steps
    loads = 6 + 2 * requests + 8 + 1
    return pl.pallas_call(
        functools.partial(ladder_kernel, dict(ranks=ranks, line=line)),
        out_shape=(
            pltpu.VMEM((steps, 1, requests, heads, KV_RANK), bf16),
            pltpu.VMEM((steps, 1, requests, width), bf16),
        ),
        in_specs=[hbm] * 11,
        out_specs=(pl.BlockSpec(memory_space=pltpu.VMEM),) * 2,
        scratch_shapes=[
            pltpu.SMEM((requests, ranks), jnp.int32),
            pltpu.SMEM((requests, ranks), jnp.int32),
            pltpu.VMEM(new_latent.shape, bf16),
            pltpu.VMEM(hidden.shape, bf16),
            pltpu.VMEM(routes.shape, jnp.int32),
            pltpu.VMEM(route_logits.shape, bf16),
            pltpu.VMEM((line, layers, own_rows, LANES), bf16),
            pltpu.VMEM((slices * 4, layers, cell_rows, LANES), bf16),
            pltpu.VMEM((requests, steps, lat, heads), bf16),
            pltpu.VMEM((requests, lat, keys), bf16),
            pltpu.VMEM((width, units), bf16),
            pltpu.VMEM((width, units), bf16),
            pltpu.VMEM((units, width), bf16),
            pltpu.VMEM((requests, steps, heads, KV_RANK), bf16),
            pltpu.VMEM((steps, heads, KV_RANK), bf16),
            pltpu.VMEM((steps, heads, KV_RANK), bf16),
            pltpu.VMEM((steps, heads, KV_RANK), bf16),
            pltpu.VMEM((steps, heads, KV_RANK), bf16),
            pltpu.VMEM((RETURN_CHUNKS, 2, 4 * cell_rows, chunk), f32),
            pltpu.VMEM((RETURN_CHUNKS, 2, 4 * cell_rows, chunk), bf16),
            pltpu.VMEM((RETURN_CHUNKS, 4 * cell_rows, chunk), bf16),
            pltpu.VMEM((RETURN_CHUNKS, 4, cell_rows, chunk), f32),
            pltpu.VMEM((RETURN_CHUNKS, 4, cell_rows, chunk), bf16),
            pltpu.VMEM((RETURN_CHUNKS, 2, cell_rows, chunk), bf16),
            pltpu.VMEM((RETURN_CHUNKS, cell_rows, chunk), f32),
            pltpu.VMEM((RETURN_CHUNKS, cell_rows, chunk), bf16),
            pltpu.VMEM((RETURN_CHUNKS, cell_rows, chunk), bf16),
            pltpu.VMEM((RETURN_CHUNKS, line, own_rows, chunk), f32),
            pltpu.VMEM((RETURN_CHUNKS, line, own_rows, chunk), bf16),
            pltpu.VMEM((RETURN_CHUNKS, line - 1, own_rows, chunk), bf16),
            pltpu.SemaphoreType.DMA((loads,)),
            pltpu.SemaphoreType.DMA((sends,)),
            pltpu.SemaphoreType.DMA((sends,)),
        ],
        compiler_params=pltpu.CompilerParams(
            collective_id=0, has_side_effects=True, vmem_limit_bytes=56 * 1024 * 1024
        ),
        name="ladder",
    )(
        lengths.T,
        new_home.T,
        new_latent,
        hidden,
        routes,
        route_logits,
        jnp.swapaxes(latent_cache, 2, 3),
        jnp.swapaxes(queries, 3, 4),
        w_gate,
        w_up,
        w_down,
    )


def attend_kernel(length_ref, query_ref, cache_ref, fresh_ref, out_ref):
    step_count, head_count, lat_width = query_ref.shape
    rows = step_count * head_count
    length = length_ref[pl.program_id(0)]
    scale = HEAD_QK ** (-0.5)
    query = query_ref[...].reshape(rows, lat_width)
    keys = cache_ref[...]
    scores = (
        lax.dot_general(
            query, keys, (((1,), (1,)), ((), ())), preferred_element_type=jnp.float32
        )
        * scale
    )
    place = lax.broadcasted_iota(jnp.int32, scores.shape, 1)
    scores = jnp.where(place < length, scores, -jnp.inf)
    row_step = lax.broadcasted_iota(jnp.int32, (rows, 1), 0) // head_count
    wide_query = query.astype(jnp.float32)
    fresh = fresh_ref[...].astype(jnp.float32)
    fresh_scores = []
    row_max = jnp.max(scores, 1, keepdims=True)
    for step in range(step_count):
        one = jnp.sum(wide_query * fresh[step : step + 1], 1, keepdims=True) * scale
        one = jnp.where(row_step >= step, one, -jnp.inf)
        row_max = jnp.maximum(row_max, one)
        fresh_scores.append(one)
    weights = jnp.exp(scores - row_max)
    fresh_weights = [jnp.exp(one - row_max) for one in fresh_scores]
    total = jnp.sum(weights, 1, keepdims=True)
    for one in fresh_weights:
        total = total + one
    probs = (weights / total).astype(jnp.bfloat16)
    served = jnp.dot(probs, keys[:, :KV_RANK], preferred_element_type=jnp.float32)
    for step in range(step_count):
        part = (fresh_weights[step] / total).astype(jnp.bfloat16).astype(jnp.float32)
        served = served + part * fresh[step : step + 1, :KV_RANK]
    out_ref[...] = served.astype(jnp.bfloat16).reshape(step_count, head_count, KV_RANK)


def attend(own_lengths, queries, cache, fresh):
    step_count, _, requests, heads, lat = queries.shape
    keys = cache.shape[2]
    return pl.pallas_call(
        attend_kernel,
        grid_spec=pltpu.PrefetchScalarGridSpec(
            num_scalar_prefetch=1,
            grid=(requests,),
            in_specs=[
                pl.BlockSpec((step_count, None, None, heads, lat), lambda r, n: (0, 0, r, 0, 0)),
                pl.BlockSpec((None, None, keys, lat), lambda r, n: (0, r, 0, 0)),
                pl.BlockSpec((None, step_count, lat), lambda r, n: (r, 0, 0)),
            ],
            out_specs=pl.BlockSpec((None, step_count, heads, KV_RANK), lambda r, n: (r, 0, 0, 0)),
        ),
        out_shape=jax.ShapeDtypeStruct((requests, step_count, heads, KV_RANK), jnp.bfloat16),
        name="attend",
    )(own_lengths, queries, cache, fresh)


def travel(even, odd, ranks):
    half = ranks // 2
    across = [(e, (e + half) % ranks) for e in range(ranks)]
    ahead = [(e, (e + 1) % ranks) for e in range(ranks)]
    behind = [(e, (e - 1) % ranks) for e in range(ranks)]
    far = lax.ppermute(even, "ep", across)
    left = lax.ppermute(odd, "ep", ahead)
    right = lax.ppermute(odd, "ep", behind)
    return far, left, right


def relocate(computed, arrived, new_home, ranks, own_rank):
    requests = computed.shape[0]
    far, left, right = arrived
    anchor = new_home[own_rank]
    results = []
    for request in range(requests):
        home, slot = anchor[request], request // 2
        if request % 2 == 0:
            moved = far[slot]
        else:
            moved = jnp.where(home == (own_rank + 1) % ranks, right[slot], left[slot])
        results.append(jnp.where(home == own_rank, computed[request], moved))
    return jnp.stack(results, 1)[:, None]


def shards(
    latent_cache,
    lengths,
    new_home,
    queries,
    new_latent,
    hidden,
    routes,
    route_logits,
    w_gate,
    w_up,
    w_down,
):
    ranks = lax.axis_size("ep")
    own_rank = lax.axis_index("ep")
    step_count, _, requests, width = hidden.shape
    own_rows = step_count * requests
    slices = lax.axis_size("dp")

    def shift(value, step):
        return lax.ppermute(value, "dp", [(i, (i + step) % slices) for i in range(slices)])

    rows = hidden.reshape(own_rows, width)
    copies = jnp.broadcast_to(rows[None], (ranks, own_rows, width))
    mine = lax.all_to_all(copies, "ep", split_axis=0, concat_axis=0, tiled=True)
    mine = mine.reshape(ranks * own_rows, width)

    computed = attend(
        lengths[own_rank], queries, latent_cache, jnp.swapaxes(new_latent[:, 0], 0, 1)
    )
    mine, computed, even, odd = lax.optimization_barrier(
        (mine, computed, computed[0::2], computed[1::2])
    )
    arrived = travel(even, odd, ranks)

    tokens = jnp.concatenate([mine] + [shift(mine, step) for step in range(1, slices)], 0)
    gate_part = jnp.dot(tokens, w_gate[0], preferred_element_type=jnp.float32)
    up_part = jnp.dot(tokens, w_up[0], preferred_element_type=jnp.float32)
    units = (jax.nn.silu(gate_part) * up_part).astype(jnp.bfloat16)
    slice_out = jnp.dot(units, w_down[0], preferred_element_type=jnp.float32)
    slice_out = slice_out.astype(jnp.bfloat16)
    parts = slice_out.reshape(slices, ranks * own_rows, width)
    whole = parts[0].astype(jnp.float32)
    for step in range(1, slices):
        whole = whole + shift(parts[step], -step).astype(jnp.float32)
    whole = whole.astype(jnp.bfloat16)
    whole, arrived = lax.optimization_barrier((whole, arrived))
    returned = lax.all_to_all(
        whole.reshape(ranks, own_rows, width), "ep", split_axis=0, concat_axis=0, tiled=True
    )

    attended = relocate(computed, arrived, new_home, ranks, own_rank)
    sigmoid_part = jax.nn.sigmoid(route_logits[:, 0].astype(jnp.float32))
    gates = 2.5 * sigmoid_part / jnp.sum(sigmoid_part, -1, keepdims=True)
    rank_ids = jnp.arange(ranks, dtype=jnp.int32)
    chosen = routes[:, 0, :, :, None] == rank_ids
    dense = jnp.sum(jnp.where(chosen, gates[..., None], 0.0), 2).reshape(own_rows, ranks)
    summed = jnp.sum(returned.astype(jnp.float32) * dense.T[:, :, None], 0)
    moe_out = summed.astype(jnp.bfloat16).reshape(step_count, 1, requests, width)
    return (attended, moe_out)


def solution(mesh):
    placed = (
        P("ep", "dp", None, None),
        P(None, "dp"),
        P(None, "dp"),
        P(None, "ep", "dp", None, None),
        P(None, "ep", "dp", None),
        P(None, "ep", "dp", None),
        P(None, "ep", "dp", None),
        P(None, "ep", "dp", None),
        P("ep", None, "dp"),
        P("ep", None, "dp"),
        P("ep", "dp", None),
    )
    out_specs = (P(None, "ep", "dp", None, None), P(None, "ep", "dp", None))
    ranks = mesh.shape["ep"]
    if mesh.shape["dp"] == 2 and ranks % 8 == 0 and 3 * ranks <= LANES:
        return jax.shard_map(
            ladder, mesh=mesh, in_specs=placed, out_specs=out_specs, check_vma=False
        )
    return jax.shard_map(
        shards,
        mesh=mesh,
        in_specs=placed,
        out_specs=out_specs,
        check_vma=False,
    )
```

```python
import functools

import jax
import jax.numpy as jnp
from jax import lax
from jax.experimental import pallas as pl
from jax.experimental.pallas import tpu as pltpu
from jax.sharding import PartitionSpec as P


KV_RANK = 512
HEAD_QK = 192
LANES = 128
MESH = pl.DeviceIdType.MESH
GATHER_CHUNKS = 1
RETURN_CHUNKS = 4


def ladder_kernel(
    plan,
    lengths_hbm,
    homes_hbm,
    fresh_hbm,
    hidden_hbm,
    routes_hbm,
    logits_hbm,
    cache_hbm,
    query_hbm,
    gate_hbm,
    up_hbm,
    down_hbm,
    attended_ref,
    moe_ref,
    lengths_ref,
    homes_ref,
    fresh_ref,
    hidden_ref,
    routes_ref,
    logits_ref,
    column,
    tokens,
    query,
    cache,
    w_gate,
    w_up,
    w_down,
    served,
    far,
    near,
    onward,
    beyond,
    own_part,
    pair_send,
    pair_recv,
    chip_part,
    chip_send,
    first_recv,
    second_keep,
    second_send,
    second_recv,
    line_part,
    line_send,
    line_recv,
    load_sem,
    send_sem,
    recv_sem,
):
    ranks, line = plan["ranks"], plan["line"]
    steps, requests = hidden_ref.shape[0], hidden_ref.shape[2]
    own_rows = steps * requests
    lat = cache.shape[1]
    heads = query.shape[-1]
    width = hidden_ref.shape[-1]
    blocks = width // LANES
    layers = blocks + 1
    half = 4
    core = lax.axis_index("dp")
    rank = lax.axis_index("ep")
    side, up, place = lax.rem(rank, 2), lax.rem(lax.div(rank, 2), 2), lax.div(rank, 4)
    cell = lax.rem(rank, 4)
    across_side, across_up = rank + 1 - 2 * side, rank + 2 - 4 * up
    diagonal = rank - cell + 3 - cell
    plane = (diagonal, across_side, across_up)
    other = 1 - core
    far_rank = lax.rem(rank + ranks // 2, ranks)
    beyond_rank = lax.rem(rank + 4 - 8 * side + ranks, ranks)

    loads, sends = [], []

    def load(source, target):
        copy = pltpu.make_async_copy(source, target, load_sem.at[len(loads)])
        copy.start()
        loads.append(copy)
        return copy

    def send(source, target, to_core, to_rank):
        spot = len(sends)
        copy = pltpu.make_async_remote_copy(
            src_ref=source,
            dst_ref=target,
            send_sem=send_sem.at[spot],
            recv_sem=recv_sem.at[spot],
            device_id=(to_core, to_rank),
            device_id_type=MESH,
        )
        copy.start()
        sends.append(copy)
        return copy

    barrier = pltpu.get_barrier_semaphore()
    peers = [(other, rank)] + [(core, peer) for peer in plane]
    peers += [(core, lax.rem(rank + 4 * step, ranks)) for step in range(1, line)]
    for peer in peers:
        pl.semaphore_signal(barrier, inc=1, device_id=peer, device_id_type=MESH)

    token_loads = [
        load(hidden_hbm, hidden_ref),
        load(routes_hbm, routes_ref),
        load(logits_hbm, logits_ref),
    ]
    small_loads = [
        load(fresh_hbm, fresh_ref),
        load(lengths_hbm, lengths_ref),
        load(homes_hbm, homes_ref),
    ]
    attend_loads = {}
    for request in reversed(range(requests)):
        attend_loads[request] = (
            load(query_hbm.at[:, 0, request], query.at[request]),
            load(cache_hbm.at[0, request], cache.at[request]),
        )
    parts = 4
    rows = width // parts
    gate_loads = []
    for part in range(parts):
        span = pl.ds(part * rows, rows)
        gate_loads.append(
            (load(gate_hbm.at[0, span], w_gate.at[span]), load(up_hbm.at[0, span], w_up.at[span]))
        )
    down_load = load(down_hbm.at[0], w_down)

    for copy in token_loads:
        copy.wait()
    lane = lax.broadcasted_iota(jnp.int32, (requests, LANES), 1)
    expert = lane - jnp.where(lane >= 2 * ranks, 2 * ranks, jnp.where(lane >= ranks, ranks, 0))
    dense = []
    for step in range(steps):
        logits = logits_ref[step, 0].astype(jnp.float32)
        chosen = routes_ref[step, 0]
        sigmoid_part = 1.0 / (1.0 + jnp.exp(-logits))
        gates = 2.5 * sigmoid_part / jnp.sum(sigmoid_part, 1, keepdims=True)
        total = jnp.zeros((requests, LANES), jnp.float32)
        for k in range(chosen.shape[1]):
            total = total + jnp.where(chosen[:, k : k + 1] == expert, gates[:, k : k + 1], 0.0)
        dense.append(total)
    dense = jnp.concatenate(dense, 0)
    lane = lax.broadcasted_iota(jnp.int32, (own_rows, LANES), 1)
    high = dense.astype(jnp.bfloat16).astype(jnp.float32)
    middle = (dense - high).astype(jnp.bfloat16).astype(jnp.float32)
    low = dense - high - middle
    coded = jnp.where(lane < ranks, high, jnp.where(lane < 2 * ranks, middle, low))
    coded = jnp.where(lane < 3 * ranks, coded, 0.0)
    own = jnp.concatenate(
        [hidden_ref[step, 0].astype(jnp.float32) for step in range(steps)], 0
    )
    for block in range(blocks):
        column[place, block] = own[:, block * LANES : (block + 1) * LANES].astype(jnp.bfloat16)
    column[place, blocks] = coded.astype(jnp.bfloat16)

    pl.semaphore_wait(barrier, len(peers))

    cuts = [blocks * c // GATHER_CHUNKS for c in range(GATHER_CHUNKS)] + [layers]
    spans = [pl.ds(cuts[c], cuts[c + 1] - cuts[c]) for c in range(GATHER_CHUNKS)]
    line_sends = []
    for span in spans:
        line_sends.append(
            [
                send(
                    column.at[place, span],
                    column.at[place, span],
                    core,
                    lax.rem(rank + 4 * step, ranks),
                )
                for step in reversed(range(1, line))
            ]
        )

    near_sends, onward_sends, beyond_sends, far_sends = {}, {}, {}, {}
    quarter = heads // 2

    def cut(ref, piece):
        return ref.at[piece // 2, pl.ds(piece % 2 * quarter, quarter)]

    def send_near(piece):
        near_sends[piece] = send(cut(served.at[1], piece), cut(near, piece), core, across_side)

    def send_onward(piece):
        near_sends[piece].wait_recv()
        onward_sends[piece] = send(cut(near, piece), cut(onward, piece), core, across_up)

    def send_beyond(piece):
        onward_sends[piece].wait_recv()
        beyond_sends[piece] = send(cut(onward, piece), cut(beyond, piece), core, beyond_rank)

    def attend(request):
        for copy in attend_loads[request]:
            copy.wait()
        length = lengths_ref[request, rank]
        scale = HEAD_QK ** (-0.5)
        lines = jnp.concatenate([query[request, step] for step in range(steps)], 1)
        keys = cache[request]
        scores = (
            lax.dot_general(
                lines, keys, (((0,), (0,)), ((), ())), preferred_element_type=jnp.float32
            )
            * scale
        )
        spot = lax.broadcasted_iota(jnp.int32, scores.shape, 1)
        scores = jnp.where(spot < length, scores, -jnp.inf)
        row_step = lax.broadcasted_iota(jnp.int32, (steps * heads, 1), 0) // heads
        fresh = [
            fresh_ref[step, 0].astype(jnp.float32)[request : request + 1] for step in range(steps)
        ]
        pad = jnp.zeros((16 - steps, lat), jnp.float32)
        fresh_keys = jnp.concatenate(fresh + [pad], 0).astype(jnp.bfloat16)
        fresh_all = (
            lax.dot_general(
                lines, fresh_keys, (((0,), (1,)), ((), ())), preferred_element_type=jnp.float32
            )
            * scale
        )
        row_max = jnp.max(scores, 1, keepdims=True)
        fresh_scores = []
        for step in range(steps):
            one = jnp.where(row_step >= step, fresh_all[:, step : step + 1], -jnp.inf)
            row_max = jnp.maximum(row_max, one)
            fresh_scores.append(one)
        weights = jnp.exp(scores - row_max)
        fresh_weights = [jnp.exp(one - row_max) for one in fresh_scores]
        total = jnp.sum(weights, 1, keepdims=True)
        for one in fresh_weights:
            total = total + one
        share = 1.0 / total
        probs = (weights * share).astype(jnp.bfloat16)
        result = lax.dot_general(
            probs, keys[:KV_RANK], (((1,), (1,)), ((), ())), preferred_element_type=jnp.float32
        )
        for step in range(steps):
            part = (fresh_weights[step] * share).astype(jnp.bfloat16).astype(jnp.float32)
            result = result + part * fresh[step][:, :KV_RANK]
        result = result.astype(jnp.bfloat16)
        for step in range(steps):
            served[request, step] = result[step * heads : (step + 1) * heads]

    for copy in small_loads:
        copy.wait()
    attend(1)
    send_near(0)
    send_near(1)
    attend(0)
    far_sends = [send(served.at[0, step], far.at[step], core, far_rank) for step in range(steps)]

    mine = core * half + cell
    plane_sends, pair_sends = [], []
    for c, span in enumerate(spans):
        for copy in line_sends[c]:
            copy.wait_recv()
        merged = [column[spot, span].astype(jnp.float32) for spot in range(line)]
        tokens[mine, span] = jnp.concatenate(merged, 1).astype(jnp.bfloat16)
        block = tokens.at[mine, span]
        plane_sends.append([send(block, block, core, peer) for peer in plane])
        pair_sends.append([send(block, block, other, rank)])

    send_near(2)
    send_near(3)
    gate_part = jnp.zeros((2 * half * line * own_rows, w_gate.shape[1]), jnp.float32)
    up_part = gate_part
    piece = blocks // parts
    done = 0
    for c, span in enumerate(spans):
        for copy, peer in zip(plane_sends[c], plane):
            copy.wait_recv()
            block = core * half + lax.rem(peer, 4)
            pair_sends[c].append(
                send(tokens.at[block, span], tokens.at[block, span], other, rank)
            )
        if c == GATHER_CHUNKS - 1:
            send_onward(0)
            send_onward(1)
        for copy in pair_sends[c]:
            copy.wait_recv()
        while done < parts and (done + 1) * piece <= cuts[c + 1]:
            for copy in gate_loads[done]:
                copy.wait()
            pieces = [
                tokens[:, block].reshape(gate_part.shape[0], LANES)
                for block in range(done * piece, (done + 1) * piece)
            ]
            values = jnp.concatenate(pieces, 1)
            span_rows = pl.ds(done * rows, rows)
            gate_part = gate_part + jnp.dot(
                values, w_gate[span_rows], preferred_element_type=jnp.float32
            )
            up_part = up_part + jnp.dot(
                values, w_up[span_rows], preferred_element_type=jnp.float32
            )
            done += 1
    send_onward(2)
    send_onward(3)
    units = (gate_part / (1.0 + jnp.exp(-gate_part)) * up_part).astype(jnp.bfloat16)
    coded = tokens[:, blocks].reshape(gate_part.shape[0], LANES).astype(jnp.float32)
    lane = lax.broadcasted_iota(jnp.int32, coded.shape, 1)
    hit = (lane == rank) | (lane == rank + ranks) | (lane == rank + 2 * ranks)
    gain = jnp.sum(jnp.where(hit, coded, 0.0), 1, keepdims=True)
    down_load.wait()

    chunk = width // RETURN_CHUNKS
    side_rows = half * line * own_rows
    cell_rows = line * own_rows
    pairs, firsts, seconds, lines = {}, {}, {}, {}

    def stage_down(c):
        out = jnp.dot(
            units, w_down[:, c * chunk : (c + 1) * chunk], preferred_element_type=jnp.float32
        )
        out = out * gain
        for part in range(2):
            value = out[part * side_rows : (part + 1) * side_rows]
            own_part[c, part] = value
            pair_send[c, part] = value.astype(jnp.bfloat16)
        pairs[c] = send(pair_send.at[c, other], pair_recv.at[c], other, rank)

    def route(c):
        turn = core if c % 2 == 0 else other
        to_second = across_side * (1 - turn) + across_up * turn
        to_first = across_up * (1 - turn) + across_side * turn
        return to_first, to_second

    def stage_chip(c):
        _, second = route(c)
        pairs[c].wait_recv()
        value = own_part[c, core] + pair_recv[c].astype(jnp.float32)
        for part in range(half):
            cut = value[part * cell_rows : (part + 1) * cell_rows]
            chip_part[c, part] = cut
            chip_send[c, part] = cut.astype(jnp.bfloat16)
        firsts[c] = [
            send(chip_send.at[c, 3 - cell], first_recv.at[c, 1], core, second),
            send(chip_send.at[c, lax.rem(second, 4)], first_recv.at[c, 0], core, second),
        ]

    def stage_plane(c):
        first, _ = route(c)
        firsts[c][0].wait_recv()
        value = chip_part[c, lax.rem(first, 4)] + first_recv[c, 1].astype(jnp.float32)
        second_send[c] = value.astype(jnp.bfloat16)
        seconds[c] = send(second_send.at[c], second_recv.at[c], core, first)
        firsts[c][1].wait_recv()
        second_keep[c] = chip_part[c, cell] + first_recv[c, 0].astype(jnp.float32)

    def stage_line(c):
        seconds[c].wait_recv()
        value = second_keep[c] + second_recv[c].astype(jnp.float32)
        for spot in range(line):
            cut = value[spot * own_rows : (spot + 1) * own_rows]
            line_part[c, spot] = cut
            line_send[c, spot] = cut.astype(jnp.bfloat16)
        lines[c] = [
            send(
                line_send.at[c, lax.rem(place + step, line)],
                line_recv.at[c, step - 1],
                core,
                lax.rem(rank + 4 * step, ranks),
            )
            for step in range(1, line)
        ]

    def stage_sum(c):
        value = line_part[c, place]
        for step in range(1, line):
            lines[c][step - 1].wait_recv()
            value = value + line_recv[c, step - 1].astype(jnp.float32)
        value = value.astype(jnp.bfloat16)
        for step in range(steps):
            moe_ref[step, 0, :, c * chunk : (c + 1) * chunk] = value[
                step * requests : (step + 1) * requests
            ]

    def settle(request, step):
        home = homes_ref[request, rank]
        arrived = far[step]
        if request % 2:
            arrived = jnp.where(side == up, beyond[step], onward[step])
            arrived = jnp.where(home == across_side, near[step], arrived)
        attended_ref[step, 0, request] = jnp.where(home == rank, served[request, step], arrived)

    for c in range(RETURN_CHUNKS):
        stage_down(c)
    send_beyond(0)
    send_beyond(1)
    for c in range(RETURN_CHUNKS):
        stage_chip(c)
    send_beyond(2)
    send_beyond(3)
    for c in range(RETURN_CHUNKS):
        stage_plane(c)
    for c in range(RETURN_CHUNKS):
        stage_line(c)
    for step in range(steps):
        far_sends[step].wait_recv()
        settle(0, step)
    for piece in (0, 1):
        beyond_sends[piece].wait_recv()
    settle(1, 0)
    for c in range(RETURN_CHUNKS):
        stage_sum(c)
    for step in range(1, steps):
        for piece in (2, 3):
            beyond_sends[piece].wait_recv()
        settle(1, step)
    for copy in sends:
        copy.wait_send()


def settle_kernel(attended_ref, moe_ref, attended_hbm, moe_hbm, sems):
    copies = (
        pltpu.make_async_copy(attended_ref, attended_hbm, sems.at[0]),
        pltpu.make_async_copy(moe_ref, moe_hbm, sems.at[1]),
    )
    for copy in copies:
        copy.start()
    for copy in copies:
        copy.wait()


def ladder(
    latent_cache,
    lengths,
    new_home,
    queries,
    new_latent,
    hidden,
    routes,
    route_logits,
    w_gate,
    w_up,
    w_down,
):
    ranks, slices = lax.axis_size("ep"), lax.axis_size("dp")
    line = ranks // 4
    steps, _, requests, width = hidden.shape
    heads, lat = queries.shape[3:]
    keys = latent_cache.shape[2]
    units = w_gate.shape[2]
    layers = width // LANES + 1
    own_rows = steps * requests
    chunk = width // RETURN_CHUNKS
    cell_rows = line * own_rows
    bf16, f32 = jnp.bfloat16, jnp.float32
    hbm = pl.BlockSpec(memory_space=pl.ANY)
    gather_sends = GATHER_CHUNKS * (line - 1 + 3 + 4)
    return_sends = RETURN_CHUNKS * (1 + 2 + 1 + line - 1)
    sends = gather_sends + return_sends + 12 + steps
    loads = 6 + 2 * requests + 8 + 1
    attended, moe_out = pl.pallas_call(
        functools.partial(ladder_kernel, dict(ranks=ranks, line=line)),
        out_shape=(
            pltpu.VMEM((steps, 1, requests, heads, KV_RANK), bf16),
            pltpu.VMEM((steps, 1, requests, width), bf16),
        ),
        in_specs=[hbm] * 11,
        out_specs=(pl.BlockSpec(memory_space=pltpu.VMEM),) * 2,
        scratch_shapes=[
            pltpu.SMEM((requests, ranks), jnp.int32),
            pltpu.SMEM((requests, ranks), jnp.int32),
            pltpu.VMEM(new_latent.shape, bf16),
            pltpu.VMEM(hidden.shape, bf16),
            pltpu.VMEM(routes.shape, jnp.int32),
            pltpu.VMEM(route_logits.shape, bf16),
            pltpu.VMEM((line, layers, own_rows, LANES), bf16),
            pltpu.VMEM((slices * 4, layers, cell_rows, LANES), bf16),
            pltpu.VMEM((requests, steps, lat, heads), bf16),
            pltpu.VMEM((requests, lat, keys), bf16),
            pltpu.VMEM((width, units), bf16),
            pltpu.VMEM((width, units), bf16),
            pltpu.VMEM((units, width), bf16),
            pltpu.VMEM((requests, steps, heads, KV_RANK), bf16),
            pltpu.VMEM((steps, heads, KV_RANK), bf16),
            pltpu.VMEM((steps, heads, KV_RANK), bf16),
            pltpu.VMEM((steps, heads, KV_RANK), bf16),
            pltpu.VMEM((steps, heads, KV_RANK), bf16),
            pltpu.VMEM((RETURN_CHUNKS, 2, 4 * cell_rows, chunk), f32),
            pltpu.VMEM((RETURN_CHUNKS, 2, 4 * cell_rows, chunk), bf16),
            pltpu.VMEM((RETURN_CHUNKS, 4 * cell_rows, chunk), bf16),
            pltpu.VMEM((RETURN_CHUNKS, 4, cell_rows, chunk), f32),
            pltpu.VMEM((RETURN_CHUNKS, 4, cell_rows, chunk), bf16),
            pltpu.VMEM((RETURN_CHUNKS, 2, cell_rows, chunk), bf16),
            pltpu.VMEM((RETURN_CHUNKS, cell_rows, chunk), f32),
            pltpu.VMEM((RETURN_CHUNKS, cell_rows, chunk), bf16),
            pltpu.VMEM((RETURN_CHUNKS, cell_rows, chunk), bf16),
            pltpu.VMEM((RETURN_CHUNKS, line, own_rows, chunk), f32),
            pltpu.VMEM((RETURN_CHUNKS, line, own_rows, chunk), bf16),
            pltpu.VMEM((RETURN_CHUNKS, line - 1, own_rows, chunk), bf16),
            pltpu.SemaphoreType.DMA((loads,)),
            pltpu.SemaphoreType.DMA((sends,)),
            pltpu.SemaphoreType.DMA((sends,)),
        ],
        compiler_params=pltpu.CompilerParams(
            collective_id=0, has_side_effects=True, vmem_limit_bytes=56 * 1024 * 1024
        ),
        name="ladder",
    )(
        lengths.T,
        new_home.T,
        new_latent,
        hidden,
        routes,
        route_logits,
        jnp.swapaxes(latent_cache, 2, 3),
        jnp.swapaxes(queries, 3, 4),
        w_gate,
        w_up,
        w_down,
    )
    results = (attended, moe_out)
    return pl.pallas_call(
        settle_kernel,
        out_shape=tuple(jax.ShapeDtypeStruct(one.shape, one.dtype) for one in results),
        in_specs=[pl.BlockSpec(memory_space=pltpu.VMEM)] * 2,
        out_specs=(hbm, hbm),
        scratch_shapes=[pltpu.SemaphoreType.DMA((2,))],
        compiler_params=pltpu.CompilerParams(vmem_limit_bytes=1024 * 1024),
        name="settle",
    )(*results)


def attend_kernel(length_ref, query_ref, cache_ref, fresh_ref, out_ref):
    step_count, head_count, lat_width = query_ref.shape
    rows = step_count * head_count
    length = length_ref[pl.program_id(0)]
    scale = HEAD_QK ** (-0.5)
    query = query_ref[...].reshape(rows, lat_width)
    keys = cache_ref[...]
    scores = (
        lax.dot_general(
            query, keys, (((1,), (1,)), ((), ())), preferred_element_type=jnp.float32
        )
        * scale
    )
    place = lax.broadcasted_iota(jnp.int32, scores.shape, 1)
    scores = jnp.where(place < length, scores, -jnp.inf)
    row_step = lax.broadcasted_iota(jnp.int32, (rows, 1), 0) // head_count
    wide_query = query.astype(jnp.float32)
    fresh = fresh_ref[...].astype(jnp.float32)
    fresh_scores = []
    row_max = jnp.max(scores, 1, keepdims=True)
    for step in range(step_count):
        one = jnp.sum(wide_query * fresh[step : step + 1], 1, keepdims=True) * scale
        one = jnp.where(row_step >= step, one, -jnp.inf)
        row_max = jnp.maximum(row_max, one)
        fresh_scores.append(one)
    weights = jnp.exp(scores - row_max)
    fresh_weights = [jnp.exp(one - row_max) for one in fresh_scores]
    total = jnp.sum(weights, 1, keepdims=True)
    for one in fresh_weights:
        total = total + one
    probs = (weights / total).astype(jnp.bfloat16)
    served = jnp.dot(probs, keys[:, :KV_RANK], preferred_element_type=jnp.float32)
    for step in range(step_count):
        part = (fresh_weights[step] / total).astype(jnp.bfloat16).astype(jnp.float32)
        served = served + part * fresh[step : step + 1, :KV_RANK]
    out_ref[...] = served.astype(jnp.bfloat16).reshape(step_count, head_count, KV_RANK)


def attend(own_lengths, queries, cache, fresh):
    step_count, _, requests, heads, lat = queries.shape
    keys = cache.shape[2]
    return pl.pallas_call(
        attend_kernel,
        grid_spec=pltpu.PrefetchScalarGridSpec(
            num_scalar_prefetch=1,
            grid=(requests,),
            in_specs=[
                pl.BlockSpec((step_count, None, None, heads, lat), lambda r, n: (0, 0, r, 0, 0)),
                pl.BlockSpec((None, None, keys, lat), lambda r, n: (0, r, 0, 0)),
                pl.BlockSpec((None, step_count, lat), lambda r, n: (r, 0, 0)),
            ],
            out_specs=pl.BlockSpec((None, step_count, heads, KV_RANK), lambda r, n: (r, 0, 0, 0)),
        ),
        out_shape=jax.ShapeDtypeStruct((requests, step_count, heads, KV_RANK), jnp.bfloat16),
        name="attend",
    )(own_lengths, queries, cache, fresh)


def travel(even, odd, ranks):
    half = ranks // 2
    across = [(e, (e + half) % ranks) for e in range(ranks)]
    ahead = [(e, (e + 1) % ranks) for e in range(ranks)]
    behind = [(e, (e - 1) % ranks) for e in range(ranks)]
    far = lax.ppermute(even, "ep", across)
    left = lax.ppermute(odd, "ep", ahead)
    right = lax.ppermute(odd, "ep", behind)
    return far, left, right


def relocate(computed, arrived, new_home, ranks, own_rank):
    requests = computed.shape[0]
    far, left, right = arrived
    anchor = new_home[own_rank]
    results = []
    for request in range(requests):
        home, slot = anchor[request], request // 2
        if request % 2 == 0:
            moved = far[slot]
        else:
            moved = jnp.where(home == (own_rank + 1) % ranks, right[slot], left[slot])
        results.append(jnp.where(home == own_rank, computed[request], moved))
    return jnp.stack(results, 1)[:, None]


def shards(
    latent_cache,
    lengths,
    new_home,
    queries,
    new_latent,
    hidden,
    routes,
    route_logits,
    w_gate,
    w_up,
    w_down,
):
    ranks = lax.axis_size("ep")
    own_rank = lax.axis_index("ep")
    step_count, _, requests, width = hidden.shape
    own_rows = step_count * requests
    slices = lax.axis_size("dp")

    def shift(value, step):
        return lax.ppermute(value, "dp", [(i, (i + step) % slices) for i in range(slices)])

    rows = hidden.reshape(own_rows, width)
    copies = jnp.broadcast_to(rows[None], (ranks, own_rows, width))
    mine = lax.all_to_all(copies, "ep", split_axis=0, concat_axis=0, tiled=True)
    mine = mine.reshape(ranks * own_rows, width)

    computed = attend(
        lengths[own_rank], queries, latent_cache, jnp.swapaxes(new_latent[:, 0], 0, 1)
    )
    mine, computed, even, odd = lax.optimization_barrier(
        (mine, computed, computed[0::2], computed[1::2])
    )
    arrived = travel(even, odd, ranks)

    tokens = jnp.concatenate([mine] + [shift(mine, step) for step in range(1, slices)], 0)
    gate_part = jnp.dot(tokens, w_gate[0], preferred_element_type=jnp.float32)
    up_part = jnp.dot(tokens, w_up[0], preferred_element_type=jnp.float32)
    units = (jax.nn.silu(gate_part) * up_part).astype(jnp.bfloat16)
    slice_out = jnp.dot(units, w_down[0], preferred_element_type=jnp.float32)
    slice_out = slice_out.astype(jnp.bfloat16)
    parts = slice_out.reshape(slices, ranks * own_rows, width)
    whole = parts[0].astype(jnp.float32)
    for step in range(1, slices):
        whole = whole + shift(parts[step], -step).astype(jnp.float32)
    whole = whole.astype(jnp.bfloat16)
    whole, arrived = lax.optimization_barrier((whole, arrived))
    returned = lax.all_to_all(
        whole.reshape(ranks, own_rows, width), "ep", split_axis=0, concat_axis=0, tiled=True
    )

    attended = relocate(computed, arrived, new_home, ranks, own_rank)
    sigmoid_part = jax.nn.sigmoid(route_logits[:, 0].astype(jnp.float32))
    gates = 2.5 * sigmoid_part / jnp.sum(sigmoid_part, -1, keepdims=True)
    rank_ids = jnp.arange(ranks, dtype=jnp.int32)
    chosen = routes[:, 0, :, :, None] == rank_ids
    dense = jnp.sum(jnp.where(chosen, gates[..., None], 0.0), 2).reshape(own_rows, ranks)
    summed = jnp.sum(returned.astype(jnp.float32) * dense.T[:, :, None], 0)
    moe_out = summed.astype(jnp.bfloat16).reshape(step_count, 1, requests, width)
    return (attended, moe_out)


def solution(mesh):
    placed = (
        P("ep", "dp", None, None),
        P(None, "dp"),
        P(None, "dp"),
        P(None, "ep", "dp", None, None),
        P(None, "ep", "dp", None),
        P(None, "ep", "dp", None),
        P(None, "ep", "dp", None),
        P(None, "ep", "dp", None),
        P("ep", None, "dp"),
        P("ep", None, "dp"),
        P("ep", "dp", None),
    )
    out_specs = (P(None, "ep", "dp", None, None), P(None, "ep", "dp", None))
    ranks = mesh.shape["ep"]
    if mesh.shape["dp"] == 2 and ranks % 8 == 0 and 3 * ranks <= LANES:
        return jax.shard_map(
            ladder, mesh=mesh, in_specs=placed, out_specs=out_specs, check_vma=False
        )
    return jax.shard_map(
        shards,
        mesh=mesh,
        in_specs=placed,
        out_specs=out_specs,
        check_vma=False,
    )
```

```python
import functools

import jax
import jax.numpy as jnp
from jax import lax
from jax.experimental import pallas as pl
from jax.experimental.pallas import tpu as pltpu
from jax.sharding import PartitionSpec as P


KV_RANK = 512
HEAD_QK = 192
LANES = 128
MESH = pl.DeviceIdType.MESH
RETURN_CHUNKS = 4


def ladder_kernel(
    plan,
    lengths_hbm,
    homes_hbm,
    fresh_hbm,
    hidden_hbm,
    routes_hbm,
    logits_hbm,
    cache_hbm,
    query_hbm,
    gate_hbm,
    up_hbm,
    down_hbm,
    attended_ref,
    moe_ref,
    lengths_ref,
    homes_ref,
    fresh_ref,
    hidden_ref,
    routes_ref,
    logits_ref,
    slots,
    tokens,
    query,
    cache,
    w_gate,
    w_up,
    w_down,
    served,
    far,
    near,
    onward,
    beyond,
    own_part,
    pair_send,
    pair_recv,
    chip_part,
    chip_send,
    first_recv,
    second_keep,
    second_send,
    second_recv,
    line_part,
    line_send,
    line_recv,
    line_sems,
    load_sem,
    send_sem,
    recv_sem,
):
    ranks, line = plan["ranks"], plan["line"]
    steps, requests = hidden_ref.shape[0], hidden_ref.shape[2]
    own_rows = steps * requests
    lat = cache.shape[1]
    heads = query.shape[-1]
    width = hidden_ref.shape[-1]
    blocks = width // LANES
    half = 4
    core = lax.axis_index("dp")
    rank = lax.axis_index("ep")
    side, up, place = lax.rem(rank, 2), lax.rem(lax.div(rank, 2), 2), lax.div(rank, 4)
    cell = lax.rem(rank, 4)
    across_side, across_up = rank + 1 - 2 * side, rank + 2 - 4 * up
    diagonal = rank - cell + 3 - cell
    plane = (diagonal, across_side, across_up)
    other = 1 - core
    mine = core * half + cell
    far_rank = lax.rem(rank + ranks // 2, ranks)
    beyond_rank = lax.rem(rank + 4 - 8 * side + ranks, ranks)

    loads, sends = [], []

    def load(source, target):
        copy = pltpu.make_async_copy(source, target, load_sem.at[len(loads)])
        copy.start()
        loads.append(copy)
        return copy

    def send(source, target, to_core, to_rank):
        spot = len(sends)
        copy = pltpu.make_async_remote_copy(
            src_ref=source,
            dst_ref=target,
            send_sem=send_sem.at[spot],
            recv_sem=recv_sem.at[spot],
            device_id=(to_core, to_rank),
            device_id_type=MESH,
        )
        copy.start()
        sends.append(copy)
        return copy

    barrier = pltpu.get_barrier_semaphore()
    peers = [(other, rank)] + [(core, peer) for peer in plane]
    peers += [(core, lax.rem(rank + 4 * step, ranks)) for step in range(1, line)]
    for peer in peers:
        pl.semaphore_signal(barrier, inc=1, device_id=peer, device_id_type=MESH)

    token_loads = [
        load(hidden_hbm, hidden_ref),
        load(routes_hbm, routes_ref),
        load(logits_hbm, logits_ref),
    ]
    small_loads = [
        load(fresh_hbm, fresh_ref),
        load(lengths_hbm, lengths_ref),
        load(homes_hbm, homes_ref),
    ]
    attend_loads = {}
    for request in reversed(range(requests)):
        attend_loads[request] = (
            load(query_hbm.at[:, 0, request], query.at[request]),
            load(cache_hbm.at[0, request], cache.at[request]),
        )
    parts = 4
    rows = width // parts
    gate_loads = []
    for part in range(parts):
        span = pl.ds(part * rows, rows)
        gate_loads.append(
            (load(gate_hbm.at[0, span], w_gate.at[span]), load(up_hbm.at[0, span], w_up.at[span]))
        )
    down_load = load(down_hbm.at[0], w_down)

    for copy in token_loads:
        copy.wait()
    lane = lax.broadcasted_iota(jnp.int32, (requests, LANES), 1)
    expert = lane - jnp.where(lane >= 2 * ranks, 2 * ranks, jnp.where(lane >= ranks, ranks, 0))
    dense = []
    for step in range(steps):
        logits = logits_ref[step, 0].astype(jnp.float32)
        chosen = routes_ref[step, 0]
        sigmoid_part = 1.0 / (1.0 + jnp.exp(-logits))
        gates = 2.5 * sigmoid_part / jnp.sum(sigmoid_part, 1, keepdims=True)
        total = jnp.zeros((requests, LANES), jnp.float32)
        for k in range(chosen.shape[1]):
            total = total + jnp.where(chosen[:, k : k + 1] == expert, gates[:, k : k + 1], 0.0)
        dense.append(total)
    dense = jnp.concatenate(dense, 0)
    lane = lax.broadcasted_iota(jnp.int32, (own_rows, LANES), 1)
    high = dense.astype(jnp.bfloat16).astype(jnp.float32)
    middle = (dense - high).astype(jnp.bfloat16).astype(jnp.float32)
    low = dense - high - middle
    coded = jnp.where(lane < ranks, high, jnp.where(lane < 2 * ranks, middle, low))
    coded = jnp.where(lane < 3 * ranks, coded, 0.0)
    own = jnp.concatenate(
        [hidden_ref[step, 0].astype(jnp.float32) for step in range(steps)], 0
    )
    for block in range(blocks):
        slots[mine, place, block] = own[:, block * LANES : (block + 1) * LANES].astype(jnp.bfloat16)
    slots[mine, place, blocks] = coded.astype(jnp.bfloat16)

    pl.semaphore_wait(barrier, len(peers))

    def share(block, slot, to_core, to_rank):
        return send(slots.at[block, slot], slots.at[block, slot], to_core, to_rank)

    def spread(slot):
        plane_sends.append([share(mine, slot, core, peer) for peer in plane])
        pair_sends.append([share(mine, slot, other, rank)])

    def arrival(step, slot):
        return pltpu.make_async_remote_copy(
            src_ref=slots.at[mine, slot],
            dst_ref=slots.at[mine, slot],
            send_sem=line_sems.at[0, step - 1],
            recv_sem=line_sems.at[1, step - 1],
            device_id=(core, lax.rem(rank + 4 * step, ranks)),
            device_id_type=MESH,
        )

    def merge(block):
        tokens[block] = jnp.concatenate([slots[block, slot] for slot in range(line)], 1)

    plane_sends, pair_sends = [], []
    for step in reversed(range(1, line)):
        arrival(step, place).start()
    spread(place)

    near_sends, onward_sends, beyond_sends, far_sends = {}, {}, {}, {}
    quarter = heads // 2

    def cut(ref, piece):
        return ref.at[piece // 2, pl.ds(piece % 2 * quarter, quarter)]

    def send_near(piece):
        near_sends[piece] = send(cut(served.at[1], piece), cut(near, piece), core, across_side)

    def send_onward(piece):
        near_sends[piece].wait_recv()
        onward_sends[piece] = send(cut(near, piece), cut(onward, piece), core, across_up)

    def send_beyond(piece):
        onward_sends[piece].wait_recv()
        beyond_sends[piece] = send(cut(onward, piece), cut(beyond, piece), core, beyond_rank)

    def attend(request):
        for copy in attend_loads[request]:
            copy.wait()
        length = lengths_ref[request, rank]
        scale = HEAD_QK ** (-0.5)
        lines = jnp.concatenate([query[request, step] for step in range(steps)], 1)
        keys = cache[request]
        scores = (
            lax.dot_general(
                lines, keys, (((0,), (0,)), ((), ())), preferred_element_type=jnp.float32
            )
            * scale
        )
        spot = lax.broadcasted_iota(jnp.int32, scores.shape, 1)
        scores = jnp.where(spot < length, scores, -jnp.inf)
        row_step = lax.broadcasted_iota(jnp.int32, (steps * heads, 1), 0) // heads
        fresh = [
            fresh_ref[step, 0].astype(jnp.float32)[request : request + 1] for step in range(steps)
        ]
        pad = jnp.zeros((16 - steps, lat), jnp.float32)
        fresh_keys = jnp.concatenate(fresh + [pad], 0).astype(jnp.bfloat16)
        fresh_all = (
            lax.dot_general(
                lines, fresh_keys, (((0,), (1,)), ((), ())), preferred_element_type=jnp.float32
            )
            * scale
        )
        row_max = jnp.max(scores, 1, keepdims=True)
        fresh_scores = []
        for step in range(steps):
            one = jnp.where(row_step >= step, fresh_all[:, step : step + 1], -jnp.inf)
            row_max = jnp.maximum(row_max, one)
            fresh_scores.append(one)
        weights = jnp.exp(scores - row_max)
        fresh_weights = [jnp.exp(one - row_max) for one in fresh_scores]
        total = jnp.sum(weights, 1, keepdims=True)
        for one in fresh_weights:
            total = total + one
        share = 1.0 / total
        probs = (weights * share).astype(jnp.bfloat16)
        result = lax.dot_general(
            probs, keys[:KV_RANK], (((1,), (1,)), ((), ())), preferred_element_type=jnp.float32
        )
        for step in range(steps):
            part = (fresh_weights[step] * share).astype(jnp.bfloat16).astype(jnp.float32)
            result = result + part * fresh[step][:, :KV_RANK]
        result = result.astype(jnp.bfloat16)
        for step in range(steps):
            served[request, step] = result[step * heads : (step + 1) * heads]

    for copy in small_loads:
        copy.wait()
    attend(1)
    send_near(0)
    attend(0)
    far_sends = [send(served.at[0, step], far.at[step], core, far_rank) for step in range(steps)]

    lower = place < line // 2
    for reach in range(1, line):
        step = jnp.where(lower, line - reach, reach)
        slot = lax.rem(place - step + line, line)
        arrival(step, slot).wait_recv()
        spread(slot)
    merge(mine)
    send_near(1)
    send_near(2)
    send_near(3)
    for reach in range(line):
        slot = jnp.where(lower, place + reach, place - reach + line)
        slot = lax.rem(slot, line)
        for copy, peer in zip(plane_sends[reach], plane):
            copy.wait_recv()
            pair_sends[reach].append(share(core * half + lax.rem(peer, 4), slot, other, rank))
    send_onward(0)
    send_onward(1)
    for peer in plane:
        merge(core * half + lax.rem(peer, 4))
    for copies in pair_sends:
        for copy in copies:
            copy.wait_recv()
    for block in range(half):
        merge(other * half + block)

    gate_part = jnp.zeros((2 * half * line * own_rows, w_gate.shape[1]), jnp.float32)
    up_part = gate_part
    piece = blocks // parts
    for done in range(parts):
        for copy in gate_loads[done]:
            copy.wait()
        pieces = [
            tokens[:, block].reshape(gate_part.shape[0], LANES)
            for block in range(done * piece, (done + 1) * piece)
        ]
        values = jnp.concatenate(pieces, 1)
        span_rows = pl.ds(done * rows, rows)
        gate_part = gate_part + jnp.dot(
            values, w_gate[span_rows], preferred_element_type=jnp.float32
        )
        up_part = up_part + jnp.dot(values, w_up[span_rows], preferred_element_type=jnp.float32)
    send_onward(2)
    send_onward(3)
    units = (gate_part / (1.0 + jnp.exp(-gate_part)) * up_part).astype(jnp.bfloat16)
    coded = tokens[:, blocks].reshape(gate_part.shape[0], LANES).astype(jnp.float32)
    lane = lax.broadcasted_iota(jnp.int32, coded.shape, 1)
    hit = (lane == rank) | (lane == rank + ranks) | (lane == rank + 2 * ranks)
    gain = jnp.sum(jnp.where(hit, coded, 0.0), 1, keepdims=True)
    down_load.wait()

    chunk = width // RETURN_CHUNKS
    side_rows = half * line * own_rows
    cell_rows = line * own_rows
    pairs, firsts, seconds, lines = {}, {}, {}, {}

    def stage_down(c):
        out = jnp.dot(
            units, w_down[:, c * chunk : (c + 1) * chunk], preferred_element_type=jnp.float32
        )
        out = out * gain
        for part in range(2):
            value = out[part * side_rows : (part + 1) * side_rows]
            own_part[c, part] = value
            pair_send[c, part] = value.astype(jnp.bfloat16)
        pairs[c] = send(pair_send.at[c, other], pair_recv.at[c], other, rank)

    def route(c):
        turn = core if c % 2 == 0 else other
        to_second = across_side * (1 - turn) + across_up * turn
        to_first = across_up * (1 - turn) + across_side * turn
        return to_first, to_second

    def stage_chip(c):
        _, second = route(c)
        pairs[c].wait_recv()
        value = own_part[c, core] + pair_recv[c].astype(jnp.float32)
        for part in range(half):
            cut = value[part * cell_rows : (part + 1) * cell_rows]
            chip_part[c, part] = cut
            chip_send[c, part] = cut.astype(jnp.bfloat16)
        firsts[c] = [
            send(chip_send.at[c, 3 - cell], first_recv.at[c, 1], core, second),
            send(chip_send.at[c, lax.rem(second, 4)], first_recv.at[c, 0], core, second),
        ]

    def stage_plane(c):
        first, _ = route(c)
        firsts[c][0].wait_recv()
        value = chip_part[c, lax.rem(first, 4)] + first_recv[c, 1].astype(jnp.float32)
        second_send[c] = value.astype(jnp.bfloat16)
        seconds[c] = send(second_send.at[c], second_recv.at[c], core, first)
        firsts[c][1].wait_recv()
        second_keep[c] = chip_part[c, cell] + first_recv[c, 0].astype(jnp.float32)

    def stage_line(c):
        seconds[c].wait_recv()
        value = second_keep[c] + second_recv[c].astype(jnp.float32)
        for spot in range(line):
            cut = value[spot * own_rows : (spot + 1) * own_rows]
            line_part[c, spot] = cut
            line_send[c, spot] = cut.astype(jnp.bfloat16)
        lines[c] = [
            send(
                line_send.at[c, lax.rem(place + step, line)],
                line_recv.at[c, step - 1],
                core,
                lax.rem(rank + 4 * step, ranks),
            )
            for step in range(1, line)
        ]

    def stage_sum(c):
        value = line_part[c, place]
        for step in range(1, line):
            lines[c][step - 1].wait_recv()
            value = value + line_recv[c, step - 1].astype(jnp.float32)
        value = value.astype(jnp.bfloat16)
        for step in range(steps):
            moe_ref[step, 0, :, c * chunk : (c + 1) * chunk] = value[
                step * requests : (step + 1) * requests
            ]

    def settle(request, step):
        home = homes_ref[request, rank]
        arrived = far[step]
        if request % 2:
            arrived = jnp.where(side == up, beyond[step], onward[step])
            arrived = jnp.where(home == across_side, near[step], arrived)
        attended_ref[step, 0, request] = jnp.where(home == rank, served[request, step], arrived)

    for c in range(RETURN_CHUNKS):
        stage_down(c)
    send_beyond(0)
    send_beyond(1)
    for c in range(RETURN_CHUNKS):
        stage_chip(c)
    send_beyond(2)
    send_beyond(3)
    for c in range(RETURN_CHUNKS):
        stage_plane(c)
    for c in range(RETURN_CHUNKS):
        stage_line(c)
    for step in range(steps):
        far_sends[step].wait_recv()
        settle(0, step)
    for piece in (0, 1):
        beyond_sends[piece].wait_recv()
    settle(1, 0)
    for c in range(RETURN_CHUNKS):
        stage_sum(c)
    for step in range(1, steps):
        for piece in (2, 3):
            beyond_sends[piece].wait_recv()
        settle(1, step)
    for copy in sends:
        copy.wait_send()
    for step in range(1, line):
        arrival(step, place).wait_send()


def settle_kernel(attended_ref, moe_ref, attended_hbm, moe_hbm, sems):
    copies = (
        pltpu.make_async_copy(attended_ref, attended_hbm, sems.at[0]),
        pltpu.make_async_copy(moe_ref, moe_hbm, sems.at[1]),
    )
    for copy in copies:
        copy.start()
    for copy in copies:
        copy.wait()


def ladder(
    latent_cache,
    lengths,
    new_home,
    queries,
    new_latent,
    hidden,
    routes,
    route_logits,
    w_gate,
    w_up,
    w_down,
):
    ranks, slices = lax.axis_size("ep"), lax.axis_size("dp")
    line = ranks // 4
    steps, _, requests, width = hidden.shape
    heads, lat = queries.shape[3:]
    keys = latent_cache.shape[2]
    units = w_gate.shape[2]
    layers = width // LANES + 1
    own_rows = steps * requests
    chunk = width // RETURN_CHUNKS
    cell_rows = line * own_rows
    bf16, f32 = jnp.bfloat16, jnp.float32
    hbm = pl.BlockSpec(memory_space=pl.ANY)
    gather_sends = line * (3 + 4)
    return_sends = RETURN_CHUNKS * (1 + 2 + 1 + line - 1)
    sends = gather_sends + return_sends + 12 + steps
    loads = 6 + 2 * requests + 8 + 1
    attended, moe_out = pl.pallas_call(
        functools.partial(ladder_kernel, dict(ranks=ranks, line=line)),
        out_shape=(
            pltpu.VMEM((steps, 1, requests, heads, KV_RANK), bf16),
            pltpu.VMEM((steps, 1, requests, width), bf16),
        ),
        in_specs=[hbm] * 11,
        out_specs=(pl.BlockSpec(memory_space=pltpu.VMEM),) * 2,
        scratch_shapes=[
            pltpu.SMEM((requests, ranks), jnp.int32),
            pltpu.SMEM((requests, ranks), jnp.int32),
            pltpu.VMEM(new_latent.shape, bf16),
            pltpu.VMEM(hidden.shape, bf16),
            pltpu.VMEM(routes.shape, jnp.int32),
            pltpu.VMEM(route_logits.shape, bf16),
            pltpu.VMEM((slices * 4, line, layers, own_rows, LANES), bf16),
            pltpu.VMEM((slices * 4, layers, cell_rows, LANES), bf16),
            pltpu.VMEM((requests, steps, lat, heads), bf16),
            pltpu.VMEM((requests, lat, keys), bf16),
            pltpu.VMEM((width, units), bf16),
            pltpu.VMEM((width, units), bf16),
            pltpu.VMEM((units, width), bf16),
            pltpu.VMEM((requests, steps, heads, KV_RANK), bf16),
            pltpu.VMEM((steps, heads, KV_RANK), bf16),
            pltpu.VMEM((steps, heads, KV_RANK), bf16),
            pltpu.VMEM((steps, heads, KV_RANK), bf16),
            pltpu.VMEM((steps, heads, KV_RANK), bf16),
            pltpu.VMEM((RETURN_CHUNKS, 2, 4 * cell_rows, chunk), f32),
            pltpu.VMEM((RETURN_CHUNKS, 2, 4 * cell_rows, chunk), bf16),
            pltpu.VMEM((RETURN_CHUNKS, 4 * cell_rows, chunk), bf16),
            pltpu.VMEM((RETURN_CHUNKS, 4, cell_rows, chunk), f32),
            pltpu.VMEM((RETURN_CHUNKS, 4, cell_rows, chunk), bf16),
            pltpu.VMEM((RETURN_CHUNKS, 2, cell_rows, chunk), bf16),
            pltpu.VMEM((RETURN_CHUNKS, cell_rows, chunk), f32),
            pltpu.VMEM((RETURN_CHUNKS, cell_rows, chunk), bf16),
            pltpu.VMEM((RETURN_CHUNKS, cell_rows, chunk), bf16),
            pltpu.VMEM((RETURN_CHUNKS, line, own_rows, chunk), f32),
            pltpu.VMEM((RETURN_CHUNKS, line, own_rows, chunk), bf16),
            pltpu.VMEM((RETURN_CHUNKS, line - 1, own_rows, chunk), bf16),
            pltpu.SemaphoreType.DMA((2, line - 1)),
            pltpu.SemaphoreType.DMA((loads,)),
            pltpu.SemaphoreType.DMA((sends,)),
            pltpu.SemaphoreType.DMA((sends,)),
        ],
        compiler_params=pltpu.CompilerParams(
            collective_id=0, has_side_effects=True, vmem_limit_bytes=56 * 1024 * 1024
        ),
        name="ladder",
    )(
        lengths.T,
        new_home.T,
        new_latent,
        hidden,
        routes,
        route_logits,
        jnp.swapaxes(latent_cache, 2, 3),
        jnp.swapaxes(queries, 3, 4),
        w_gate,
        w_up,
        w_down,
    )
    results = (attended, moe_out)
    return pl.pallas_call(
        settle_kernel,
        out_shape=tuple(jax.ShapeDtypeStruct(one.shape, one.dtype) for one in results),
        in_specs=[pl.BlockSpec(memory_space=pltpu.VMEM)] * 2,
        out_specs=(hbm, hbm),
        scratch_shapes=[pltpu.SemaphoreType.DMA((2,))],
        compiler_params=pltpu.CompilerParams(vmem_limit_bytes=1024 * 1024),
        name="settle",
    )(*results)


def attend_kernel(length_ref, query_ref, cache_ref, fresh_ref, out_ref):
    step_count, head_count, lat_width = query_ref.shape
    rows = step_count * head_count
    length = length_ref[pl.program_id(0)]
    scale = HEAD_QK ** (-0.5)
    query = query_ref[...].reshape(rows, lat_width)
    keys = cache_ref[...]
    scores = (
        lax.dot_general(
            query, keys, (((1,), (1,)), ((), ())), preferred_element_type=jnp.float32
        )
        * scale
    )
    place = lax.broadcasted_iota(jnp.int32, scores.shape, 1)
    scores = jnp.where(place < length, scores, -jnp.inf)
    row_step = lax.broadcasted_iota(jnp.int32, (rows, 1), 0) // head_count
    wide_query = query.astype(jnp.float32)
    fresh = fresh_ref[...].astype(jnp.float32)
    fresh_scores = []
    row_max = jnp.max(scores, 1, keepdims=True)
    for step in range(step_count):
        one = jnp.sum(wide_query * fresh[step : step + 1], 1, keepdims=True) * scale
        one = jnp.where(row_step >= step, one, -jnp.inf)
        row_max = jnp.maximum(row_max, one)
        fresh_scores.append(one)
    weights = jnp.exp(scores - row_max)
    fresh_weights = [jnp.exp(one - row_max) for one in fresh_scores]
    total = jnp.sum(weights, 1, keepdims=True)
    for one in fresh_weights:
        total = total + one
    probs = (weights / total).astype(jnp.bfloat16)
    served = jnp.dot(probs, keys[:, :KV_RANK], preferred_element_type=jnp.float32)
    for step in range(step_count):
        part = (fresh_weights[step] / total).astype(jnp.bfloat16).astype(jnp.float32)
        served = served + part * fresh[step : step + 1, :KV_RANK]
    out_ref[...] = served.astype(jnp.bfloat16).reshape(step_count, head_count, KV_RANK)


def attend(own_lengths, queries, cache, fresh):
    step_count, _, requests, heads, lat = queries.shape
    keys = cache.shape[2]
    return pl.pallas_call(
        attend_kernel,
        grid_spec=pltpu.PrefetchScalarGridSpec(
            num_scalar_prefetch=1,
            grid=(requests,),
            in_specs=[
                pl.BlockSpec((step_count, None, None, heads, lat), lambda r, n: (0, 0, r, 0, 0)),
                pl.BlockSpec((None, None, keys, lat), lambda r, n: (0, r, 0, 0)),
                pl.BlockSpec((None, step_count, lat), lambda r, n: (r, 0, 0)),
            ],
            out_specs=pl.BlockSpec((None, step_count, heads, KV_RANK), lambda r, n: (r, 0, 0, 0)),
        ),
        out_shape=jax.ShapeDtypeStruct((requests, step_count, heads, KV_RANK), jnp.bfloat16),
        name="attend",
    )(own_lengths, queries, cache, fresh)


def travel(even, odd, ranks):
    half = ranks // 2
    across = [(e, (e + half) % ranks) for e in range(ranks)]
    ahead = [(e, (e + 1) % ranks) for e in range(ranks)]
    behind = [(e, (e - 1) % ranks) for e in range(ranks)]
    far = lax.ppermute(even, "ep", across)
    left = lax.ppermute(odd, "ep", ahead)
    right = lax.ppermute(odd, "ep", behind)
    return far, left, right


def relocate(computed, arrived, new_home, ranks, own_rank):
    requests = computed.shape[0]
    far, left, right = arrived
    anchor = new_home[own_rank]
    results = []
    for request in range(requests):
        home, slot = anchor[request], request // 2
        if request % 2 == 0:
            moved = far[slot]
        else:
            moved = jnp.where(home == (own_rank + 1) % ranks, right[slot], left[slot])
        results.append(jnp.where(home == own_rank, computed[request], moved))
    return jnp.stack(results, 1)[:, None]


def shards(
    latent_cache,
    lengths,
    new_home,
    queries,
    new_latent,
    hidden,
    routes,
    route_logits,
    w_gate,
    w_up,
    w_down,
):
    ranks = lax.axis_size("ep")
    own_rank = lax.axis_index("ep")
    step_count, _, requests, width = hidden.shape
    own_rows = step_count * requests
    slices = lax.axis_size("dp")

    def shift(value, step):
        return lax.ppermute(value, "dp", [(i, (i + step) % slices) for i in range(slices)])

    rows = hidden.reshape(own_rows, width)
    copies = jnp.broadcast_to(rows[None], (ranks, own_rows, width))
    mine = lax.all_to_all(copies, "ep", split_axis=0, concat_axis=0, tiled=True)
    mine = mine.reshape(ranks * own_rows, width)

    computed = attend(
        lengths[own_rank], queries, latent_cache, jnp.swapaxes(new_latent[:, 0], 0, 1)
    )
    mine, computed, even, odd = lax.optimization_barrier(
        (mine, computed, computed[0::2], computed[1::2])
    )
    arrived = travel(even, odd, ranks)

    tokens = jnp.concatenate([mine] + [shift(mine, step) for step in range(1, slices)], 0)
    gate_part = jnp.dot(tokens, w_gate[0], preferred_element_type=jnp.float32)
    up_part = jnp.dot(tokens, w_up[0], preferred_element_type=jnp.float32)
    units = (jax.nn.silu(gate_part) * up_part).astype(jnp.bfloat16)
    slice_out = jnp.dot(units, w_down[0], preferred_element_type=jnp.float32)
    slice_out = slice_out.astype(jnp.bfloat16)
    parts = slice_out.reshape(slices, ranks * own_rows, width)
    whole = parts[0].astype(jnp.float32)
    for step in range(1, slices):
        whole = whole + shift(parts[step], -step).astype(jnp.float32)
    whole = whole.astype(jnp.bfloat16)
    whole, arrived = lax.optimization_barrier((whole, arrived))
    returned = lax.all_to_all(
        whole.reshape(ranks, own_rows, width), "ep", split_axis=0, concat_axis=0, tiled=True
    )

    attended = relocate(computed, arrived, new_home, ranks, own_rank)
    sigmoid_part = jax.nn.sigmoid(route_logits[:, 0].astype(jnp.float32))
    gates = 2.5 * sigmoid_part / jnp.sum(sigmoid_part, -1, keepdims=True)
    rank_ids = jnp.arange(ranks, dtype=jnp.int32)
    chosen = routes[:, 0, :, :, None] == rank_ids
    dense = jnp.sum(jnp.where(chosen, gates[..., None], 0.0), 2).reshape(own_rows, ranks)
    summed = jnp.sum(returned.astype(jnp.float32) * dense.T[:, :, None], 0)
    moe_out = summed.astype(jnp.bfloat16).reshape(step_count, 1, requests, width)
    return (attended, moe_out)


def solution(mesh):
    placed = (
        P("ep", "dp", None, None),
        P(None, "dp"),
        P(None, "dp"),
        P(None, "ep", "dp", None, None),
        P(None, "ep", "dp", None),
        P(None, "ep", "dp", None),
        P(None, "ep", "dp", None),
        P(None, "ep", "dp", None),
        P("ep", None, "dp"),
        P("ep", None, "dp"),
        P("ep", "dp", None),
    )
    out_specs = (P(None, "ep", "dp", None, None), P(None, "ep", "dp", None))
    ranks = mesh.shape["ep"]
    if mesh.shape["dp"] == 2 and ranks % 8 == 0 and 3 * ranks <= LANES:
        return jax.shard_map(
            ladder, mesh=mesh, in_specs=placed, out_specs=out_specs, check_vma=False
        )
    return jax.shard_map(
        shards,
        mesh=mesh,
        in_specs=placed,
        out_specs=out_specs,
        check_vma=False,
    )
```

```python
import functools

import jax
import jax.numpy as jnp
from jax import lax
from jax.experimental import pallas as pl
from jax.experimental.pallas import tpu as pltpu
from jax.sharding import PartitionSpec as P


KV_RANK = 512
HEAD_QK = 192
LANES = 128
MESH = pl.DeviceIdType.MESH
RETURN_CHUNKS = 4


def ladder_kernel(
    plan,
    lengths_hbm,
    homes_hbm,
    fresh_hbm,
    hidden_hbm,
    routes_hbm,
    logits_hbm,
    cache_hbm,
    query_hbm,
    gate_hbm,
    up_hbm,
    down_hbm,
    attended_ref,
    moe_ref,
    lengths_ref,
    homes_ref,
    fresh_ref,
    hidden_ref,
    routes_ref,
    logits_ref,
    slots,
    tokens,
    query,
    cache,
    w_gate,
    w_up,
    w_down,
    served,
    far,
    near,
    onward,
    beyond,
    own_part,
    pair_send,
    pair_recv,
    chip_part,
    chip_send,
    first_recv,
    second_keep,
    second_send,
    second_recv,
    line_part,
    line_send,
    line_recv,
    line_sems,
    load_sem,
    send_sem,
    recv_sem,
):
    ranks, line = plan["ranks"], plan["line"]
    steps, requests = hidden_ref.shape[0], hidden_ref.shape[2]
    own_rows = steps * requests
    lat = cache.shape[1]
    heads = query.shape[-1]
    width = hidden_ref.shape[-1]
    blocks = width // LANES
    half = 4
    core = lax.axis_index("dp")
    rank = lax.axis_index("ep")
    side, up, place = lax.rem(rank, 2), lax.rem(lax.div(rank, 2), 2), lax.div(rank, 4)
    cell = lax.rem(rank, 4)
    across_side, across_up = rank + 1 - 2 * side, rank + 2 - 4 * up
    diagonal = rank - cell + 3 - cell
    plane = (diagonal, across_side, across_up)
    other = 1 - core
    mine = core * half + cell
    far_rank = lax.rem(rank + ranks // 2, ranks)
    beyond_rank = lax.rem(rank + 4 - 8 * side + ranks, ranks)

    loads, sends = [], []

    def load(source, target):
        copy = pltpu.make_async_copy(source, target, load_sem.at[len(loads)])
        copy.start()
        loads.append(copy)
        return copy

    def send(source, target, to_core, to_rank):
        spot = len(sends)
        copy = pltpu.make_async_remote_copy(
            src_ref=source,
            dst_ref=target,
            send_sem=send_sem.at[spot],
            recv_sem=recv_sem.at[spot],
            device_id=(to_core, to_rank),
            device_id_type=MESH,
        )
        copy.start()
        sends.append(copy)
        return copy

    barrier = pltpu.get_barrier_semaphore()
    peers = [(other, rank)] + [(core, peer) for peer in plane]
    peers += [(core, lax.rem(rank + 4 * step, ranks)) for step in range(1, line)]
    for peer in peers:
        pl.semaphore_signal(barrier, inc=1, device_id=peer, device_id_type=MESH)

    token_loads = [
        load(hidden_hbm, hidden_ref),
        load(routes_hbm, routes_ref),
        load(logits_hbm, logits_ref),
    ]
    small_loads = [
        load(fresh_hbm, fresh_ref),
        load(lengths_hbm, lengths_ref),
        load(homes_hbm, homes_ref),
    ]
    attend_loads = {}
    for request in reversed(range(requests)):
        attend_loads[request] = (
            load(query_hbm.at[:, 0, request], query.at[request]),
            load(cache_hbm.at[0, request], cache.at[request]),
        )
    parts = 4
    rows = width // parts
    gate_loads = []
    for part in range(parts):
        span = pl.ds(part * rows, rows)
        gate_loads.append(
            (load(gate_hbm.at[0, span], w_gate.at[span]), load(up_hbm.at[0, span], w_up.at[span]))
        )
    down_load = load(down_hbm.at[0], w_down)

    for copy in token_loads:
        copy.wait()
    lane = lax.broadcasted_iota(jnp.int32, (requests, LANES), 1)
    expert = lane - jnp.where(lane >= 2 * ranks, 2 * ranks, jnp.where(lane >= ranks, ranks, 0))
    dense = []
    for step in range(steps):
        logits = logits_ref[step, 0].astype(jnp.float32)
        chosen = routes_ref[step, 0]
        sigmoid_part = 1.0 / (1.0 + jnp.exp(-logits))
        gates = 2.5 * sigmoid_part / jnp.sum(sigmoid_part, 1, keepdims=True)
        total = jnp.zeros((requests, LANES), jnp.float32)
        for k in range(chosen.shape[1]):
            total = total + jnp.where(chosen[:, k : k + 1] == expert, gates[:, k : k + 1], 0.0)
        dense.append(total)
    dense = jnp.concatenate(dense, 0)
    lane = lax.broadcasted_iota(jnp.int32, (own_rows, LANES), 1)
    high = dense.astype(jnp.bfloat16).astype(jnp.float32)
    middle = (dense - high).astype(jnp.bfloat16).astype(jnp.float32)
    low = dense - high - middle
    coded = jnp.where(lane < ranks, high, jnp.where(lane < 2 * ranks, middle, low))
    coded = jnp.where(lane < 3 * ranks, coded, 0.0)
    own = jnp.concatenate(
        [hidden_ref[step, 0].astype(jnp.float32) for step in range(steps)], 0
    )
    for block in range(blocks):
        slots[mine, place, block] = own[:, block * LANES : (block + 1) * LANES].astype(jnp.bfloat16)
    slots[mine, place, blocks] = coded.astype(jnp.bfloat16)

    pl.semaphore_wait(barrier, len(peers))

    def share(block, slot, to_core, to_rank):
        return send(slots.at[block, slot], slots.at[block, slot], to_core, to_rank)

    def spread(slot):
        plane_sends.append([share(mine, slot, core, peer) for peer in plane])
        pair_sends.append([share(mine, slot, other, rank)])

    def arrival(step, slot):
        return pltpu.make_async_remote_copy(
            src_ref=slots.at[mine, slot],
            dst_ref=slots.at[mine, slot],
            send_sem=line_sems.at[0, step - 1],
            recv_sem=line_sems.at[1, step - 1],
            device_id=(core, lax.rem(rank + 4 * step, ranks)),
            device_id_type=MESH,
        )

    def merge(block):
        tokens[block] = jnp.concatenate([slots[block, slot] for slot in range(line)], 1)

    plane_sends, pair_sends = [], []
    for step in reversed(range(1, line)):
        arrival(step, place).start()
    spread(place)

    near_sends, onward_sends, beyond_sends, far_sends = {}, {}, {}, {}
    quarter = heads // 2

    def cut(ref, piece):
        return ref.at[piece // 2, pl.ds(piece % 2 * quarter, quarter)]

    def send_near(piece):
        near_sends[piece] = send(cut(served.at[1], piece), cut(near, piece), core, across_side)

    def send_onward(piece):
        near_sends[piece].wait_recv()
        onward_sends[piece] = send(cut(near, piece), cut(onward, piece), core, across_up)

    def send_beyond(piece):
        onward_sends[piece].wait_recv()
        beyond_sends[piece] = send(cut(onward, piece), cut(beyond, piece), core, beyond_rank)

    def attend(request):
        for copy in attend_loads[request]:
            copy.wait()
        length = lengths_ref[request, rank]
        scale = HEAD_QK ** (-0.5)
        lines = jnp.concatenate([query[request, step] for step in range(steps)], 1)
        keys = cache[request]
        scores = (
            lax.dot_general(
                lines, keys, (((0,), (0,)), ((), ())), preferred_element_type=jnp.float32
            )
            * scale
        )
        spot = lax.broadcasted_iota(jnp.int32, scores.shape, 1)
        scores = jnp.where(spot < length, scores, -jnp.inf)
        row_step = lax.broadcasted_iota(jnp.int32, (steps * heads, 1), 0) // heads
        fresh = [
            fresh_ref[step, 0].astype(jnp.float32)[request : request + 1] for step in range(steps)
        ]
        pad = jnp.zeros((16 - steps, lat), jnp.float32)
        fresh_keys = jnp.concatenate(fresh + [pad], 0).astype(jnp.bfloat16)
        fresh_all = (
            lax.dot_general(
                lines, fresh_keys, (((0,), (1,)), ((), ())), preferred_element_type=jnp.float32
            )
            * scale
        )
        row_max = jnp.max(scores, 1, keepdims=True)
        fresh_scores = []
        for step in range(steps):
            one = jnp.where(row_step >= step, fresh_all[:, step : step + 1], -jnp.inf)
            row_max = jnp.maximum(row_max, one)
            fresh_scores.append(one)
        weights = jnp.exp(scores - row_max)
        fresh_weights = [jnp.exp(one - row_max) for one in fresh_scores]
        total = jnp.sum(weights, 1, keepdims=True)
        for one in fresh_weights:
            total = total + one
        share = 1.0 / total
        probs = (weights * share).astype(jnp.bfloat16)
        result = lax.dot_general(
            probs, keys[:KV_RANK], (((1,), (1,)), ((), ())), preferred_element_type=jnp.float32
        )
        for step in range(steps):
            part = (fresh_weights[step] * share).astype(jnp.bfloat16).astype(jnp.float32)
            result = result + part * fresh[step][:, :KV_RANK]
        result = result.astype(jnp.bfloat16)
        for step in range(steps):
            served[request, step] = result[step * heads : (step + 1) * heads]

    for copy in small_loads:
        copy.wait()
    attend(1)
    send_near(0)
    attend(0)
    far_sends = [send(served.at[0, step], far.at[step], core, far_rank) for step in range(steps)]

    lower = place < line // 2
    for reach in range(1, line):
        step = jnp.where(lower, line - reach, reach)
        slot = lax.rem(place - step + line, line)
        arrival(step, slot).wait_recv()
        spread(slot)
    merge(mine)
    send_near(1)
    send_near(2)
    send_near(3)
    for reach in range(line):
        slot = jnp.where(lower, place + reach, place - reach + line)
        slot = lax.rem(slot, line)
        for copy, peer in zip(plane_sends[reach], plane):
            copy.wait_recv()
            pair_sends[reach].append(share(core * half + lax.rem(peer, 4), slot, other, rank))
    send_onward(0)
    send_onward(1)
    for peer in plane:
        merge(core * half + lax.rem(peer, 4))
    for copies in pair_sends:
        for copy in copies:
            copy.wait_recv()
    for block in range(half):
        merge(other * half + block)

    gate_part = jnp.zeros((2 * half * line * own_rows, w_gate.shape[1]), jnp.float32)
    up_part = gate_part
    piece = blocks // parts
    for done in range(parts):
        for copy in gate_loads[done]:
            copy.wait()
        pieces = [
            tokens[:, block].reshape(gate_part.shape[0], LANES)
            for block in range(done * piece, (done + 1) * piece)
        ]
        values = jnp.concatenate(pieces, 1)
        span_rows = pl.ds(done * rows, rows)
        gate_part = gate_part + jnp.dot(
            values, w_gate[span_rows], preferred_element_type=jnp.float32
        )
        up_part = up_part + jnp.dot(values, w_up[span_rows], preferred_element_type=jnp.float32)
    send_onward(2)
    send_onward(3)
    units = (gate_part / (1.0 + jnp.exp(-gate_part)) * up_part).astype(jnp.bfloat16)
    coded = tokens[:, blocks].reshape(gate_part.shape[0], LANES).astype(jnp.float32)
    lane = lax.broadcasted_iota(jnp.int32, coded.shape, 1)
    hit = (lane == rank) | (lane == rank + ranks) | (lane == rank + 2 * ranks)
    gain = jnp.sum(jnp.where(hit, coded, 0.0), 1, keepdims=True)
    down_load.wait()

    chunk = width // RETURN_CHUNKS
    side_rows = half * line * own_rows
    cell_rows = line * own_rows
    pairs, firsts, seconds, lines = {}, {}, {}, {}

    def stage_down(c):
        out = jnp.dot(
            units, w_down[:, c * chunk : (c + 1) * chunk], preferred_element_type=jnp.float32
        )
        out = out * gain
        for part in range(2):
            value = out[part * side_rows : (part + 1) * side_rows]
            own_part[c, part] = value
            pair_send[c, part] = value.astype(jnp.bfloat16)
        pairs[c] = send(pair_send.at[c, other], pair_recv.at[c], other, rank)

    second = across_side * other + across_up * core
    first = across_up * other + across_side * core

    def stage_chip(c):
        pairs[c].wait_recv()
        value = own_part[c, core] + pair_recv[c].astype(jnp.float32)
        for part in range(half):
            cut = value[part * cell_rows : (part + 1) * cell_rows]
            chip_part[c, part] = cut
            chip_send[c, part] = cut.astype(jnp.bfloat16)
        firsts[c] = [
            send(chip_send.at[c, 3 - cell], first_recv.at[c, 1], core, second),
            send(chip_send.at[c, lax.rem(second, 4)], first_recv.at[c, 0], core, second),
        ]

    def stage_plane(c):
        firsts[c][0].wait_recv()
        value = chip_part[c, lax.rem(first, 4)] + first_recv[c, 1].astype(jnp.float32)
        second_send[c] = value.astype(jnp.bfloat16)
        seconds[c] = send(second_send.at[c], second_recv.at[c], core, first)
        firsts[c][1].wait_recv()
        second_keep[c] = chip_part[c, cell] + first_recv[c, 0].astype(jnp.float32)

    def stage_line(c):
        seconds[c].wait_recv()
        value = second_keep[c] + second_recv[c].astype(jnp.float32)
        for spot in range(line):
            cut = value[spot * own_rows : (spot + 1) * own_rows]
            line_part[c, spot] = cut
            line_send[c, spot] = cut.astype(jnp.bfloat16)
        lines[c] = [
            send(
                line_send.at[c, lax.rem(place + step, line)],
                line_recv.at[c, step - 1],
                core,
                lax.rem(rank + 4 * step, ranks),
            )
            for step in range(1, line)
        ]

    def stage_sum(c):
        value = line_part[c, place]
        for step in range(1, line):
            lines[c][step - 1].wait_recv()
            value = value + line_recv[c, step - 1].astype(jnp.float32)
        value = value.astype(jnp.bfloat16)
        for step in range(steps):
            moe_ref[step, 0, :, c * chunk : (c + 1) * chunk] = value[
                step * requests : (step + 1) * requests
            ]

    def settle(request, step):
        home = homes_ref[request, rank]
        arrived = far[step]
        if request % 2:
            arrived = jnp.where(side == up, beyond[step], onward[step])
            arrived = jnp.where(home == across_side, near[step], arrived)
        attended_ref[step, 0, request] = jnp.where(home == rank, served[request, step], arrived)

    for c in range(RETURN_CHUNKS):
        stage_down(c)
    send_beyond(0)
    send_beyond(1)
    for c in range(RETURN_CHUNKS):
        stage_chip(c)
    send_beyond(2)
    send_beyond(3)
    for c in range(RETURN_CHUNKS):
        stage_plane(c)
    for c in range(RETURN_CHUNKS):
        stage_line(c)
    for step in range(steps):
        far_sends[step].wait_recv()
        settle(0, step)
    for piece in (0, 1):
        beyond_sends[piece].wait_recv()
    settle(1, 0)
    for c in range(RETURN_CHUNKS):
        stage_sum(c)
    for step in range(1, steps):
        for piece in (2, 3):
            beyond_sends[piece].wait_recv()
        settle(1, step)
    for copy in sends:
        copy.wait_send()
    for step in range(1, line):
        arrival(step, place).wait_send()


def settle_kernel(attended_ref, moe_ref, attended_hbm, moe_hbm, sems):
    copies = (
        pltpu.make_async_copy(attended_ref, attended_hbm, sems.at[0]),
        pltpu.make_async_copy(moe_ref, moe_hbm, sems.at[1]),
    )
    for copy in copies:
        copy.start()
    for copy in copies:
        copy.wait()


def ladder(
    latent_cache,
    lengths,
    new_home,
    queries,
    new_latent,
    hidden,
    routes,
    route_logits,
    w_gate,
    w_up,
    w_down,
):
    ranks, slices = lax.axis_size("ep"), lax.axis_size("dp")
    line = ranks // 4
    steps, _, requests, width = hidden.shape
    heads, lat = queries.shape[3:]
    keys = latent_cache.shape[2]
    units = w_gate.shape[2]
    layers = width // LANES + 1
    own_rows = steps * requests
    chunk = width // RETURN_CHUNKS
    cell_rows = line * own_rows
    bf16, f32 = jnp.bfloat16, jnp.float32
    hbm = pl.BlockSpec(memory_space=pl.ANY)
    gather_sends = line * (3 + 4)
    return_sends = RETURN_CHUNKS * (1 + 2 + 1 + line - 1)
    sends = gather_sends + return_sends + 12 + steps
    loads = 6 + 2 * requests + 8 + 1
    attended, moe_out = pl.pallas_call(
        functools.partial(ladder_kernel, dict(ranks=ranks, line=line)),
        out_shape=(
            pltpu.VMEM((steps, 1, requests, heads, KV_RANK), bf16),
            pltpu.VMEM((steps, 1, requests, width), bf16),
        ),
        in_specs=[hbm] * 11,
        out_specs=(pl.BlockSpec(memory_space=pltpu.VMEM),) * 2,
        scratch_shapes=[
            pltpu.SMEM((requests, ranks), jnp.int32),
            pltpu.SMEM((requests, ranks), jnp.int32),
            pltpu.VMEM(new_latent.shape, bf16),
            pltpu.VMEM(hidden.shape, bf16),
            pltpu.VMEM(routes.shape, jnp.int32),
            pltpu.VMEM(route_logits.shape, bf16),
            pltpu.VMEM((slices * 4, line, layers, own_rows, LANES), bf16),
            pltpu.VMEM((slices * 4, layers, cell_rows, LANES), bf16),
            pltpu.VMEM((requests, steps, lat, heads), bf16),
            pltpu.VMEM((requests, lat, keys), bf16),
            pltpu.VMEM((width, units), bf16),
            pltpu.VMEM((width, units), bf16),
            pltpu.VMEM((units, width), bf16),
            pltpu.VMEM((requests, steps, heads, KV_RANK), bf16),
            pltpu.VMEM((steps, heads, KV_RANK), bf16),
            pltpu.VMEM((steps, heads, KV_RANK), bf16),
            pltpu.VMEM((steps, heads, KV_RANK), bf16),
            pltpu.VMEM((steps, heads, KV_RANK), bf16),
            pltpu.VMEM((RETURN_CHUNKS, 2, 4 * cell_rows, chunk), f32),
            pltpu.VMEM((RETURN_CHUNKS, 2, 4 * cell_rows, chunk), bf16),
            pltpu.VMEM((RETURN_CHUNKS, 4 * cell_rows, chunk), bf16),
            pltpu.VMEM((RETURN_CHUNKS, 4, cell_rows, chunk), f32),
            pltpu.VMEM((RETURN_CHUNKS, 4, cell_rows, chunk), bf16),
            pltpu.VMEM((RETURN_CHUNKS, 2, cell_rows, chunk), bf16),
            pltpu.VMEM((RETURN_CHUNKS, cell_rows, chunk), f32),
            pltpu.VMEM((RETURN_CHUNKS, cell_rows, chunk), bf16),
            pltpu.VMEM((RETURN_CHUNKS, cell_rows, chunk), bf16),
            pltpu.VMEM((RETURN_CHUNKS, line, own_rows, chunk), f32),
            pltpu.VMEM((RETURN_CHUNKS, line, own_rows, chunk), bf16),
            pltpu.VMEM((RETURN_CHUNKS, line - 1, own_rows, chunk), bf16),
            pltpu.SemaphoreType.DMA((2, line - 1)),
            pltpu.SemaphoreType.DMA((loads,)),
            pltpu.SemaphoreType.DMA((sends,)),
            pltpu.SemaphoreType.DMA((sends,)),
        ],
        compiler_params=pltpu.CompilerParams(
            collective_id=0, has_side_effects=True, vmem_limit_bytes=56 * 1024 * 1024
        ),
        name="ladder",
    )(
        lengths.T,
        new_home.T,
        new_latent,
        hidden,
        routes,
        route_logits,
        jnp.swapaxes(latent_cache, 2, 3),
        jnp.swapaxes(queries, 3, 4),
        w_gate,
        w_up,
        w_down,
    )
    results = (attended, moe_out)
    return pl.pallas_call(
        settle_kernel,
        out_shape=tuple(jax.ShapeDtypeStruct(one.shape, one.dtype) for one in results),
        in_specs=[pl.BlockSpec(memory_space=pltpu.VMEM)] * 2,
        out_specs=(hbm, hbm),
        scratch_shapes=[pltpu.SemaphoreType.DMA((2,))],
        compiler_params=pltpu.CompilerParams(vmem_limit_bytes=1024 * 1024),
        name="settle",
    )(*results)


def attend_kernel(length_ref, query_ref, cache_ref, fresh_ref, out_ref):
    step_count, head_count, lat_width = query_ref.shape
    rows = step_count * head_count
    length = length_ref[pl.program_id(0)]
    scale = HEAD_QK ** (-0.5)
    query = query_ref[...].reshape(rows, lat_width)
    keys = cache_ref[...]
    scores = (
        lax.dot_general(
            query, keys, (((1,), (1,)), ((), ())), preferred_element_type=jnp.float32
        )
        * scale
    )
    place = lax.broadcasted_iota(jnp.int32, scores.shape, 1)
    scores = jnp.where(place < length, scores, -jnp.inf)
    row_step = lax.broadcasted_iota(jnp.int32, (rows, 1), 0) // head_count
    wide_query = query.astype(jnp.float32)
    fresh = fresh_ref[...].astype(jnp.float32)
    fresh_scores = []
    row_max = jnp.max(scores, 1, keepdims=True)
    for step in range(step_count):
        one = jnp.sum(wide_query * fresh[step : step + 1], 1, keepdims=True) * scale
        one = jnp.where(row_step >= step, one, -jnp.inf)
        row_max = jnp.maximum(row_max, one)
        fresh_scores.append(one)
    weights = jnp.exp(scores - row_max)
    fresh_weights = [jnp.exp(one - row_max) for one in fresh_scores]
    total = jnp.sum(weights, 1, keepdims=True)
    for one in fresh_weights:
        total = total + one
    probs = (weights / total).astype(jnp.bfloat16)
    served = jnp.dot(probs, keys[:, :KV_RANK], preferred_element_type=jnp.float32)
    for step in range(step_count):
        part = (fresh_weights[step] / total).astype(jnp.bfloat16).astype(jnp.float32)
        served = served + part * fresh[step : step + 1, :KV_RANK]
    out_ref[...] = served.astype(jnp.bfloat16).reshape(step_count, head_count, KV_RANK)


def attend(own_lengths, queries, cache, fresh):
    step_count, _, requests, heads, lat = queries.shape
    keys = cache.shape[2]
    return pl.pallas_call(
        attend_kernel,
        grid_spec=pltpu.PrefetchScalarGridSpec(
            num_scalar_prefetch=1,
            grid=(requests,),
            in_specs=[
                pl.BlockSpec((step_count, None, None, heads, lat), lambda r, n: (0, 0, r, 0, 0)),
                pl.BlockSpec((None, None, keys, lat), lambda r, n: (0, r, 0, 0)),
                pl.BlockSpec((None, step_count, lat), lambda r, n: (r, 0, 0)),
            ],
            out_specs=pl.BlockSpec((None, step_count, heads, KV_RANK), lambda r, n: (r, 0, 0, 0)),
        ),
        out_shape=jax.ShapeDtypeStruct((requests, step_count, heads, KV_RANK), jnp.bfloat16),
        name="attend",
    )(own_lengths, queries, cache, fresh)


def travel(even, odd, ranks):
    half = ranks // 2
    across = [(e, (e + half) % ranks) for e in range(ranks)]
    ahead = [(e, (e + 1) % ranks) for e in range(ranks)]
    behind = [(e, (e - 1) % ranks) for e in range(ranks)]
    far = lax.ppermute(even, "ep", across)
    left = lax.ppermute(odd, "ep", ahead)
    right = lax.ppermute(odd, "ep", behind)
    return far, left, right


def relocate(computed, arrived, new_home, ranks, own_rank):
    requests = computed.shape[0]
    far, left, right = arrived
    anchor = new_home[own_rank]
    results = []
    for request in range(requests):
        home, slot = anchor[request], request // 2
        if request % 2 == 0:
            moved = far[slot]
        else:
            moved = jnp.where(home == (own_rank + 1) % ranks, right[slot], left[slot])
        results.append(jnp.where(home == own_rank, computed[request], moved))
    return jnp.stack(results, 1)[:, None]


def shards(
    latent_cache,
    lengths,
    new_home,
    queries,
    new_latent,
    hidden,
    routes,
    route_logits,
    w_gate,
    w_up,
    w_down,
):
    ranks = lax.axis_size("ep")
    own_rank = lax.axis_index("ep")
    step_count, _, requests, width = hidden.shape
    own_rows = step_count * requests
    slices = lax.axis_size("dp")

    def shift(value, step):
        return lax.ppermute(value, "dp", [(i, (i + step) % slices) for i in range(slices)])

    rows = hidden.reshape(own_rows, width)
    copies = jnp.broadcast_to(rows[None], (ranks, own_rows, width))
    mine = lax.all_to_all(copies, "ep", split_axis=0, concat_axis=0, tiled=True)
    mine = mine.reshape(ranks * own_rows, width)

    computed = attend(
        lengths[own_rank], queries, latent_cache, jnp.swapaxes(new_latent[:, 0], 0, 1)
    )
    mine, computed, even, odd = lax.optimization_barrier(
        (mine, computed, computed[0::2], computed[1::2])
    )
    arrived = travel(even, odd, ranks)

    tokens = jnp.concatenate([mine] + [shift(mine, step) for step in range(1, slices)], 0)
    gate_part = jnp.dot(tokens, w_gate[0], preferred_element_type=jnp.float32)
    up_part = jnp.dot(tokens, w_up[0], preferred_element_type=jnp.float32)
    units = (jax.nn.silu(gate_part) * up_part).astype(jnp.bfloat16)
    slice_out = jnp.dot(units, w_down[0], preferred_element_type=jnp.float32)
    slice_out = slice_out.astype(jnp.bfloat16)
    parts = slice_out.reshape(slices, ranks * own_rows, width)
    whole = parts[0].astype(jnp.float32)
    for step in range(1, slices):
        whole = whole + shift(parts[step], -step).astype(jnp.float32)
    whole = whole.astype(jnp.bfloat16)
    whole, arrived = lax.optimization_barrier((whole, arrived))
    returned = lax.all_to_all(
        whole.reshape(ranks, own_rows, width), "ep", split_axis=0, concat_axis=0, tiled=True
    )

    attended = relocate(computed, arrived, new_home, ranks, own_rank)
    sigmoid_part = jax.nn.sigmoid(route_logits[:, 0].astype(jnp.float32))
    gates = 2.5 * sigmoid_part / jnp.sum(sigmoid_part, -1, keepdims=True)
    rank_ids = jnp.arange(ranks, dtype=jnp.int32)
    chosen = routes[:, 0, :, :, None] == rank_ids
    dense = jnp.sum(jnp.where(chosen, gates[..., None], 0.0), 2).reshape(own_rows, ranks)
    summed = jnp.sum(returned.astype(jnp.float32) * dense.T[:, :, None], 0)
    moe_out = summed.astype(jnp.bfloat16).reshape(step_count, 1, requests, width)
    return (attended, moe_out)


def solution(mesh):
    placed = (
        P("ep", "dp", None, None),
        P(None, "dp"),
        P(None, "dp"),
        P(None, "ep", "dp", None, None),
        P(None, "ep", "dp", None),
        P(None, "ep", "dp", None),
        P(None, "ep", "dp", None),
        P(None, "ep", "dp", None),
        P("ep", None, "dp"),
        P("ep", None, "dp"),
        P("ep", "dp", None),
    )
    out_specs = (P(None, "ep", "dp", None, None), P(None, "ep", "dp", None))
    ranks = mesh.shape["ep"]
    if mesh.shape["dp"] == 2 and ranks % 8 == 0 and 3 * ranks <= LANES:
        return jax.shard_map(
            ladder, mesh=mesh, in_specs=placed, out_specs=out_specs, check_vma=False
        )
    return jax.shard_map(
        shards,
        mesh=mesh,
        in_specs=placed,
        out_specs=out_specs,
        check_vma=False,
    )
```

```python
import functools

import jax
import jax.numpy as jnp
from jax import lax
from jax.experimental import pallas as pl
from jax.experimental.pallas import tpu as pltpu
from jax.sharding import PartitionSpec as P


KV_RANK = 512
HEAD_QK = 192
LANES = 128
MESH = pl.DeviceIdType.MESH
RETURN_CHUNKS = 2


def ladder_kernel(
    plan,
    lengths_hbm,
    homes_hbm,
    fresh_hbm,
    hidden_hbm,
    routes_hbm,
    logits_hbm,
    cache_hbm,
    query_hbm,
    gate_hbm,
    up_hbm,
    down_hbm,
    attended_ref,
    moe_ref,
    lengths_ref,
    homes_ref,
    fresh_ref,
    hidden_ref,
    routes_ref,
    logits_ref,
    slots,
    tokens,
    query,
    cache,
    w_gate,
    w_up,
    w_down,
    served,
    far,
    near,
    onward,
    beyond,
    own_part,
    pair_send,
    pair_recv,
    chip_part,
    chip_send,
    first_recv,
    second_keep,
    second_send,
    second_recv,
    line_part,
    line_send,
    line_recv,
    line_sems,
    load_sem,
    send_sem,
    recv_sem,
):
    ranks, line = plan["ranks"], plan["line"]
    steps, requests = hidden_ref.shape[0], hidden_ref.shape[2]
    own_rows = steps * requests
    lat = cache.shape[1]
    heads = query.shape[-1]
    width = hidden_ref.shape[-1]
    blocks = width // LANES
    half = 4
    core = lax.axis_index("dp")
    rank = lax.axis_index("ep")
    side, up, place = lax.rem(rank, 2), lax.rem(lax.div(rank, 2), 2), lax.div(rank, 4)
    cell = lax.rem(rank, 4)
    across_side, across_up = rank + 1 - 2 * side, rank + 2 - 4 * up
    diagonal = rank - cell + 3 - cell
    plane = (diagonal, across_side, across_up)
    other = 1 - core
    mine = core * half + cell
    far_rank = lax.rem(rank + ranks // 2, ranks)
    beyond_rank = lax.rem(rank + 4 - 8 * side + ranks, ranks)

    loads, sends = [], []

    def load(source, target):
        copy = pltpu.make_async_copy(source, target, load_sem.at[len(loads)])
        copy.start()
        loads.append(copy)
        return copy

    def send(source, target, to_core, to_rank):
        spot = len(sends)
        copy = pltpu.make_async_remote_copy(
            src_ref=source,
            dst_ref=target,
            send_sem=send_sem.at[spot],
            recv_sem=recv_sem.at[spot],
            device_id=(to_core, to_rank),
            device_id_type=MESH,
        )
        copy.start()
        sends.append(copy)
        return copy

    barrier = pltpu.get_barrier_semaphore()
    peers = [(other, rank)] + [(core, peer) for peer in plane]
    peers += [(core, lax.rem(rank + 4 * step, ranks)) for step in range(1, line)]
    for peer in peers:
        pl.semaphore_signal(barrier, inc=1, device_id=peer, device_id_type=MESH)

    token_loads = [
        load(hidden_hbm, hidden_ref),
        load(routes_hbm, routes_ref),
        load(logits_hbm, logits_ref),
    ]
    small_loads = [
        load(fresh_hbm, fresh_ref),
        load(lengths_hbm, lengths_ref),
        load(homes_hbm, homes_ref),
    ]
    attend_loads = {}
    for request in reversed(range(requests)):
        attend_loads[request] = (
            load(query_hbm.at[:, 0, request], query.at[request]),
            load(cache_hbm.at[0, request], cache.at[request]),
        )
    parts = 2
    rows = width // parts
    gate_loads = []
    for part in range(parts):
        span = pl.ds(part * rows, rows)
        gate_loads.append(
            (load(gate_hbm.at[0, span], w_gate.at[span]), load(up_hbm.at[0, span], w_up.at[span]))
        )
    down_load = load(down_hbm.at[0], w_down)

    for copy in token_loads:
        copy.wait()
    lane = lax.broadcasted_iota(jnp.int32, (requests, LANES), 1)
    expert = lane - jnp.where(lane >= 2 * ranks, 2 * ranks, jnp.where(lane >= ranks, ranks, 0))
    dense = []
    for step in range(steps):
        logits = logits_ref[step, 0].astype(jnp.float32)
        chosen = routes_ref[step, 0]
        sigmoid_part = 1.0 / (1.0 + jnp.exp(-logits))
        gates = 2.5 * sigmoid_part / jnp.sum(sigmoid_part, 1, keepdims=True)
        total = jnp.zeros((requests, LANES), jnp.float32)
        for k in range(chosen.shape[1]):
            total = total + jnp.where(chosen[:, k : k + 1] == expert, gates[:, k : k + 1], 0.0)
        dense.append(total)
    dense = jnp.concatenate(dense, 0)
    lane = lax.broadcasted_iota(jnp.int32, (own_rows, LANES), 1)
    high = dense.astype(jnp.bfloat16).astype(jnp.float32)
    middle = (dense - high).astype(jnp.bfloat16).astype(jnp.float32)
    low = dense - high - middle
    coded = jnp.where(lane < ranks, high, jnp.where(lane < 2 * ranks, middle, low))
    coded = jnp.where(lane < 3 * ranks, coded, 0.0)
    own = jnp.concatenate(
        [hidden_ref[step, 0].astype(jnp.float32) for step in range(steps)], 0
    )
    for block in range(blocks):
        slots[mine, place, block] = own[:, block * LANES : (block + 1) * LANES].astype(jnp.bfloat16)
    slots[mine, place, blocks] = coded.astype(jnp.bfloat16)

    pl.semaphore_wait(barrier, len(peers))

    def share(block, slot, to_core, to_rank):
        return send(slots.at[block, slot], slots.at[block, slot], to_core, to_rank)

    def spread(slot):
        plane_sends.append([share(mine, slot, core, peer) for peer in plane])
        pair_sends.append([share(mine, slot, other, rank)])

    def arrival(step, slot):
        return pltpu.make_async_remote_copy(
            src_ref=slots.at[mine, slot],
            dst_ref=slots.at[mine, slot],
            send_sem=line_sems.at[0, step - 1],
            recv_sem=line_sems.at[1, step - 1],
            device_id=(core, lax.rem(rank + 4 * step, ranks)),
            device_id_type=MESH,
        )

    def merge(block):
        tokens[block] = jnp.concatenate([slots[block, slot] for slot in range(line)], 1)

    plane_sends, pair_sends = [], []
    for step in reversed(range(1, line)):
        arrival(step, place).start()
    spread(place)

    near_sends, onward_sends, beyond_sends, far_sends = {}, {}, {}, {}
    quarter = heads // 2

    def cut(ref, piece):
        return ref.at[piece // 2, pl.ds(piece % 2 * quarter, quarter)]

    def send_near(piece):
        near_sends[piece] = send(cut(served.at[1], piece), cut(near, piece), core, across_side)

    def send_onward(piece):
        near_sends[piece].wait_recv()
        onward_sends[piece] = send(cut(near, piece), cut(onward, piece), core, across_up)

    def send_beyond(piece):
        onward_sends[piece].wait_recv()
        beyond_sends[piece] = send(cut(onward, piece), cut(beyond, piece), core, beyond_rank)

    def attend(request):
        for copy in attend_loads[request]:
            copy.wait()
        length = lengths_ref[request, rank]
        scale = HEAD_QK ** (-0.5)
        lines = jnp.concatenate([query[request, step] for step in range(steps)], 1)
        keys = cache[request]
        scores = (
            lax.dot_general(
                lines, keys, (((0,), (0,)), ((), ())), preferred_element_type=jnp.float32
            )
            * scale
        )
        spot = lax.broadcasted_iota(jnp.int32, scores.shape, 1)
        scores = jnp.where(spot < length, scores, -jnp.inf)
        row_step = lax.broadcasted_iota(jnp.int32, (steps * heads, 1), 0) // heads
        fresh = [
            fresh_ref[step, 0].astype(jnp.float32)[request : request + 1] for step in range(steps)
        ]
        pad = jnp.zeros((16 - steps, lat), jnp.float32)
        fresh_keys = jnp.concatenate(fresh + [pad], 0).astype(jnp.bfloat16)
        fresh_all = (
            lax.dot_general(
                lines, fresh_keys, (((0,), (1,)), ((), ())), preferred_element_type=jnp.float32
            )
            * scale
        )
        row_max = jnp.max(scores, 1, keepdims=True)
        fresh_scores = []
        for step in range(steps):
            one = jnp.where(row_step >= step, fresh_all[:, step : step + 1], -jnp.inf)
            row_max = jnp.maximum(row_max, one)
            fresh_scores.append(one)
        weights = jnp.exp(scores - row_max)
        fresh_weights = [jnp.exp(one - row_max) for one in fresh_scores]
        total = jnp.sum(weights, 1, keepdims=True)
        for one in fresh_weights:
            total = total + one
        share = 1.0 / total
        probs = (weights * share).astype(jnp.bfloat16)
        result = lax.dot_general(
            probs, keys[:KV_RANK], (((1,), (1,)), ((), ())), preferred_element_type=jnp.float32
        )
        for step in range(steps):
            part = (fresh_weights[step] * share).astype(jnp.bfloat16).astype(jnp.float32)
            result = result + part * fresh[step][:, :KV_RANK]
        result = result.astype(jnp.bfloat16)
        for step in range(steps):
            served[request, step] = result[step * heads : (step + 1) * heads]

    for copy in small_loads:
        copy.wait()
    attend(1)
    send_near(0)
    attend(0)
    far_sends = [send(served.at[0, step], far.at[step], core, far_rank) for step in range(steps)]

    lower = place < line // 2
    for reach in range(1, line):
        step = jnp.where(lower, line - reach, reach)
        slot = lax.rem(place - step + line, line)
        arrival(step, slot).wait_recv()
        spread(slot)
    merge(mine)
    send_near(1)
    send_near(2)
    send_near(3)
    for reach in range(line):
        slot = jnp.where(lower, place + reach, place - reach + line)
        slot = lax.rem(slot, line)
        for copy, peer in zip(plane_sends[reach], plane):
            copy.wait_recv()
            pair_sends[reach].append(share(core * half + lax.rem(peer, 4), slot, other, rank))
    send_onward(0)
    send_onward(1)
    for peer in plane:
        merge(core * half + lax.rem(peer, 4))
    for copies in pair_sends:
        for copy in copies:
            copy.wait_recv()
    for block in range(half):
        merge(other * half + block)

    gate_part = jnp.zeros((2 * half * line * own_rows, w_gate.shape[1]), jnp.float32)
    up_part = gate_part
    piece = blocks // parts
    for done in range(parts):
        for copy in gate_loads[done]:
            copy.wait()
        pieces = [
            tokens[:, block].reshape(gate_part.shape[0], LANES)
            for block in range(done * piece, (done + 1) * piece)
        ]
        values = jnp.concatenate(pieces, 1)
        span_rows = pl.ds(done * rows, rows)
        gate_part = gate_part + jnp.dot(
            values, w_gate[span_rows], preferred_element_type=jnp.float32
        )
        up_part = up_part + jnp.dot(values, w_up[span_rows], preferred_element_type=jnp.float32)
    send_onward(2)
    send_onward(3)
    units = (gate_part / (1.0 + jnp.exp(-gate_part)) * up_part).astype(jnp.bfloat16)
    coded = tokens[:, blocks].reshape(gate_part.shape[0], LANES).astype(jnp.float32)
    lane = lax.broadcasted_iota(jnp.int32, coded.shape, 1)
    hit = (lane == rank) | (lane == rank + ranks) | (lane == rank + 2 * ranks)
    gain = jnp.sum(jnp.where(hit, coded, 0.0), 1, keepdims=True)
    down_load.wait()

    chunk = width // RETURN_CHUNKS
    side_rows = half * line * own_rows
    cell_rows = line * own_rows
    pairs, firsts, seconds, lines = {}, {}, {}, {}

    def stage_down(c):
        out = jnp.dot(
            units, w_down[:, c * chunk : (c + 1) * chunk], preferred_element_type=jnp.float32
        )
        out = out * gain
        for part in range(2):
            value = out[part * side_rows : (part + 1) * side_rows]
            own_part[c, part] = value
            pair_send[c, part] = value.astype(jnp.bfloat16)
        pairs[c] = send(pair_send.at[c, other], pair_recv.at[c], other, rank)

    second = across_side * other + across_up * core
    first = across_up * other + across_side * core

    def stage_chip(c):
        pairs[c].wait_recv()
        value = own_part[c, core] + pair_recv[c].astype(jnp.float32)
        for part in range(half):
            cut = value[part * cell_rows : (part + 1) * cell_rows]
            chip_part[c, part] = cut
            chip_send[c, part] = cut.astype(jnp.bfloat16)
        firsts[c] = [
            send(chip_send.at[c, 3 - cell], first_recv.at[c, 1], core, second),
            send(chip_send.at[c, lax.rem(second, 4)], first_recv.at[c, 0], core, second),
        ]

    def stage_plane(c):
        firsts[c][0].wait_recv()
        value = chip_part[c, lax.rem(first, 4)] + first_recv[c, 1].astype(jnp.float32)
        second_send[c] = value.astype(jnp.bfloat16)
        seconds[c] = send(second_send.at[c], second_recv.at[c], core, first)
        firsts[c][1].wait_recv()
        second_keep[c] = chip_part[c, cell] + first_recv[c, 0].astype(jnp.float32)

    def stage_line(c):
        seconds[c].wait_recv()
        value = second_keep[c] + second_recv[c].astype(jnp.float32)
        for spot in range(line):
            cut = value[spot * own_rows : (spot + 1) * own_rows]
            line_part[c, spot] = cut
            line_send[c, spot] = cut.astype(jnp.bfloat16)
        lines[c] = [
            send(
                line_send.at[c, lax.rem(place + step, line)],
                line_recv.at[c, step - 1],
                core,
                lax.rem(rank + 4 * step, ranks),
            )
            for step in range(1, line)
        ]

    def stage_sum(c):
        value = line_part[c, place]
        for step in range(1, line):
            lines[c][step - 1].wait_recv()
            value = value + line_recv[c, step - 1].astype(jnp.float32)
        value = value.astype(jnp.bfloat16)
        for step in range(steps):
            moe_ref[step, 0, :, c * chunk : (c + 1) * chunk] = value[
                step * requests : (step + 1) * requests
            ]

    def settle(request, step):
        home = homes_ref[request, rank]
        arrived = far[step]
        if request % 2:
            arrived = jnp.where(side == up, beyond[step], onward[step])
            arrived = jnp.where(home == across_side, near[step], arrived)
        attended_ref[step, 0, request] = jnp.where(home == rank, served[request, step], arrived)

    for c in range(RETURN_CHUNKS):
        stage_down(c)
    send_beyond(0)
    send_beyond(1)
    for c in range(RETURN_CHUNKS):
        stage_chip(c)
    send_beyond(2)
    send_beyond(3)
    for c in range(RETURN_CHUNKS):
        stage_plane(c)
    for c in range(RETURN_CHUNKS):
        stage_line(c)
    for step in range(steps):
        far_sends[step].wait_recv()
        settle(0, step)
    for piece in (0, 1):
        beyond_sends[piece].wait_recv()
    settle(1, 0)
    for c in range(RETURN_CHUNKS):
        stage_sum(c)
    for step in range(1, steps):
        for piece in (2, 3):
            beyond_sends[piece].wait_recv()
        settle(1, step)
    for copy in sends:
        copy.wait_send()
    for step in range(1, line):
        arrival(step, place).wait_send()


def settle_kernel(attended_ref, moe_ref, attended_hbm, moe_hbm, sems):
    copies = (
        pltpu.make_async_copy(attended_ref, attended_hbm, sems.at[0]),
        pltpu.make_async_copy(moe_ref, moe_hbm, sems.at[1]),
    )
    for copy in copies:
        copy.start()
    for copy in copies:
        copy.wait()


def ladder(
    latent_cache,
    lengths,
    new_home,
    queries,
    new_latent,
    hidden,
    routes,
    route_logits,
    w_gate,
    w_up,
    w_down,
):
    ranks, slices = lax.axis_size("ep"), lax.axis_size("dp")
    line = ranks // 4
    steps, _, requests, width = hidden.shape
    heads, lat = queries.shape[3:]
    keys = latent_cache.shape[2]
    units = w_gate.shape[2]
    layers = width // LANES + 1
    own_rows = steps * requests
    chunk = width // RETURN_CHUNKS
    cell_rows = line * own_rows
    bf16, f32 = jnp.bfloat16, jnp.float32
    hbm = pl.BlockSpec(memory_space=pl.ANY)
    gather_sends = line * (3 + 4)
    return_sends = RETURN_CHUNKS * (1 + 2 + 1 + line - 1)
    sends = gather_sends + return_sends + 12 + steps
    loads = 6 + 2 * requests + 4 + 1
    attended, moe_out = pl.pallas_call(
        functools.partial(ladder_kernel, dict(ranks=ranks, line=line)),
        out_shape=(
            pltpu.VMEM((steps, 1, requests, heads, KV_RANK), bf16),
            pltpu.VMEM((steps, 1, requests, width), bf16),
        ),
        in_specs=[hbm] * 11,
        out_specs=(pl.BlockSpec(memory_space=pltpu.VMEM),) * 2,
        scratch_shapes=[
            pltpu.SMEM((requests, ranks), jnp.int32),
            pltpu.SMEM((requests, ranks), jnp.int32),
            pltpu.VMEM(new_latent.shape, bf16),
            pltpu.VMEM(hidden.shape, bf16),
            pltpu.VMEM(routes.shape, jnp.int32),
            pltpu.VMEM(route_logits.shape, bf16),
            pltpu.VMEM((slices * 4, line, layers, own_rows, LANES), bf16),
            pltpu.VMEM((slices * 4, layers, cell_rows, LANES), bf16),
            pltpu.VMEM((requests, steps, lat, heads), bf16),
            pltpu.VMEM((requests, lat, keys), bf16),
            pltpu.VMEM((width, units), bf16),
            pltpu.VMEM((width, units), bf16),
            pltpu.VMEM((units, width), bf16),
            pltpu.VMEM((requests, steps, heads, KV_RANK), bf16),
            pltpu.VMEM((steps, heads, KV_RANK), bf16),
            pltpu.VMEM((steps, heads, KV_RANK), bf16),
            pltpu.VMEM((steps, heads, KV_RANK), bf16),
            pltpu.VMEM((steps, heads, KV_RANK), bf16),
            pltpu.VMEM((RETURN_CHUNKS, 2, 4 * cell_rows, chunk), f32),
            pltpu.VMEM((RETURN_CHUNKS, 2, 4 * cell_rows, chunk), bf16),
            pltpu.VMEM((RETURN_CHUNKS, 4 * cell_rows, chunk), bf16),
            pltpu.VMEM((RETURN_CHUNKS, 4, cell_rows, chunk), f32),
            pltpu.VMEM((RETURN_CHUNKS, 4, cell_rows, chunk), bf16),
            pltpu.VMEM((RETURN_CHUNKS, 2, cell_rows, chunk), bf16),
            pltpu.VMEM((RETURN_CHUNKS, cell_rows, chunk), f32),
            pltpu.VMEM((RETURN_CHUNKS, cell_rows, chunk), bf16),
            pltpu.VMEM((RETURN_CHUNKS, cell_rows, chunk), bf16),
            pltpu.VMEM((RETURN_CHUNKS, line, own_rows, chunk), f32),
            pltpu.VMEM((RETURN_CHUNKS, line, own_rows, chunk), bf16),
            pltpu.VMEM((RETURN_CHUNKS, line - 1, own_rows, chunk), bf16),
            pltpu.SemaphoreType.DMA((2, line - 1)),
            pltpu.SemaphoreType.DMA((loads,)),
            pltpu.SemaphoreType.DMA((sends,)),
            pltpu.SemaphoreType.DMA((sends,)),
        ],
        compiler_params=pltpu.CompilerParams(
            collective_id=0, has_side_effects=True, vmem_limit_bytes=56 * 1024 * 1024
        ),
        name="ladder",
    )(
        lengths.T,
        new_home.T,
        new_latent,
        hidden,
        routes,
        route_logits,
        jnp.swapaxes(latent_cache, 2, 3),
        jnp.swapaxes(queries, 3, 4),
        w_gate,
        w_up,
        w_down,
    )
    results = (attended, moe_out)
    return pl.pallas_call(
        settle_kernel,
        out_shape=tuple(jax.ShapeDtypeStruct(one.shape, one.dtype) for one in results),
        in_specs=[pl.BlockSpec(memory_space=pltpu.VMEM)] * 2,
        out_specs=(hbm, hbm),
        scratch_shapes=[pltpu.SemaphoreType.DMA((2,))],
        compiler_params=pltpu.CompilerParams(vmem_limit_bytes=1024 * 1024),
        name="settle",
    )(*results)


def attend_kernel(length_ref, query_ref, cache_ref, fresh_ref, out_ref):
    step_count, head_count, lat_width = query_ref.shape
    rows = step_count * head_count
    length = length_ref[pl.program_id(0)]
    scale = HEAD_QK ** (-0.5)
    query = query_ref[...].reshape(rows, lat_width)
    keys = cache_ref[...]
    scores = (
        lax.dot_general(
            query, keys, (((1,), (1,)), ((), ())), preferred_element_type=jnp.float32
        )
        * scale
    )
    place = lax.broadcasted_iota(jnp.int32, scores.shape, 1)
    scores = jnp.where(place < length, scores, -jnp.inf)
    row_step = lax.broadcasted_iota(jnp.int32, (rows, 1), 0) // head_count
    wide_query = query.astype(jnp.float32)
    fresh = fresh_ref[...].astype(jnp.float32)
    fresh_scores = []
    row_max = jnp.max(scores, 1, keepdims=True)
    for step in range(step_count):
        one = jnp.sum(wide_query * fresh[step : step + 1], 1, keepdims=True) * scale
        one = jnp.where(row_step >= step, one, -jnp.inf)
        row_max = jnp.maximum(row_max, one)
        fresh_scores.append(one)
    weights = jnp.exp(scores - row_max)
    fresh_weights = [jnp.exp(one - row_max) for one in fresh_scores]
    total = jnp.sum(weights, 1, keepdims=True)
    for one in fresh_weights:
        total = total + one
    probs = (weights / total).astype(jnp.bfloat16)
    served = jnp.dot(probs, keys[:, :KV_RANK], preferred_element_type=jnp.float32)
    for step in range(step_count):
        part = (fresh_weights[step] / total).astype(jnp.bfloat16).astype(jnp.float32)
        served = served + part * fresh[step : step + 1, :KV_RANK]
    out_ref[...] = served.astype(jnp.bfloat16).reshape(step_count, head_count, KV_RANK)


def attend(own_lengths, queries, cache, fresh):
    step_count, _, requests, heads, lat = queries.shape
    keys = cache.shape[2]
    return pl.pallas_call(
        attend_kernel,
        grid_spec=pltpu.PrefetchScalarGridSpec(
            num_scalar_prefetch=1,
            grid=(requests,),
            in_specs=[
                pl.BlockSpec((step_count, None, None, heads, lat), lambda r, n: (0, 0, r, 0, 0)),
                pl.BlockSpec((None, None, keys, lat), lambda r, n: (0, r, 0, 0)),
                pl.BlockSpec((None, step_count, lat), lambda r, n: (r, 0, 0)),
            ],
            out_specs=pl.BlockSpec((None, step_count, heads, KV_RANK), lambda r, n: (r, 0, 0, 0)),
        ),
        out_shape=jax.ShapeDtypeStruct((requests, step_count, heads, KV_RANK), jnp.bfloat16),
        name="attend",
    )(own_lengths, queries, cache, fresh)


def travel(even, odd, ranks):
    half = ranks // 2
    across = [(e, (e + half) % ranks) for e in range(ranks)]
    ahead = [(e, (e + 1) % ranks) for e in range(ranks)]
    behind = [(e, (e - 1) % ranks) for e in range(ranks)]
    far = lax.ppermute(even, "ep", across)
    left = lax.ppermute(odd, "ep", ahead)
    right = lax.ppermute(odd, "ep", behind)
    return far, left, right


def relocate(computed, arrived, new_home, ranks, own_rank):
    requests = computed.shape[0]
    far, left, right = arrived
    anchor = new_home[own_rank]
    results = []
    for request in range(requests):
        home, slot = anchor[request], request // 2
        if request % 2 == 0:
            moved = far[slot]
        else:
            moved = jnp.where(home == (own_rank + 1) % ranks, right[slot], left[slot])
        results.append(jnp.where(home == own_rank, computed[request], moved))
    return jnp.stack(results, 1)[:, None]


def shards(
    latent_cache,
    lengths,
    new_home,
    queries,
    new_latent,
    hidden,
    routes,
    route_logits,
    w_gate,
    w_up,
    w_down,
):
    ranks = lax.axis_size("ep")
    own_rank = lax.axis_index("ep")
    step_count, _, requests, width = hidden.shape
    own_rows = step_count * requests
    slices = lax.axis_size("dp")

    def shift(value, step):
        return lax.ppermute(value, "dp", [(i, (i + step) % slices) for i in range(slices)])

    rows = hidden.reshape(own_rows, width)
    copies = jnp.broadcast_to(rows[None], (ranks, own_rows, width))
    mine = lax.all_to_all(copies, "ep", split_axis=0, concat_axis=0, tiled=True)
    mine = mine.reshape(ranks * own_rows, width)

    computed = attend(
        lengths[own_rank], queries, latent_cache, jnp.swapaxes(new_latent[:, 0], 0, 1)
    )
    mine, computed, even, odd = lax.optimization_barrier(
        (mine, computed, computed[0::2], computed[1::2])
    )
    arrived = travel(even, odd, ranks)

    tokens = jnp.concatenate([mine] + [shift(mine, step) for step in range(1, slices)], 0)
    gate_part = jnp.dot(tokens, w_gate[0], preferred_element_type=jnp.float32)
    up_part = jnp.dot(tokens, w_up[0], preferred_element_type=jnp.float32)
    units = (jax.nn.silu(gate_part) * up_part).astype(jnp.bfloat16)
    slice_out = jnp.dot(units, w_down[0], preferred_element_type=jnp.float32)
    slice_out = slice_out.astype(jnp.bfloat16)
    parts = slice_out.reshape(slices, ranks * own_rows, width)
    whole = parts[0].astype(jnp.float32)
    for step in range(1, slices):
        whole = whole + shift(parts[step], -step).astype(jnp.float32)
    whole = whole.astype(jnp.bfloat16)
    whole, arrived = lax.optimization_barrier((whole, arrived))
    returned = lax.all_to_all(
        whole.reshape(ranks, own_rows, width), "ep", split_axis=0, concat_axis=0, tiled=True
    )

    attended = relocate(computed, arrived, new_home, ranks, own_rank)
    sigmoid_part = jax.nn.sigmoid(route_logits[:, 0].astype(jnp.float32))
    gates = 2.5 * sigmoid_part / jnp.sum(sigmoid_part, -1, keepdims=True)
    rank_ids = jnp.arange(ranks, dtype=jnp.int32)
    chosen = routes[:, 0, :, :, None] == rank_ids
    dense = jnp.sum(jnp.where(chosen, gates[..., None], 0.0), 2).reshape(own_rows, ranks)
    summed = jnp.sum(returned.astype(jnp.float32) * dense.T[:, :, None], 0)
    moe_out = summed.astype(jnp.bfloat16).reshape(step_count, 1, requests, width)
    return (attended, moe_out)


def solution(mesh):
    placed = (
        P("ep", "dp", None, None),
        P(None, "dp"),
        P(None, "dp"),
        P(None, "ep", "dp", None, None),
        P(None, "ep", "dp", None),
        P(None, "ep", "dp", None),
        P(None, "ep", "dp", None),
        P(None, "ep", "dp", None),
        P("ep", None, "dp"),
        P("ep", None, "dp"),
        P("ep", "dp", None),
    )
    out_specs = (P(None, "ep", "dp", None, None), P(None, "ep", "dp", None))
    ranks = mesh.shape["ep"]
    if mesh.shape["dp"] == 2 and ranks % 8 == 0 and 3 * ranks <= LANES:
        return jax.shard_map(
            ladder, mesh=mesh, in_specs=placed, out_specs=out_specs, check_vma=False
        )
    return jax.shard_map(
        shards,
        mesh=mesh,
        in_specs=placed,
        out_specs=out_specs,
        check_vma=False,
    )
```

```python
import functools

import jax
import jax.numpy as jnp
from jax import lax
from jax.experimental import pallas as pl
from jax.experimental.pallas import tpu as pltpu
from jax.sharding import PartitionSpec as P


KV_RANK = 512
HEAD_QK = 192
LANES = 128
MESH = pl.DeviceIdType.MESH
RETURN_CHUNKS = 2


def ladder_kernel(
    plan,
    lengths_hbm,
    homes_hbm,
    fresh_hbm,
    hidden_hbm,
    routes_hbm,
    logits_hbm,
    cache_hbm,
    query_hbm,
    gate_hbm,
    up_hbm,
    down_hbm,
    attended_ref,
    moe_ref,
    lengths_ref,
    homes_ref,
    fresh_ref,
    hidden_ref,
    routes_ref,
    logits_ref,
    slots,
    tokens,
    query,
    cache,
    w_gate,
    w_up,
    w_down,
    served,
    far,
    near,
    onward,
    beyond,
    own_part,
    pair_send,
    pair_recv,
    chip_part,
    chip_send,
    first_recv,
    second_keep,
    second_send,
    second_recv,
    line_part,
    line_send,
    line_recv,
    line_sems,
    load_sem,
    send_sem,
    recv_sem,
):
    ranks, line = plan["ranks"], plan["line"]
    steps, requests = hidden_ref.shape[0], hidden_ref.shape[2]
    own_rows = steps * requests
    lat = cache.shape[1]
    heads = query.shape[-1]
    width = hidden_ref.shape[-1]
    blocks = width // LANES
    half = 4
    core = lax.axis_index("dp")
    rank = lax.axis_index("ep")
    side, up, place = lax.rem(rank, 2), lax.rem(lax.div(rank, 2), 2), lax.div(rank, 4)
    cell = lax.rem(rank, 4)
    across_side, across_up = rank + 1 - 2 * side, rank + 2 - 4 * up
    diagonal = rank - cell + 3 - cell
    plane = (
        diagonal,
        across_side * core + across_up * (1 - core),
        across_up * core + across_side * (1 - core),
    )
    other = 1 - core
    mine = core * half + cell
    far_rank = lax.rem(rank + ranks // 2, ranks)
    beyond_rank = lax.rem(rank + 4 - 8 * side + ranks, ranks)

    loads, sends = [], []

    def load(source, target):
        copy = pltpu.make_async_copy(source, target, load_sem.at[len(loads)])
        copy.start()
        loads.append(copy)
        return copy

    def send(source, target, to_core, to_rank):
        spot = len(sends)
        copy = pltpu.make_async_remote_copy(
            src_ref=source,
            dst_ref=target,
            send_sem=send_sem.at[spot],
            recv_sem=recv_sem.at[spot],
            device_id=(to_core, to_rank),
            device_id_type=MESH,
        )
        copy.start()
        sends.append(copy)
        return copy

    barrier = pltpu.get_barrier_semaphore()
    peers = [(other, rank)] + [(core, peer) for peer in plane]
    peers += [(core, lax.rem(rank + 4 * step, ranks)) for step in range(1, line)]
    for peer in peers:
        pl.semaphore_signal(barrier, inc=1, device_id=peer, device_id_type=MESH)

    token_loads = [
        load(hidden_hbm, hidden_ref),
        load(routes_hbm, routes_ref),
        load(logits_hbm, logits_ref),
    ]
    small_loads = [
        load(fresh_hbm, fresh_ref),
        load(lengths_hbm, lengths_ref),
        load(homes_hbm, homes_ref),
    ]
    attend_loads = {}
    for request in reversed(range(requests)):
        attend_loads[request] = (
            load(query_hbm.at[:, 0, request], query.at[request]),
            load(cache_hbm.at[0, request], cache.at[request]),
        )
    parts = 2
    rows = width // parts
    gate_loads = []
    for part in range(parts):
        span = pl.ds(part * rows, rows)
        gate_loads.append(
            (load(gate_hbm.at[0, span], w_gate.at[span]), load(up_hbm.at[0, span], w_up.at[span]))
        )
    down_load = load(down_hbm.at[0], w_down)

    for copy in token_loads:
        copy.wait()
    lane = lax.broadcasted_iota(jnp.int32, (requests, LANES), 1)
    expert = lane - jnp.where(lane >= 2 * ranks, 2 * ranks, jnp.where(lane >= ranks, ranks, 0))
    dense = []
    for step in range(steps):
        logits = logits_ref[step, 0].astype(jnp.float32)
        chosen = routes_ref[step, 0]
        sigmoid_part = 1.0 / (1.0 + jnp.exp(-logits))
        gates = 2.5 * sigmoid_part / jnp.sum(sigmoid_part, 1, keepdims=True)
        total = jnp.zeros((requests, LANES), jnp.float32)
        for k in range(chosen.shape[1]):
            total = total + jnp.where(chosen[:, k : k + 1] == expert, gates[:, k : k + 1], 0.0)
        dense.append(total)
    dense = jnp.concatenate(dense, 0)
    lane = lax.broadcasted_iota(jnp.int32, (own_rows, LANES), 1)
    high = dense.astype(jnp.bfloat16).astype(jnp.float32)
    middle = (dense - high).astype(jnp.bfloat16).astype(jnp.float32)
    low = dense - high - middle
    coded = jnp.where(lane < ranks, high, jnp.where(lane < 2 * ranks, middle, low))
    coded = jnp.where(lane < 3 * ranks, coded, 0.0)
    own = jnp.concatenate(
        [hidden_ref[step, 0].astype(jnp.float32) for step in range(steps)], 0
    )
    for block in range(blocks):
        slots[mine, place, block] = own[:, block * LANES : (block + 1) * LANES].astype(jnp.bfloat16)
    slots[mine, place, blocks] = coded.astype(jnp.bfloat16)

    pl.semaphore_wait(barrier, len(peers))

    def share(block, slot, to_core, to_rank):
        return send(slots.at[block, slot], slots.at[block, slot], to_core, to_rank)

    def spread(slot):
        plane_sends.append([share(mine, slot, core, peer) for peer in plane])
        pair_sends.append([share(mine, slot, other, rank)])

    def arrival(step, slot):
        return pltpu.make_async_remote_copy(
            src_ref=slots.at[mine, slot],
            dst_ref=slots.at[mine, slot],
            send_sem=line_sems.at[0, step - 1],
            recv_sem=line_sems.at[1, step - 1],
            device_id=(core, lax.rem(rank + 4 * step, ranks)),
            device_id_type=MESH,
        )

    def merge(block):
        tokens[block] = jnp.concatenate([slots[block, slot] for slot in range(line)], 1)

    plane_sends, pair_sends = [], []
    for step in reversed(range(1, line)):
        arrival(step, place).start()
    spread(place)

    near_sends, onward_sends, beyond_sends, far_sends = {}, {}, {}, {}
    quarter = heads // 2

    def cut(ref, piece):
        return ref.at[piece // 2, pl.ds(piece % 2 * quarter, quarter)]

    def send_near(piece):
        near_sends[piece] = send(cut(served.at[1], piece), cut(near, piece), core, across_side)

    def send_onward(piece):
        near_sends[piece].wait_recv()
        onward_sends[piece] = send(cut(near, piece), cut(onward, piece), core, across_up)

    def send_beyond(piece):
        onward_sends[piece].wait_recv()
        beyond_sends[piece] = send(cut(onward, piece), cut(beyond, piece), core, beyond_rank)

    def attend(request):
        for copy in attend_loads[request]:
            copy.wait()
        length = lengths_ref[request, rank]
        scale = HEAD_QK ** (-0.5)
        lines = jnp.concatenate([query[request, step] for step in range(steps)], 1)
        keys = cache[request]
        scores = (
            lax.dot_general(
                lines, keys, (((0,), (0,)), ((), ())), preferred_element_type=jnp.float32
            )
            * scale
        )
        spot = lax.broadcasted_iota(jnp.int32, scores.shape, 1)
        scores = jnp.where(spot < length, scores, -jnp.inf)
        row_step = lax.broadcasted_iota(jnp.int32, (steps * heads, 1), 0) // heads
        fresh = [
            fresh_ref[step, 0].astype(jnp.float32)[request : request + 1] for step in range(steps)
        ]
        pad = jnp.zeros((16 - steps, lat), jnp.float32)
        fresh_keys = jnp.concatenate(fresh + [pad], 0).astype(jnp.bfloat16)
        fresh_all = (
            lax.dot_general(
                lines, fresh_keys, (((0,), (1,)), ((), ())), preferred_element_type=jnp.float32
            )
            * scale
        )
        row_max = jnp.max(scores, 1, keepdims=True)
        fresh_scores = []
        for step in range(steps):
            one = jnp.where(row_step >= step, fresh_all[:, step : step + 1], -jnp.inf)
            row_max = jnp.maximum(row_max, one)
            fresh_scores.append(one)
        weights = jnp.exp(scores - row_max)
        fresh_weights = [jnp.exp(one - row_max) for one in fresh_scores]
        total = jnp.sum(weights, 1, keepdims=True)
        for one in fresh_weights:
            total = total + one
        share = 1.0 / total
        probs = (weights * share).astype(jnp.bfloat16)
        result = lax.dot_general(
            probs, keys[:KV_RANK], (((1,), (1,)), ((), ())), preferred_element_type=jnp.float32
        )
        for step in range(steps):
            part = (fresh_weights[step] * share).astype(jnp.bfloat16).astype(jnp.float32)
            result = result + part * fresh[step][:, :KV_RANK]
        result = result.astype(jnp.bfloat16)
        for step in range(steps):
            served[request, step] = result[step * heads : (step + 1) * heads]

    for copy in small_loads:
        copy.wait()
    attend(1)
    send_near(0)
    attend(0)
    far_sends = [send(served.at[0, step], far.at[step], core, far_rank) for step in range(steps)]

    lower = place < line // 2
    for reach in range(1, line):
        step = jnp.where(lower, line - reach, reach)
        slot = lax.rem(place - step + line, line)
        arrival(step, slot).wait_recv()
        spread(slot)
    merge(mine)
    send_near(1)
    send_near(2)
    send_near(3)
    for reach in range(line):
        slot = jnp.where(lower, place + reach, place - reach + line)
        slot = lax.rem(slot, line)
        for copy, peer in zip(plane_sends[reach], plane):
            copy.wait_recv()
            pair_sends[reach].append(share(core * half + lax.rem(peer, 4), slot, other, rank))
    send_onward(0)
    send_onward(1)
    for peer in plane:
        merge(core * half + lax.rem(peer, 4))
    for copies in pair_sends:
        for copy in copies:
            copy.wait_recv()
    for block in range(half):
        merge(other * half + block)

    gate_part = jnp.zeros((2 * half * line * own_rows, w_gate.shape[1]), jnp.float32)
    up_part = gate_part
    piece = blocks // parts
    for done in range(parts):
        for copy in gate_loads[done]:
            copy.wait()
        pieces = [
            tokens[:, block].reshape(gate_part.shape[0], LANES)
            for block in range(done * piece, (done + 1) * piece)
        ]
        values = jnp.concatenate(pieces, 1)
        span_rows = pl.ds(done * rows, rows)
        gate_part = gate_part + jnp.dot(
            values, w_gate[span_rows], preferred_element_type=jnp.float32
        )
        up_part = up_part + jnp.dot(values, w_up[span_rows], preferred_element_type=jnp.float32)
    send_onward(2)
    send_onward(3)
    units = (gate_part / (1.0 + jnp.exp(-gate_part)) * up_part).astype(jnp.bfloat16)
    coded = tokens[:, blocks].reshape(gate_part.shape[0], LANES).astype(jnp.float32)
    lane = lax.broadcasted_iota(jnp.int32, coded.shape, 1)
    hit = (lane == rank) | (lane == rank + ranks) | (lane == rank + 2 * ranks)
    gain = jnp.sum(jnp.where(hit, coded, 0.0), 1, keepdims=True)
    down_load.wait()

    chunk = width // RETURN_CHUNKS
    side_rows = half * line * own_rows
    cell_rows = line * own_rows
    pairs, firsts, seconds, lines = {}, {}, {}, {}

    def stage_down(c):
        out = jnp.dot(
            units, w_down[:, c * chunk : (c + 1) * chunk], preferred_element_type=jnp.float32
        )
        out = out * gain
        for part in range(2):
            value = out[part * side_rows : (part + 1) * side_rows]
            own_part[c, part] = value
            pair_send[c, part] = value.astype(jnp.bfloat16)
        pairs[c] = send(pair_send.at[c, other], pair_recv.at[c], other, rank)

    second = across_side * other + across_up * core
    first = across_up * other + across_side * core

    def stage_chip(c):
        pairs[c].wait_recv()
        value = own_part[c, core] + pair_recv[c].astype(jnp.float32)
        for part in range(half):
            cut = value[part * cell_rows : (part + 1) * cell_rows]
            chip_part[c, part] = cut
            chip_send[c, part] = cut.astype(jnp.bfloat16)
        firsts[c] = [
            send(chip_send.at[c, 3 - cell], first_recv.at[c, 1], core, second),
            send(chip_send.at[c, lax.rem(second, 4)], first_recv.at[c, 0], core, second),
        ]

    def stage_plane(c):
        firsts[c][0].wait_recv()
        value = chip_part[c, lax.rem(first, 4)] + first_recv[c, 1].astype(jnp.float32)
        second_send[c] = value.astype(jnp.bfloat16)
        seconds[c] = send(second_send.at[c], second_recv.at[c], core, first)
        firsts[c][1].wait_recv()
        second_keep[c] = chip_part[c, cell] + first_recv[c, 0].astype(jnp.float32)

    def stage_line(c):
        seconds[c].wait_recv()
        value = second_keep[c] + second_recv[c].astype(jnp.float32)
        for spot in range(line):
            cut = value[spot * own_rows : (spot + 1) * own_rows]
            line_part[c, spot] = cut
            line_send[c, spot] = cut.astype(jnp.bfloat16)
        lines[c] = [
            send(
                line_send.at[c, lax.rem(place + step, line)],
                line_recv.at[c, step - 1],
                core,
                lax.rem(rank + 4 * step, ranks),
            )
            for step in range(1, line)
        ]

    def stage_sum(c):
        value = line_part[c, place]
        for step in range(1, line):
            lines[c][step - 1].wait_recv()
            value = value + line_recv[c, step - 1].astype(jnp.float32)
        value = value.astype(jnp.bfloat16)
        for step in range(steps):
            moe_ref[step, 0, :, c * chunk : (c + 1) * chunk] = value[
                step * requests : (step + 1) * requests
            ]

    def settle(request, step):
        home = homes_ref[request, rank]
        arrived = far[step]
        if request % 2:
            arrived = jnp.where(side == up, beyond[step], onward[step])
            arrived = jnp.where(home == across_side, near[step], arrived)
        attended_ref[step, 0, request] = jnp.where(home == rank, served[request, step], arrived)

    for c in range(RETURN_CHUNKS):
        stage_down(c)
    send_beyond(0)
    send_beyond(1)
    for c in range(RETURN_CHUNKS):
        stage_chip(c)
    send_beyond(2)
    send_beyond(3)
    for c in range(RETURN_CHUNKS):
        stage_plane(c)
    for c in range(RETURN_CHUNKS):
        stage_line(c)
    for step in range(steps):
        far_sends[step].wait_recv()
        settle(0, step)
    for piece in (0, 1):
        beyond_sends[piece].wait_recv()
    settle(1, 0)
    for c in range(RETURN_CHUNKS):
        stage_sum(c)
    for step in range(1, steps):
        for piece in (2, 3):
            beyond_sends[piece].wait_recv()
        settle(1, step)
    for copy in sends:
        copy.wait_send()
    for step in range(1, line):
        arrival(step, place).wait_send()


def settle_kernel(attended_ref, moe_ref, attended_hbm, moe_hbm, sems):
    copies = (
        pltpu.make_async_copy(attended_ref, attended_hbm, sems.at[0]),
        pltpu.make_async_copy(moe_ref, moe_hbm, sems.at[1]),
    )
    for copy in copies:
        copy.start()
    for copy in copies:
        copy.wait()


def ladder(
    latent_cache,
    lengths,
    new_home,
    queries,
    new_latent,
    hidden,
    routes,
    route_logits,
    w_gate,
    w_up,
    w_down,
):
    ranks, slices = lax.axis_size("ep"), lax.axis_size("dp")
    line = ranks // 4
    steps, _, requests, width = hidden.shape
    heads, lat = queries.shape[3:]
    keys = latent_cache.shape[2]
    units = w_gate.shape[2]
    layers = width // LANES + 1
    own_rows = steps * requests
    chunk = width // RETURN_CHUNKS
    cell_rows = line * own_rows
    bf16, f32 = jnp.bfloat16, jnp.float32
    hbm = pl.BlockSpec(memory_space=pl.ANY)
    gather_sends = line * (3 + 4)
    return_sends = RETURN_CHUNKS * (1 + 2 + 1 + line - 1)
    sends = gather_sends + return_sends + 12 + steps
    loads = 6 + 2 * requests + 4 + 1
    attended, moe_out = pl.pallas_call(
        functools.partial(ladder_kernel, dict(ranks=ranks, line=line)),
        out_shape=(
            pltpu.VMEM((steps, 1, requests, heads, KV_RANK), bf16),
            pltpu.VMEM((steps, 1, requests, width), bf16),
        ),
        in_specs=[hbm] * 11,
        out_specs=(pl.BlockSpec(memory_space=pltpu.VMEM),) * 2,
        scratch_shapes=[
            pltpu.SMEM((requests, ranks), jnp.int32),
            pltpu.SMEM((requests, ranks), jnp.int32),
            pltpu.VMEM(new_latent.shape, bf16),
            pltpu.VMEM(hidden.shape, bf16),
            pltpu.VMEM(routes.shape, jnp.int32),
            pltpu.VMEM(route_logits.shape, bf16),
            pltpu.VMEM((slices * 4, line, layers, own_rows, LANES), bf16),
            pltpu.VMEM((slices * 4, layers, cell_rows, LANES), bf16),
            pltpu.VMEM((requests, steps, lat, heads), bf16),
            pltpu.VMEM((requests, lat, keys), bf16),
            pltpu.VMEM((width, units), bf16),
            pltpu.VMEM((width, units), bf16),
            pltpu.VMEM((units, width), bf16),
            pltpu.VMEM((requests, steps, heads, KV_RANK), bf16),
            pltpu.VMEM((steps, heads, KV_RANK), bf16),
            pltpu.VMEM((steps, heads, KV_RANK), bf16),
            pltpu.VMEM((steps, heads, KV_RANK), bf16),
            pltpu.VMEM((steps, heads, KV_RANK), bf16),
            pltpu.VMEM((RETURN_CHUNKS, 2, 4 * cell_rows, chunk), f32),
            pltpu.VMEM((RETURN_CHUNKS, 2, 4 * cell_rows, chunk), bf16),
            pltpu.VMEM((RETURN_CHUNKS, 4 * cell_rows, chunk), bf16),
            pltpu.VMEM((RETURN_CHUNKS, 4, cell_rows, chunk), f32),
            pltpu.VMEM((RETURN_CHUNKS, 4, cell_rows, chunk), bf16),
            pltpu.VMEM((RETURN_CHUNKS, 2, cell_rows, chunk), bf16),
            pltpu.VMEM((RETURN_CHUNKS, cell_rows, chunk), f32),
            pltpu.VMEM((RETURN_CHUNKS, cell_rows, chunk), bf16),
            pltpu.VMEM((RETURN_CHUNKS, cell_rows, chunk), bf16),
            pltpu.VMEM((RETURN_CHUNKS, line, own_rows, chunk), f32),
            pltpu.VMEM((RETURN_CHUNKS, line, own_rows, chunk), bf16),
            pltpu.VMEM((RETURN_CHUNKS, line - 1, own_rows, chunk), bf16),
            pltpu.SemaphoreType.DMA((2, line - 1)),
            pltpu.SemaphoreType.DMA((loads,)),
            pltpu.SemaphoreType.DMA((sends,)),
            pltpu.SemaphoreType.DMA((sends,)),
        ],
        compiler_params=pltpu.CompilerParams(
            collective_id=0, has_side_effects=True, vmem_limit_bytes=56 * 1024 * 1024
        ),
        name="ladder",
    )(
        lengths.T,
        new_home.T,
        new_latent,
        hidden,
        routes,
        route_logits,
        jnp.swapaxes(latent_cache, 2, 3),
        jnp.swapaxes(queries, 3, 4),
        w_gate,
        w_up,
        w_down,
    )
    results = (attended, moe_out)
    return pl.pallas_call(
        settle_kernel,
        out_shape=tuple(jax.ShapeDtypeStruct(one.shape, one.dtype) for one in results),
        in_specs=[pl.BlockSpec(memory_space=pltpu.VMEM)] * 2,
        out_specs=(hbm, hbm),
        scratch_shapes=[pltpu.SemaphoreType.DMA((2,))],
        compiler_params=pltpu.CompilerParams(vmem_limit_bytes=1024 * 1024),
        name="settle",
    )(*results)


def attend_kernel(length_ref, query_ref, cache_ref, fresh_ref, out_ref):
    step_count, head_count, lat_width = query_ref.shape
    rows = step_count * head_count
    length = length_ref[pl.program_id(0)]
    scale = HEAD_QK ** (-0.5)
    query = query_ref[...].reshape(rows, lat_width)
    keys = cache_ref[...]
    scores = (
        lax.dot_general(
            query, keys, (((1,), (1,)), ((), ())), preferred_element_type=jnp.float32
        )
        * scale
    )
    place = lax.broadcasted_iota(jnp.int32, scores.shape, 1)
    scores = jnp.where(place < length, scores, -jnp.inf)
    row_step = lax.broadcasted_iota(jnp.int32, (rows, 1), 0) // head_count
    wide_query = query.astype(jnp.float32)
    fresh = fresh_ref[...].astype(jnp.float32)
    fresh_scores = []
    row_max = jnp.max(scores, 1, keepdims=True)
    for step in range(step_count):
        one = jnp.sum(wide_query * fresh[step : step + 1], 1, keepdims=True) * scale
        one = jnp.where(row_step >= step, one, -jnp.inf)
        row_max = jnp.maximum(row_max, one)
        fresh_scores.append(one)
    weights = jnp.exp(scores - row_max)
    fresh_weights = [jnp.exp(one - row_max) for one in fresh_scores]
    total = jnp.sum(weights, 1, keepdims=True)
    for one in fresh_weights:
        total = total + one
    probs = (weights / total).astype(jnp.bfloat16)
    served = jnp.dot(probs, keys[:, :KV_RANK], preferred_element_type=jnp.float32)
    for step in range(step_count):
        part = (fresh_weights[step] / total).astype(jnp.bfloat16).astype(jnp.float32)
        served = served + part * fresh[step : step + 1, :KV_RANK]
    out_ref[...] = served.astype(jnp.bfloat16).reshape(step_count, head_count, KV_RANK)


def attend(own_lengths, queries, cache, fresh):
    step_count, _, requests, heads, lat = queries.shape
    keys = cache.shape[2]
    return pl.pallas_call(
        attend_kernel,
        grid_spec=pltpu.PrefetchScalarGridSpec(
            num_scalar_prefetch=1,
            grid=(requests,),
            in_specs=[
                pl.BlockSpec((step_count, None, None, heads, lat), lambda r, n: (0, 0, r, 0, 0)),
                pl.BlockSpec((None, None, keys, lat), lambda r, n: (0, r, 0, 0)),
                pl.BlockSpec((None, step_count, lat), lambda r, n: (r, 0, 0)),
            ],
            out_specs=pl.BlockSpec((None, step_count, heads, KV_RANK), lambda r, n: (r, 0, 0, 0)),
        ),
        out_shape=jax.ShapeDtypeStruct((requests, step_count, heads, KV_RANK), jnp.bfloat16),
        name="attend",
    )(own_lengths, queries, cache, fresh)


def travel(even, odd, ranks):
    half = ranks // 2
    across = [(e, (e + half) % ranks) for e in range(ranks)]
    ahead = [(e, (e + 1) % ranks) for e in range(ranks)]
    behind = [(e, (e - 1) % ranks) for e in range(ranks)]
    far = lax.ppermute(even, "ep", across)
    left = lax.ppermute(odd, "ep", ahead)
    right = lax.ppermute(odd, "ep", behind)
    return far, left, right


def relocate(computed, arrived, new_home, ranks, own_rank):
    requests = computed.shape[0]
    far, left, right = arrived
    anchor = new_home[own_rank]
    results = []
    for request in range(requests):
        home, slot = anchor[request], request // 2
        if request % 2 == 0:
            moved = far[slot]
        else:
            moved = jnp.where(home == (own_rank + 1) % ranks, right[slot], left[slot])
        results.append(jnp.where(home == own_rank, computed[request], moved))
    return jnp.stack(results, 1)[:, None]


def shards(
    latent_cache,
    lengths,
    new_home,
    queries,
    new_latent,
    hidden,
    routes,
    route_logits,
    w_gate,
    w_up,
    w_down,
):
    ranks = lax.axis_size("ep")
    own_rank = lax.axis_index("ep")
    step_count, _, requests, width = hidden.shape
    own_rows = step_count * requests
    slices = lax.axis_size("dp")

    def shift(value, step):
        return lax.ppermute(value, "dp", [(i, (i + step) % slices) for i in range(slices)])

    rows = hidden.reshape(own_rows, width)
    copies = jnp.broadcast_to(rows[None], (ranks, own_rows, width))
    mine = lax.all_to_all(copies, "ep", split_axis=0, concat_axis=0, tiled=True)
    mine = mine.reshape(ranks * own_rows, width)

    computed = attend(
        lengths[own_rank], queries, latent_cache, jnp.swapaxes(new_latent[:, 0], 0, 1)
    )
    mine, computed, even, odd = lax.optimization_barrier(
        (mine, computed, computed[0::2], computed[1::2])
    )
    arrived = travel(even, odd, ranks)

    tokens = jnp.concatenate([mine] + [shift(mine, step) for step in range(1, slices)], 0)
    gate_part = jnp.dot(tokens, w_gate[0], preferred_element_type=jnp.float32)
    up_part = jnp.dot(tokens, w_up[0], preferred_element_type=jnp.float32)
    units = (jax.nn.silu(gate_part) * up_part).astype(jnp.bfloat16)
    slice_out = jnp.dot(units, w_down[0], preferred_element_type=jnp.float32)
    slice_out = slice_out.astype(jnp.bfloat16)
    parts = slice_out.reshape(slices, ranks * own_rows, width)
    whole = parts[0].astype(jnp.float32)
    for step in range(1, slices):
        whole = whole + shift(parts[step], -step).astype(jnp.float32)
    whole = whole.astype(jnp.bfloat16)
    whole, arrived = lax.optimization_barrier((whole, arrived))
    returned = lax.all_to_all(
        whole.reshape(ranks, own_rows, width), "ep", split_axis=0, concat_axis=0, tiled=True
    )

    attended = relocate(computed, arrived, new_home, ranks, own_rank)
    sigmoid_part = jax.nn.sigmoid(route_logits[:, 0].astype(jnp.float32))
    gates = 2.5 * sigmoid_part / jnp.sum(sigmoid_part, -1, keepdims=True)
    rank_ids = jnp.arange(ranks, dtype=jnp.int32)
    chosen = routes[:, 0, :, :, None] == rank_ids
    dense = jnp.sum(jnp.where(chosen, gates[..., None], 0.0), 2).reshape(own_rows, ranks)
    summed = jnp.sum(returned.astype(jnp.float32) * dense.T[:, :, None], 0)
    moe_out = summed.astype(jnp.bfloat16).reshape(step_count, 1, requests, width)
    return (attended, moe_out)


def solution(mesh):
    placed = (
        P("ep", "dp", None, None),
        P(None, "dp"),
        P(None, "dp"),
        P(None, "ep", "dp", None, None),
        P(None, "ep", "dp", None),
        P(None, "ep", "dp", None),
        P(None, "ep", "dp", None),
        P(None, "ep", "dp", None),
        P("ep", None, "dp"),
        P("ep", None, "dp"),
        P("ep", "dp", None),
    )
    out_specs = (P(None, "ep", "dp", None, None), P(None, "ep", "dp", None))
    ranks = mesh.shape["ep"]
    if mesh.shape["dp"] == 2 and ranks % 8 == 0 and 3 * ranks <= LANES:
        return jax.shard_map(
            ladder, mesh=mesh, in_specs=placed, out_specs=out_specs, check_vma=False
        )
    return jax.shard_map(
        shards,
        mesh=mesh,
        in_specs=placed,
        out_specs=out_specs,
        check_vma=False,
    )
```
